32 devices in a mesh: row: 4 (over x, core), col: 8 (over z, y).
Axes of the slice: x: 2, y: 2, z: 4, core: 2. Of those that a mesh axis runs over, the one named last changes fastest.
Arguments:
- pixels: bfloat16 [16, 256, 6, 1536], P('row', 'col'), may hold values from -6 to 6
- timestamps: int32 [4, 8, 6], P('row', 'col'), may hold values from 0 to 365
- frame_count: int32 [4, 8], P('row', 'col'), may hold values from 1 to 6
- visible: int32 [16, 256, 6], P('row', 'col'), may hold values 0 or 1
- halo_reach: int32 [4, 8], P('row', 'col'), may hold values from 1 to 2
- w_patch: bfloat16 [1536, 768], replicated, may hold values from -0.15625 to 0.15625
- b_patch: bfloat16 [768], replicated, may hold values from -3 to 3
- gain_one: bfloat16 [768], replicated, may hold values from 0.099609375 to 1.8984375
- shift_one: bfloat16 [768], replicated, may hold values from -3 to 3
- w_qkv: bfloat16 [768, 2304], replicated, may hold values from -0.3125 to 0.3125
- b_query: bfloat16 [768], replicated, may hold values from -3 to 3
- b_value: bfloat16 [768], replicated, may hold values from -3 to 3
- w_out: bfloat16 [768, 768], replicated, may hold values from -1.75 to 1.75
- b_out: bfloat16 [768], replicated, may hold values from -3 to 3
- gain_two: bfloat16 [768], replicated, may hold values from 0.099609375 to 1.8984375
- shift_two: bfloat16 [768], replicated, may hold values from -3 to 3
- w_up: bfloat16 [768, 3072], replicated, may hold values from -0.21875 to 0.21875
- b_up: bfloat16 [3072], replicated, may hold values from -3 to 3
- w_down: bfloat16 [3072, 768], replicated, may hold values from -0.21875 to 0.21875
- b_down: bfloat16 [768], replicated, may hold values from -3 to 3
- w_dec: bfloat16 [768, 512], replicated, may hold values from -0.21875 to 0.21875
- b_dec: bfloat16 [512], replicated, may hold values from -3 to 3
- w_pix: bfloat16 [512, 1536], replicated, may hold values from -0.25 to 0.25
- b_pix: bfloat16 [1536], replicated, may hold values from -3 to 3
- cotangent: bfloat16 [16, 256, 6, 1536], P('row', 'col'), may hold values from -6 to 6
Outputs:
- pixel_out: bfloat16 [16, 256, 6, 1536], P('row', 'col')
- pixel_grad: bfloat16 [16, 256, 6, 1536], P('row', 'col')
- grad_w_patch: float32 [1536, 768], P('row')
- grad_b_patch: float32 [768], P('row')
- grad_gain_one: float32 [768], P('row')
- grad_shift_one: float32 [768], P('row')
- grad_w_qkv: float32 [768, 2304], P('row')
- grad_b_query: float32 [768], P('row')
- grad_b_value: float32 [768], P('row')
- grad_w_out: float32 [768, 768], P('row')
- grad_b_out: float32 [768], P('row')
- grad_gain_two: float32 [768], P('row')
- grad_shift_two: float32 [768], P('row')
- grad_w_up: float32 [768, 3072], P('row')
- grad_b_up: float32 [3072], P('row')
- grad_w_down: float32 [3072, 768], P('row')
- grad_b_down: float32 [768], P('row')
- grad_w_dec: float32 [768, 512], P('row')
- grad_b_dec: float32 [512], P('row')
- grad_w_pix: float32 [512, 1536], P('row')
- grad_b_pix: float32 [1536], P('row')
The draws below stay inside these ranges and needn't reach their ends.
All inputs are finite; a program needn't handle non-finite values. No bound on the sum of `visible` on one device may be relied on, other than what follows from the above.
Results may differ from the reference program's by a relative error of at most 0.02.
Values may be sent and summed in bfloat16 or wider, within the bound.
No kernel may reach another device: no remote copies, remote signals or barrier semaphores. Data moves between devices by JAX's collectives and lax.ppermute only.
A program may use at most 192 MiB of HBM per device.

```python
import jax
import jax.numpy as jnp
from jax import lax

D = 768
HEAD_WIDTH = 64
FF = 3072
DEC = 512
PIX = 1536
FRAMES = 6
HALO = 2
TILE_ROWS = 4
TILE_COLS = 32
TILES_DOWN = 4
TILES_ACROSS = 8
SCENE_ROWS = 16
SCENE_COLS = 256
TOK_DEV = 768
STRIP = 864
N_ROW = 4
N_COL = 8


def touch_ends(values, key, smallest, top_value):
    shape = values.shape
    index_at = [jax.random.randint(jax.random.fold_in(key, axis), (), 0, shape[axis]) for axis in range(len(shape))]
    values = values.at[tuple(index_at)].set(smallest)
    longest = shape.index(max(shape))
    index_at[longest] = (index_at[longest] + 1) % shape[longest]
    return values.at[tuple(index_at)].set(top_value)


def level_of(own_key, shape, cuts, smallest, top_value):
    factor_of, own = 1.0, jax.random.fold_in(own_key, 6)
    for axis_at, parts in cuts:
        draws = jnp.exp(jax.random.uniform(jax.random.fold_in(own, axis_at), (parts,), jnp.float32, smallest / len(cuts), top_value / len(cuts)))
        factor_of = factor_of * jnp.repeat(draws, shape[axis_at] // parts).reshape([-1 if axis == axis_at else 1 for axis in range(len(shape))])
    return factor_of


def centred(own_key, shape, width, reach, shards=(), kind=jnp.bfloat16):
    level = level_of(own_key, shape, shards, -0.22, 0.18) if shards else 1.0
    drawn = jax.random.normal(own_key, shape, jnp.float32) * width * level
    return jnp.minimum(jnp.maximum(drawn, -reach), reach).astype(kind)


def setup_inputs(seed: int = 0) -> dict:
    seeds = jax.random.split(jax.random.key(seed), 26)
    pixels = centred(seeds[0], (SCENE_ROWS, SCENE_COLS, FRAMES, PIX), 1.0, 6.0, ((0, 4), (1, 8)))
    timestamps = touch_ends(jax.random.randint(seeds[1], (TILES_DOWN, TILES_ACROSS, FRAMES), 0, 366), jax.random.fold_in(seeds[1], 1), 0, 365).astype(jnp.int32)
    frame_count = touch_ends(jax.random.randint(seeds[2], (TILES_DOWN, TILES_ACROSS), 1, FRAMES + 1), jax.random.fold_in(seeds[2], 1), 1, FRAMES).astype(jnp.int32)
    visible = touch_ends((jax.random.randint(seeds[3], (SCENE_ROWS, SCENE_COLS, FRAMES), 0, 4) < 3).astype(jnp.int32), jax.random.fold_in(seeds[3], 1), 0, 1)
    halo_reach = touch_ends(jax.random.randint(seeds[4], (TILES_DOWN, TILES_ACROSS), 1, HALO + 1), jax.random.fold_in(seeds[4], 1), 1, HALO).astype(jnp.int32)
    w_patch = centred(seeds[5], (PIX, D), PIX ** -0.5, 0.15625)
    b_patch = centred(seeds[6], (D,), 0.5, 3.0)
    gain_one = jnp.clip(1.0 + 0.18 * jax.random.normal(seeds[7], (D,), jnp.float32), 0.099609375, 1.8984375).astype(jnp.bfloat16)
    shift_one = centred(seeds[8], (D,), 0.5, 3.0)
    w_qkv = centred(seeds[9], (D, 3 * D), (D // 2) ** -0.5, 0.3125)
    b_query = centred(seeds[10], (D,), 0.5, 3.0)
    b_value = centred(seeds[11], (D,), 0.5, 3.0)
    w_out = centred(seeds[12], (D, D), (D // 64) ** -0.5, 1.75)
    b_out = centred(seeds[13], (D,), 0.5, 3.0)
    gain_two = jnp.clip(1.0 + 0.18 * jax.random.normal(seeds[14], (D,), jnp.float32), 0.099609375, 1.8984375).astype(jnp.bfloat16)
    shift_two = centred(seeds[15], (D,), 0.5, 3.0)
    w_up = centred(seeds[16], (D, FF), D ** -0.5, 0.21875)
    b_up = centred(seeds[17], (FF,), 0.5, 3.0)
    w_down = centred(seeds[18], (FF, D), (FF // 4) ** -0.5, 0.21875)
    b_down = centred(seeds[19], (D,), 0.5, 3.0)
    w_dec = centred(seeds[20], (D, DEC), D ** -0.5, 0.21875)
    b_dec = centred(seeds[21], (DEC,), 0.5, 3.0)
    w_pix = centred(seeds[22], (DEC, PIX), DEC ** -0.5, 0.25)
    b_pix = centred(seeds[23], (PIX,), 0.5, 3.0)
    cotangent = centred(seeds[24], (SCENE_ROWS, SCENE_COLS, FRAMES, PIX), 1.0, 6.0, ((0, 4), (1, 8)))
    return {"pixels": pixels, "timestamps": timestamps, "frame_count": frame_count, "visible": visible, "halo_reach": halo_reach, "w_patch": w_patch, "b_patch": b_patch, "gain_one": gain_one, "shift_one": shift_one, "w_qkv": w_qkv, "b_query": b_query, "b_value": b_value, "w_out": w_out, "b_out": b_out, "gain_two": gain_two, "shift_two": shift_two, "w_up": w_up, "b_up": b_up, "w_down": w_down, "b_down": b_down, "w_dec": w_dec, "b_dec": b_dec, "w_pix": w_pix, "b_pix": b_pix, "cotangent": cotangent}


EPS = 1e-06
NEG_FILL = -1e+30
EXACT_PRECISION = lax.Precision.HIGHEST

@jax.custom_vjp
def reduced_precision(v):
    return lax.optimization_barrier(v.astype(jnp.bfloat16)).astype(jnp.float32)

@jax.custom_vjp
def reduced_backward(v):
    return v

def low_keep(v):
    return (reduced_precision(v), None)

def low_pass(kept, grad):
    return (grad,)

def back_keep(v):
    return (v, None)

def back_low(kept, grad):
    return (reduced_precision(grad),)
reduced_precision.defvjp(low_keep, low_pass)
reduced_backward.defvjp(back_keep, back_low)

def sin_cos(places, width_part):
    half_width = width_part // 2
    frequency = 1.0 / 10000.0 ** (jnp.arange(half_width, dtype=jnp.float32) / half_width)
    angles = places[..., None] * frequency
    return jnp.concatenate([jnp.sin(angles), jnp.cos(angles)], -1)

def layer_norm(values, norm_gain, norm_shift):
    centre = values - lax.optimization_barrier(jnp.mean(values, -1, keepdims=True))
    spread = lax.optimization_barrier(jnp.mean(centre * centre, -1, keepdims=True))
    return centre * lax.rsqrt(spread + EPS) * norm_gain + norm_shift

def matmul(left_side, right_side):
    return jnp.einsum('...i,ij->...j', left_side, right_side, precision=EXACT_PRECISION)

def to_tiles(whole_array):
    shaped = whole_array.reshape((N_ROW, TILE_ROWS, N_COL, TILE_COLS) + whole_array.shape[2:])
    return jnp.swapaxes(shaped, 1, 2)

def from_tiles(tiled_up):
    shaped = jnp.swapaxes(tiled_up, 1, 2)
    return shaped.reshape((N_ROW * TILE_ROWS, N_COL * TILE_COLS) + tiled_up.shape[4:])

def strips_of(tiled_up):
    upper_strip = jnp.roll(tiled_up[:, :, TILE_ROWS - HALO:], 1, axis=0)
    lower_strip = jnp.roll(tiled_up[:, :, :HALO], -1, axis=0)
    left_strip = jnp.roll(tiled_up[:, :, :, TILE_COLS - HALO:], 1, axis=1)
    right_strip = jnp.roll(tiled_up[:, :, :, :HALO], -1, axis=1)
    trailing = tiled_up.shape[5:]
    pieces = [strip_piece.reshape((N_ROW, N_COL, -1) + trailing) for strip_piece in (upper_strip, lower_strip, left_strip, right_strip)]
    return jnp.concatenate(pieces, 2)

def strip_distance(row_count, col_count, frame_total, halo_size):
    near_index = jnp.arange(halo_size, dtype=jnp.int32)
    upper_dist = jnp.broadcast_to((halo_size - near_index)[:, None, None], (halo_size, col_count, frame_total)).reshape(-1)
    lower_dist = jnp.broadcast_to((near_index + 1)[:, None, None], (halo_size, col_count, frame_total)).reshape(-1)
    left_dist = jnp.broadcast_to((halo_size - near_index)[None, :, None], (row_count, halo_size, frame_total)).reshape(-1)
    right_dist = jnp.broadcast_to((near_index + 1)[None, :, None], (row_count, halo_size, frame_total)).reshape(-1)
    return jnp.concatenate([upper_dist, lower_dist, left_dist, right_dist])

def tile_attention(own_rows, strip_rows, key_ok, w_qkv, b_query, b_value):
    model_width = own_rows.shape[-1]
    own_count = own_rows.shape[0]
    query_all = matmul(own_rows, w_qkv)
    strip_kv = matmul(strip_rows, w_qkv[:, model_width:])
    key_value = jnp.concatenate([query_all[:, model_width:], strip_kv], 0)
    key_count = key_value.shape[0]
    query_rows = reduced_precision(reduced_backward(query_all[:, :model_width] + b_query))
    key_rows = reduced_precision(reduced_backward(key_value[:, :model_width]))
    value_rows = reduced_precision(reduced_backward(key_value[:, model_width:] + b_value))
    head_count = model_width // HEAD_WIDTH
    per_head_queries = query_rows.reshape(own_count, head_count, HEAD_WIDTH)
    per_head_keys = key_rows.reshape(key_count, head_count, HEAD_WIDTH)
    per_head_values = value_rows.reshape(key_count, head_count, HEAD_WIDTH)
    attention_scores = reduced_backward(jnp.einsum('rex,sex->ers', per_head_queries, per_head_keys, precision=EXACT_PRECISION) * HEAD_WIDTH ** (-0.5))
    allowed = (key_ok[None, :] > 0.5) | (jnp.arange(key_count)[None, :] == jnp.arange(own_count)[:, None])
    attention_scores = jnp.where(allowed[None], attention_scores, NEG_FILL)
    weight_matrices = jax.nn.softmax(attention_scores, axis=-1)
    mixed_heads_output = jnp.einsum('bfq,qbp->fbp', reduced_precision(weight_matrices), per_head_values, precision=EXACT_PRECISION)
    return reduced_precision(reduced_backward(mixed_heads_output.reshape(own_count, model_width)))

def reference(pixels, timestamps, frame_count, visible, halo_reach, w_patch, b_patch, gain_one, shift_one, w_qkv, b_query, b_value, w_out, b_out, gain_two, shift_two, w_up, b_up, w_down, b_down, w_dec, b_dec, w_pix, b_pix, cotangent):
    frame_index = jnp.arange(FRAMES, dtype=jnp.int32)
    counts_whole = jnp.repeat(jnp.repeat(frame_count, TILE_ROWS, 0), TILE_COLS, 1)
    key_whole = ((frame_index[None, None, :] < counts_whole[:, :, None]) & (visible == 1)).astype(jnp.float32)
    stamps_whole = jnp.repeat(jnp.repeat(timestamps, TILE_ROWS, 0), TILE_COLS, 1).astype(jnp.float32)
    time_part = sin_cos(stamps_whole, D // 16 * 4)
    row_part = sin_cos(jnp.arange(SCENE_ROWS).astype(jnp.float32), D // 16 * 6)
    col_part = sin_cos(jnp.arange(SCENE_COLS).astype(jnp.float32), D // 16 * 6)
    side_width = row_part.shape[-1]
    position = jnp.concatenate([time_part, jnp.broadcast_to(row_part[:, None, None, :], (SCENE_ROWS, SCENE_COLS, FRAMES, side_width)), jnp.broadcast_to(col_part[None, :, None, :], (SCENE_ROWS, SCENE_COLS, FRAMES, side_width))], -1)
    tiles_ok = to_tiles(key_whole)
    own_ok = tiles_ok.reshape(N_ROW, N_COL, -1)
    strip_ok = strips_of(tiles_ok)
    reach_ok = (halo_reach[:, :, None] >= strip_distance(TILE_ROWS, TILE_COLS, FRAMES, HALO)[None, None, :]).astype(jnp.float32)
    all_ok = jnp.concatenate([own_ok, strip_ok * reach_ok], 2).reshape(N_ROW * N_COL, -1)

    def forward(pixel_vals, w_patch, b_patch, gain_one, shift_one, w_qkv, b_query, b_value, w_out, b_out, gain_two, shift_two, w_up, b_up, w_down, b_down, w_dec, b_dec, w_pix, b_pix):
        stream_one = reduced_backward(matmul(pixel_vals, w_patch)) + b_patch + position
        normed_one = reduced_precision(layer_norm(stream_one, gain_one, shift_one))
        tiled_up = to_tiles(normed_one)
        own_rows = tiled_up.reshape(N_ROW * N_COL, TOK_DEV, D)
        strip_rows = strips_of(tiled_up).reshape(N_ROW * N_COL, STRIP, D)

        def one_tile(inputs):
            return tile_attention(inputs[0], inputs[1], inputs[2], w_qkv, b_query, b_value)
        attended = lax.map(jax.checkpoint(one_tile), (own_rows, strip_rows, all_ok))
        attended = from_tiles(attended.reshape(N_ROW, N_COL, TILE_ROWS, TILE_COLS, FRAMES, D))
        stream_two = stream_one + reduced_backward(matmul(attended, w_out) + b_out)
        normed_two = reduced_precision(layer_norm(stream_two, gain_two, shift_two))
        hidden_pre = reduced_backward(matmul(normed_two, w_up) + b_up)
        hidden_act = reduced_precision(jax.nn.gelu(hidden_pre, approximate=False))
        stream_out = stream_two + reduced_backward(matmul(hidden_act, w_down) + b_down)
        decoded = reduced_precision(reduced_backward(matmul(reduced_precision(stream_out), w_dec) + b_dec))
        return matmul(decoded, w_pix) + b_pix
    weight_list = (w_patch, b_patch, gain_one, shift_one, w_qkv, b_query, b_value, w_out, b_out, gain_two, shift_two, w_up, b_up, w_down, b_down, w_dec, b_dec, w_pix, b_pix)
    floats = (pixels.astype(jnp.float32),) + tuple((item.astype(jnp.float32) for item in weight_list))
    result, pull_back = jax.vjp(forward, *floats)
    gradients = pull_back(cotangent.astype(jnp.float32))
    return (result.astype(jnp.bfloat16), gradients[0].astype(jnp.bfloat16), gradients[1], gradients[2], gradients[3], gradients[4], gradients[5], gradients[6], gradients[7], gradients[8], gradients[9], gradients[10], gradients[11], gradients[12], gradients[13], gradients[14], gradients[15], gradients[16], gradients[17], gradients[18], gradients[19])
```

```python
import functools
import math

import jax
import jax.numpy as jnp
from jax import lax
from jax.experimental import pallas as pl
from jax.experimental.pallas import tpu as pltpu
from jax.sharding import PartitionSpec as P

HEAD_WIDTH = 64
HALO = 2
EPS = 1e-06
NEG_FILL = -1e30
BLOCK = 256
LANES = 128
SCALE = HEAD_WIDTH**-0.5
LOG_SCALE = SCALE * math.log2(math.e)
F32 = jnp.float32
BF16 = jnp.bfloat16


def sin_cos(places, width_part):
    half_width = width_part // 2
    frequency = 1.0 / 10000.0 ** (jnp.arange(half_width, dtype=F32) / half_width)
    angles = places[..., None] * frequency
    return jnp.concatenate([jnp.sin(angles), jnp.cos(angles)], -1)


def layer_norm(values, norm_gain, norm_shift):
    centre = values - jnp.mean(values, -1, keepdims=True)
    spread = jnp.mean(centre * centre, -1, keepdims=True)
    return centre * lax.rsqrt(spread + EPS) * norm_gain + norm_shift


def norm_backward(values, norm_gain, norm_shift, upstream):
    _, pull_back = jax.vjp(layer_norm, values, norm_gain.astype(F32), norm_shift.astype(F32))
    return pull_back(upstream)


def gelu_exact(values):
    return jax.nn.gelu(values, approximate=False)


def mat_low(left_side, right_side):
    return jnp.dot(left_side, right_side, preferred_element_type=F32)


def outer_sum(left_side, right_side):
    return jnp.einsum("nd,ne->de", left_side, right_side, preferred_element_type=F32)


def times_transposed(left_side, right_side):
    return jnp.einsum("ne,de->nd", left_side, right_side, preferred_element_type=F32)


def column_sum(values):
    return jnp.sum(values, 0, dtype=F32)


def dot_last(a, b):
    return lax.dot_general(a, b, (((1,), (1,)), ((), ())), preferred_element_type=F32)


def dot_plain(a, b):
    return lax.dot_general(a, b, (((1,), (0,)), ((), ())), preferred_element_type=F32)


def one_head(pair, head):
    lane = lax.broadcasted_iota(jnp.int32, pair.shape, 1)
    keep = (lane < HEAD_WIDTH) if head == 0 else (lane >= HEAD_WIDTH)
    return jnp.where(keep, pair, jnp.zeros_like(pair))


def diagonal(size):
    rows = lax.broadcasted_iota(jnp.int32, (size, size), 0)
    return rows == lax.broadcasted_iota(jnp.int32, (size, size), 1)


def attend_kernel(q_ref, k_ref, v_ref, bias_ref, out_ref, log_ref, s_ref):
    tokens = q_ref.shape[0]
    eye = diagonal(BLOCK)
    lane = lax.broadcasted_iota(jnp.int32, (BLOCK, LANES), 1)

    def step(i, carry):
        at = pl.multiple_of(i * BLOCK, BLOCK)
        q = q_ref[pl.ds(at, BLOCK), :]
        mixed = []
        for head in range(2):
            q_head = one_head(q, head)
            s_ref[head] = dot_last(q_head, k_ref[...]) + bias_ref[...]
            own = dot_last(q_head, k_ref[pl.ds(at, BLOCK), :])
            s_ref[head, :, pl.ds(at, BLOCK)] = jnp.where(
                eye, own, own + bias_ref[:, pl.ds(at, BLOCK)]
            )
            scores = s_ref[head]
            top = jnp.max(scores, axis=1, keepdims=True)
            weights = jnp.exp2(scores * LOG_SCALE - top * LOG_SCALE)
            total = jnp.sum(weights, axis=1, keepdims=True)
            mixed.append(dot_plain(weights.astype(BF16), v_ref[...]) / total)
            log_ref[0, head, pl.ds(at, BLOCK)] = (top * LOG_SCALE + jnp.log2(total))[:, 0]
        out_ref[pl.ds(at, BLOCK), :] = jnp.where(lane < HEAD_WIDTH, mixed[0], mixed[1]).astype(
            out_ref.dtype
        )
        return carry

    lax.fori_loop(0, tokens // BLOCK, step, 0)


def attend(q, k, v, bias):
    tokens, width = q.shape
    keys = k.shape[0]
    pairs = width // LANES
    return pl.pallas_call(
        attend_kernel,
        grid=(pairs,),
        in_specs=[
            pl.BlockSpec((tokens, LANES), lambda p: (0, p)),
            pl.BlockSpec((keys, LANES), lambda p: (0, p)),
            pl.BlockSpec((keys, LANES), lambda p: (0, p)),
            pl.BlockSpec((1, keys), lambda p: (0, 0)),
        ],
        out_specs=[
            pl.BlockSpec((tokens, LANES), lambda p: (0, p)),
            pl.BlockSpec((1, 2, tokens), lambda p: (p, 0, 0)),
        ],
        out_shape=[
            jax.ShapeDtypeStruct((tokens, width), BF16),
            jax.ShapeDtypeStruct((pairs, 2, tokens), F32),
        ],
        scratch_shapes=[pltpu.VMEM((2, BLOCK, keys), F32)],
        compiler_params=pltpu.CompilerParams(vmem_limit_bytes=48 << 20),
        cost_estimate=pl.CostEstimate(
            flops=16 * tokens * keys * width, bytes_accessed=8 << 20, transcendentals=0
        ),
        name="attend",
    )(q, k, v, bias)


def attend_back_kernel(
    q_ref, k_ref, v_ref, do_ref, o_ref, log_ref, bias_ref, dq_ref, dk_ref, dv_ref, kt_ref, dk_sum, dv_sum
):
    tokens = q_ref.shape[0]
    kt_ref[...] = k_ref[...].T
    eye = diagonal(BLOCK)
    dk_sum[...] = jnp.zeros_like(dk_sum)
    dv_sum[...] = jnp.zeros_like(dv_sum)

    def step(i, carry):
        at = pl.multiple_of(i * BLOCK, BLOCK)
        q = q_ref[pl.ds(at, BLOCK), :]
        do = do_ref[pl.ds(at, BLOCK), :]
        product = (do.astype(F32) * o_ref[pl.ds(at, BLOCK), :].astype(F32)).T
        parts = []
        for head in range(2):
            delta = jnp.sum(
                product[head * HEAD_WIDTH : (head + 1) * HEAD_WIDTH], axis=0, keepdims=True
            )
            q_head = one_head(q, head)
            do_head = one_head(do, head)
            log_total = log_ref[0, pl.ds(head, 1), pl.ds(at, BLOCK)]
            scores = dot_last(k_ref[...], q_head) + bias_ref[...]
            weights = jnp.exp2(scores * LOG_SCALE - log_total)
            back = dot_last(v_ref[...], do_head)
            grad = (weights * (back - delta)).astype(BF16)
            own_scores = dot_last(k_ref[pl.ds(at, BLOCK), :], q_head)
            own = jnp.where(
                eye & (bias_ref[pl.ds(at, BLOCK), :] < 0),
                jnp.exp2(own_scores * LOG_SCALE - log_total),
                0.0,
            )
            own_back = dot_last(v_ref[pl.ds(at, BLOCK), :], do_head)
            own_grad = (own * (own_back - delta)).astype(BF16)
            dv_sum[...] += dot_plain(weights.astype(BF16), do_head)
            dv_sum[pl.ds(at, BLOCK), :] += dot_plain(own.astype(BF16), do_head)
            dk_sum[...] += dot_plain(grad, q_head)
            dk_sum[pl.ds(at, BLOCK), :] += dot_plain(own_grad, q_head)
            parts.append(
                dot_plain(kt_ref[...], grad) + dot_plain(kt_ref[:, pl.ds(at, BLOCK)], own_grad)
            )
        joined = jnp.concatenate([parts[0][:HEAD_WIDTH], parts[1][HEAD_WIDTH:]], axis=0)
        dq_ref[pl.ds(at, BLOCK), :] = (joined.T * SCALE).astype(BF16)
        return carry

    lax.fori_loop(0, tokens // BLOCK, step, 0)
    dk_ref[...] = (dk_sum[...] * SCALE).astype(BF16)
    dv_ref[...] = dv_sum[...].astype(BF16)


def attend_back(q, k, v, do, o, log_total, bias):
    tokens, width = q.shape
    keys = k.shape[0]
    pairs = width // LANES
    own = pl.BlockSpec((tokens, LANES), lambda p: (0, p))
    wide = pl.BlockSpec((keys, LANES), lambda p: (0, p))
    return pl.pallas_call(
        attend_back_kernel,
        grid=(pairs,),
        in_specs=[
            own,
            wide,
            wide,
            own,
            own,
            pl.BlockSpec((1, 2, tokens), lambda p: (p, 0, 0)),
            pl.BlockSpec((keys, 1), lambda p: (0, 0)),
        ],
        out_specs=[own, wide, wide],
        out_shape=[
            jax.ShapeDtypeStruct((tokens, width), BF16),
            jax.ShapeDtypeStruct((keys, width), BF16),
            jax.ShapeDtypeStruct((keys, width), BF16),
        ],
        scratch_shapes=[
            pltpu.VMEM((LANES, keys), BF16),
            pltpu.VMEM((keys, LANES), F32),
            pltpu.VMEM((keys, LANES), F32),
        ],
        compiler_params=pltpu.CompilerParams(vmem_limit_bytes=48 << 20),
        cost_estimate=pl.CostEstimate(
            flops=24 * tokens * keys * width, bytes_accessed=16 << 20, transcendentals=0
        ),
        name="attend_back",
    )(q, k, v, do, o, log_total, bias)


def swap(value, axis, stride):
    count = lax.axis_size(axis)
    return lax.ppermute(value, axis, [(i, i ^ stride) for i in range(count)])


def rotate(value, axis, steps):
    count = lax.axis_size(axis)
    return lax.ppermute(value, axis, [(i, (i + steps) % count) for i in range(count)])


def pick(values, index):
    return lax.dynamic_index_in_dim(values, index, 0, keepdims=False)


def add(a, b):
    return (a.astype(F32) + b.astype(F32)).astype(BF16)


def reduce_quarters(quarters):
    row_total = lax.axis_size("row")
    col_total = lax.axis_size("col")
    rows, width = quarters.shape[1:]
    granule = 8 * col_total
    padded = -(-rows // granule) * granule
    if padded != rows:
        quarters = jnp.pad(quarters, ((0, 0), (0, padded - rows), (0, 0)))
    row_at = lax.axis_index("row")
    held = quarters
    stride = 1
    while stride < row_total:
        count = held.shape[0]
        bit = (row_at // stride) % 2
        split = held.reshape((count // 2, 2) + held.shape[1:])
        sent = lax.dynamic_index_in_dim(split, 1 - bit, 1, keepdims=False)
        kept = lax.dynamic_index_in_dim(split, bit, 1, keepdims=False)
        held = add(kept, swap(sent, "row", stride))
        stride *= 2
    part = held[0]
    col_at = lax.axis_index("col")
    stride = 1
    while stride < col_total:
        bit = (col_at // stride) % 2
        split = part.reshape(2, part.shape[0] // 2, width)
        part = add(pick(split, bit), swap(pick(split, 1 - bit), "col", stride))
        stride *= 2
    while stride > 1:
        stride //= 2
        bit = (col_at // stride) % 2
        other = swap(part, "col", stride)
        first = jnp.where(bit == 0, part, other)
        second = jnp.where(bit == 0, other, part)
        part = jnp.concatenate([first, second], 0)
    return part[:rows]


def pack_columns(grad, width):
    rows, cols = grad.shape
    quarter = grad.astype(BF16).reshape(4, rows // 4, cols)
    return jnp.concatenate(
        [quarter[:, :, at : at + width] for at in range(0, cols, width)], 1
    )


def unpack_columns(packed, cols):
    width = packed.shape[1]
    count = cols // width
    rows = packed.shape[0] // count
    return jnp.concatenate([packed[i * rows : (i + 1) * rows] for i in range(count)], 1)


def per_device(
    pixels,
    timestamps,
    frame_count,
    visible,
    halo_reach,
    w_patch,
    b_patch,
    gain_one,
    shift_one,
    w_qkv,
    b_query,
    b_value,
    w_out,
    b_out,
    gain_two,
    shift_two,
    w_up,
    b_up,
    w_down,
    b_down,
    w_dec,
    b_dec,
    w_pix,
    b_pix,
    cotangent,
):
    tile_rows, tile_cols, frames, pix_width = pixels.shape
    model_width = w_patch.shape[1]
    tokens = tile_rows * tile_cols * frames
    row_places = (
        lax.axis_index("row") * tile_rows + jnp.arange(tile_rows, dtype=jnp.int32)
    ).astype(F32)
    col_places = (
        lax.axis_index("col") * tile_cols + jnp.arange(tile_cols, dtype=jnp.int32)
    ).astype(F32)
    time_part = sin_cos(timestamps[0, 0].astype(F32), model_width // 16 * 4)
    row_part = sin_cos(row_places, model_width // 16 * 6)
    col_part = sin_cos(col_places, model_width // 16 * 6)
    grid_shape = (tile_rows, frames, tile_cols)
    position = jnp.concatenate(
        [
            jnp.broadcast_to(time_part[None, :, None], grid_shape + (time_part.shape[-1],)),
            jnp.broadcast_to(row_part[:, None, None], grid_shape + (row_part.shape[-1],)),
            jnp.broadcast_to(col_part[None, None], grid_shape + (col_part.shape[-1],)),
        ],
        -1,
    ).reshape(tokens, model_width)
    frame_index = jnp.arange(frames, dtype=jnp.int32)
    own_ok = (
        (frame_index[None, :, None] < frame_count[0, 0]) & (visible.transpose(0, 2, 1) == 1)
    ).astype(BF16)
    flat_pixels = pixels.transpose(0, 2, 1, 3).reshape(tokens, pix_width)
    grad_pixels_out = cotangent.transpose(0, 2, 1, 3).reshape(tokens, pix_width)
    stream_one = mat_low(flat_pixels, w_patch) + b_patch.astype(F32) + position
    normed_one = layer_norm(stream_one, gain_one.astype(F32), shift_one.astype(F32)).astype(BF16)

    grid_one = normed_one.reshape(grid_shape + (model_width,))
    side = tile_rows * frames * HALO
    band = HALO * frames * tile_cols

    def with_flags(rows, flags):
        line = jnp.zeros((8 * model_width,), BF16).at[: flags.size].set(flags.reshape(-1))
        return jnp.concatenate([rows.reshape(-1, model_width), line.reshape(8, model_width)], 0)

    upper = rotate(with_flags(grid_one[tile_rows - HALO :], own_ok[tile_rows - HALO :]), "row", 1)
    lower = rotate(with_flags(grid_one[:HALO], own_ok[:HALO]), "row", -1)
    left = rotate(
        with_flags(grid_one[:, :, tile_cols - HALO :], own_ok[:, :, tile_cols - HALO :]), "col", 1
    )
    right = rotate(with_flags(grid_one[:, :, :HALO], own_ok[:, :, :HALO]), "col", -1)

    def flags_of(strip, count):
        return strip[-8:].reshape(-1)[:count]

    near = jnp.arange(HALO, dtype=jnp.int32)
    reach = halo_reach[0, 0]
    band_shape = (HALO, frames, tile_cols)
    side_shape = (tile_rows, frames, HALO)
    far_first = reach >= HALO - near
    near_first = reach >= near + 1
    keys = tokens + 2 * band + 2 * side
    key_total = -(-keys // LANES) * LANES
    spare = key_total - keys
    strip_ok = jnp.concatenate(
        [
            (flags_of(upper, band) > 0.5)
            & jnp.broadcast_to(far_first[:, None, None], band_shape).reshape(-1),
            (flags_of(lower, band) > 0.5)
            & jnp.broadcast_to(near_first[:, None, None], band_shape).reshape(-1),
            (flags_of(left, side) > 0.5)
            & jnp.broadcast_to(far_first[None, None, :], side_shape).reshape(-1),
            (flags_of(right, side) > 0.5)
            & jnp.broadcast_to(near_first[None, None, :], side_shape).reshape(-1),
            jnp.zeros((spare,), bool),
        ]
    )
    bias = jnp.where(
        jnp.concatenate([own_ok.reshape(-1) > 0.5, strip_ok]), 0.0, NEG_FILL
    ).astype(F32)
    strip_rows = jnp.concatenate(
        [
            upper[:band],
            lower[:band],
            left[:side],
            right[:side],
            jnp.zeros((spare, model_width), BF16),
        ],
        0,
    )

    qkv_own = mat_low(normed_one, w_qkv)
    kv_strip = mat_low(strip_rows, w_qkv[:, model_width:])
    query_rows = (qkv_own[:, :model_width] + b_query.astype(F32)).astype(BF16)
    key_rows = jnp.concatenate(
        [qkv_own[:, model_width : 2 * model_width], kv_strip[:, :model_width]], 0
    ).astype(BF16)
    value_rows = (
        jnp.concatenate([qkv_own[:, 2 * model_width :], kv_strip[:, model_width:]], 0)
        + b_value.astype(F32)
    ).astype(BF16)
    attended, log_total = attend(query_rows, key_rows, value_rows, bias[None, :])

    stream_two = stream_one + mat_low(attended, w_out) + b_out.astype(F32)
    normed_two = layer_norm(stream_two, gain_two.astype(F32), shift_two.astype(F32)).astype(BF16)
    hidden_pre = mat_low(normed_two, w_up) + b_up.astype(F32)
    hidden_act = gelu_exact(hidden_pre).astype(BF16)
    stream_out = stream_two + mat_low(hidden_act, w_down) + b_down.astype(F32)
    stream_low = stream_out.astype(BF16)
    decoded = (mat_low(stream_low, w_dec) + b_dec.astype(F32)).astype(BF16)
    pixel_out = (mat_low(decoded, w_pix) + b_pix.astype(F32)).astype(BF16)

    grad_w_pix = outer_sum(decoded, grad_pixels_out)
    grad_b_pix = column_sum(grad_pixels_out)
    grad_dec = times_transposed(grad_pixels_out, w_pix).astype(BF16)
    grad_w_dec = outer_sum(stream_low, grad_dec)
    grad_b_dec = column_sum(grad_dec)
    grad_stream = times_transposed(grad_dec, w_dec)
    grad_mlp = grad_stream.astype(BF16)
    grad_w_down = outer_sum(hidden_act, grad_mlp)
    grad_b_down = column_sum(grad_mlp)
    grad_act = times_transposed(grad_mlp, w_down)
    _, gelu_pull = jax.vjp(gelu_exact, hidden_pre)
    grad_pre = gelu_pull(grad_act)[0].astype(BF16)
    grad_w_up = outer_sum(normed_two, grad_pre)
    grad_b_up = column_sum(grad_pre)

    early = reduce_quarters(
        jnp.concatenate(
            [
                pack_columns(grad_w_down, model_width),
                pack_columns(grad_w_up, model_width),
                pack_columns(grad_w_pix, model_width),
            ],
            1,
        )
    )
    early_dec = reduce_quarters(pack_columns(grad_w_dec, grad_w_dec.shape[1]))

    grad_normed_two = times_transposed(grad_pre, w_up)
    back_two, grad_gain_two, grad_shift_two = norm_backward(
        stream_two, gain_two, shift_two, grad_normed_two
    )
    grad_stream_two = grad_stream + back_two
    grad_att = grad_stream_two.astype(BF16)
    grad_w_out = outer_sum(attended, grad_att)
    grad_b_out = column_sum(grad_att)
    grad_attended = times_transposed(grad_att, w_out).astype(BF16)
    grad_query, grad_keys, grad_values = attend_back(
        query_rows, key_rows, value_rows, grad_attended, attended, log_total, bias[:, None]
    )
    grad_b_query = column_sum(grad_query)
    grad_b_value = column_sum(grad_values)
    own_grad = jnp.concatenate([grad_query, grad_keys[:tokens], grad_values[:tokens]], 1)
    strip_grad = jnp.concatenate([grad_keys[tokens:], grad_values[tokens:]], 1)
    grad_strip = times_transposed(strip_grad, w_qkv[:, model_width:]).astype(BF16)
    from_below = rotate(grad_strip[:band], "row", -1)
    from_above = rotate(grad_strip[band : 2 * band], "row", 1)
    from_right = rotate(grad_strip[2 * band : 2 * band + side], "col", -1)
    from_left = rotate(grad_strip[2 * band + side : 2 * band + 2 * side], "col", 1)

    grad_w_qkv = outer_sum(normed_one, own_grad)
    grad_w_qkv = grad_w_qkv.at[:, model_width:].add(outer_sum(strip_rows, strip_grad))
    middle = reduce_quarters(
        jnp.concatenate(
            [pack_columns(grad_w_qkv, model_width), pack_columns(grad_w_out, model_width)], 1
        )
    )

    grad_normed_one = times_transposed(own_grad, w_qkv)
    grad_grid = grad_normed_one + jnp.concatenate([from_above, from_below], 0).astype(F32)
    sides = jnp.concatenate(
        [
            from_left.reshape(side_shape + (model_width,)),
            jnp.zeros((tile_rows, frames, tile_cols - 2 * HALO, model_width), BF16),
            from_right.reshape(side_shape + (model_width,)),
        ],
        2,
    ).reshape(tokens, model_width)
    grad_grid = grad_grid + sides.astype(F32)
    back_one, grad_gain_one, grad_shift_one = norm_backward(
        stream_one, gain_one, shift_one, grad_grid
    )
    grad_stream_one = grad_stream_two + back_one
    grad_b_patch = jnp.sum(grad_stream_one, 0)
    grad_emb = grad_stream_one.astype(BF16)
    grad_w_patch = outer_sum(flat_pixels, grad_emb)
    vectors = [
        grad_b_patch,
        grad_gain_one,
        grad_shift_one,
        grad_b_query,
        grad_b_value,
        grad_b_out,
        grad_gain_two,
        grad_shift_two,
        grad_b_up,
        grad_b_down,
        grad_b_dec,
        grad_b_pix,
    ]
    flat_vectors = jnp.concatenate([item.astype(BF16).reshape(4, -1) for item in vectors], 1)
    lines = -(-flat_vectors.shape[1] // model_width)
    flat_vectors = jnp.pad(
        flat_vectors, ((0, 0), (0, lines * model_width - flat_vectors.shape[1]))
    ).reshape(4, lines, model_width)
    patch_rows = pix_width // 4
    last = reduce_quarters(
        jnp.concatenate([pack_columns(grad_w_patch, model_width), flat_vectors], 1)
    )
    pixel_grad = times_transposed(grad_emb, w_patch).astype(BF16)

    sums = last[patch_rows : patch_rows + lines].reshape(-1).astype(F32)
    pieces = []
    at = 0
    for item in vectors:
        pieces.append(sums[at : at + item.size // 4])
        at += item.size // 4
    ff = w_up.shape[1]
    quarter = model_width // 4
    down_rows = ff // 4
    up_rows = quarter * (ff // model_width)
    share_patch = last[:patch_rows].astype(F32)
    qkv_rows = 3 * quarter
    share_qkv = unpack_columns(middle[:qkv_rows], 3 * model_width).astype(F32)
    share_out = middle[qkv_rows:].astype(F32)
    share_down = early[:down_rows].astype(F32)
    share_up = unpack_columns(early[down_rows : down_rows + up_rows], ff).astype(F32)
    share_pix = unpack_columns(early[down_rows + up_rows :], pix_width).astype(F32)
    share_dec = early_dec.astype(F32)

    def to_scene(flat):
        return flat.reshape(grid_shape + (pix_width,)).transpose(0, 2, 1, 3)

    return (
        to_scene(pixel_out),
        to_scene(pixel_grad),
        share_patch,
        pieces[0],
        pieces[1],
        pieces[2],
        share_qkv,
        pieces[3],
        pieces[4],
        share_out,
        pieces[5],
        pieces[6],
        pieces[7],
        share_up,
        pieces[8],
        share_down,
        pieces[9],
        share_dec,
        pieces[10],
        share_pix,
        pieces[11],
    )


def solution(mesh):
    tiles = P("row", "col", None, None)
    return jax.shard_map(
        per_device,
        mesh=mesh,
        in_specs=(
            tiles,
            P("row", "col", None),
            P("row", "col"),
            P("row", "col", None),
            P("row", "col"),
        )
        + (P(),) * 19
        + (tiles,),
        out_specs=(
            tiles,
            tiles,
            P("row", None),
            P("row"),
            P("row"),
            P("row"),
            P("row", None),
            P("row"),
            P("row"),
            P("row", None),
            P("row"),
            P("row"),
            P("row"),
            P("row", None),
            P("row"),
            P("row", None),
            P("row"),
            P("row", None),
            P("row"),
            P("row", None),
            P("row"),
        ),
        check_vma=False,
    )
```

```python
import functools
import math

import jax
import jax.numpy as jnp
import numpy as np
from jax import lax
from jax.experimental import pallas as pl
from jax.experimental.pallas import tpu as pltpu
from jax.sharding import PartitionSpec as P

HEAD_WIDTH = 64
HALO = 2
EPS = 1e-06
NEG_FILL = -1e30
BLOCK = 256
LANES = 128
FF_BLOCK = 512
SCALE = HEAD_WIDTH**-0.5
LOG_SCALE = SCALE * math.log2(math.e)
F32 = jnp.float32
BF16 = jnp.bfloat16


def dot_last(a, b):
    return lax.dot_general(a, b, (((1,), (1,)), ((), ())), preferred_element_type=F32)


def dot_plain(a, b):
    return lax.dot_general(a, b, (((1,), (0,)), ((), ())), preferred_element_type=F32)


def one_head(pair, head):
    lane = lax.broadcasted_iota(jnp.int32, pair.shape, 1)
    keep = (lane < HEAD_WIDTH) if head == 0 else (lane >= HEAD_WIDTH)
    return jnp.where(keep, pair, jnp.zeros_like(pair))


def diagonal(size):
    rows = lax.broadcasted_iota(jnp.int32, (size, size), 0)
    return rows == lax.broadcasted_iota(jnp.int32, (size, size), 1)


def row_of(ref):
    return ref[...].astype(F32).reshape(1, -1)


def params(megabytes):
    return pltpu.CompilerParams(vmem_limit_bytes=megabytes << 20)


def cost(flops, moved):
    return pl.CostEstimate(flops=flops, bytes_accessed=moved, transcendentals=0)


def whole(shape):
    return pl.BlockSpec(shape, lambda *_: (0,) * len(shape))


def held(shape):
    return pl.BlockSpec(shape, lambda *_: (0,) * len(shape), pipeline_mode=pl.Buffered(1))


def embed_kernel(
    stamps_ref,
    count_ref,
    visible_ref,
    pixels_ref,
    w_ref,
    b_ref,
    gain_ref,
    shift_ref,
    wave_ref,
    stream_ref,
    normed_ref,
    high_ref,
    low_ref,
    tail_ref,
    head_ref,
    flags_ref,
    edge_ref,
    time_ref,
    col_ref,
    n_ref,
):
    at_row = pl.program_id(0)
    width = w_ref.shape[1]
    frames, tile_rows, tile_cols = visible_ref.shape
    line = frames * tile_cols
    band = HALO * line

    lane = lax.broadcasted_iota(jnp.int32, (1, width), 1)
    t_end, r_end = width // 4, width // 4 + width * 3 // 8
    t_mid, r_mid, c_mid = width // 8, t_end + width * 3 // 16, r_end + width * 3 // 16

    def waves(places):
        angles = places * wave_ref[...]
        is_sin = (lane < t_mid) | ((lane >= t_end) & (lane < r_mid)) | ((lane >= r_end) & (lane < c_mid))
        return jnp.where(is_sin, jnp.sin(angles), jnp.cos(angles))

    @pl.when(at_row == 0)
    def _():
        slot = lax.broadcasted_iota(jnp.int32, (8, 1), 0)
        stamps = jnp.zeros((8, 1), F32)
        for f in range(frames):
            stamps = jnp.where(slot == f, stamps_ref[f].astype(F32), stamps)
        time_ref[...] = jnp.where(lane < t_end, waves(stamps), 0.0)
        cols = lax.axis_index("col") * tile_cols + lax.broadcasted_iota(
            jnp.int32, (tile_cols, 1), 0
        )
        col_ref[...] = jnp.where(lane >= r_end, waves(cols.astype(F32)), 0.0)
        frame_at = lax.broadcasted_iota(jnp.int32, visible_ref.shape, 0)
        ok = ((frame_at < count_ref[0]) & (visible_ref[...] == 1)).astype(F32)
        pieces = [ok[f, r : r + 1, :] for r in range(tile_rows) for f in range(frames)]
        flat = jnp.concatenate(pieces, 1)
        flags_ref[...] = jnp.broadcast_to(flat, flags_ref.shape)
        edge_ref[...] = jnp.zeros_like(edge_ref)
        nothing = [jnp.zeros((8 - frames, tile_cols), F32)]
        stacked = jnp.concatenate(
            sum((pieces[r * frames : (r + 1) * frames] + nothing for r in range(tile_rows)), []), 0
        )
        slot = lax.broadcasted_iota(jnp.int32, (8, tile_cols), 0)
        col = lax.broadcasted_iota(jnp.int32, (8, tile_cols), 1)
        last = HALO * tile_rows
        chunk = 8 * tile_rows
        edge_ref[0, last, :, :chunk] = dot_last(
            (col == slot + tile_cols - HALO).astype(F32), stacked
        )
        edge_ref[1, last, :, :chunk] = dot_last((col == slot).astype(F32), stacked)

    places = (lax.axis_index("row") * tile_rows + at_row).astype(F32)
    row_part = jnp.where((lane >= t_end) & (lane < r_end), waves(jnp.full((1, 1), places)), 0.0)
    base = row_of(b_ref) + row_part
    stream = dot_plain(pixels_ref[...], w_ref[...])
    position = jnp.concatenate(
        [col_ref[...] + (time_ref[f : f + 1, :] + base) for f in range(frames)], 0
    )
    stream = stream + position
    stream_ref[...] = stream
    centre = stream - jnp.mean(stream, -1, keepdims=True)
    spread = jnp.mean(centre * centre, -1, keepdims=True)
    normed = centre * lax.rsqrt(spread + EPS) * row_of(gain_ref) + row_of(shift_ref)
    low = normed.astype(BF16)
    normed_ref[...] = low
    n_ref[...] = low.astype(F32)
    for j in range(HALO):
        target = j * tile_rows + at_row
        for f in range(frames):
            near = f * tile_cols + j
            far = near + tile_cols - HALO
            edge_ref[0, target, f : f + 1, :] = n_ref[far : far + 1, :]
            edge_ref[1, target, f : f + 1, :] = n_ref[near : near + 1, :]

    @pl.when(at_row < HALO)
    def _():
        low_ref[pl.ds(pl.multiple_of(at_row * line, line), line), :] = low

    @pl.when(at_row >= tile_rows - HALO)
    def _():
        start = (at_row - (tile_rows - HALO)) * line
        high_ref[pl.ds(pl.multiple_of(start, line), line), :] = low

    @pl.when(at_row == tile_rows - 1)
    def _():
        tail_ref[...] = edge_ref[0].reshape(tail_ref.shape).astype(BF16)
        head_ref[...] = edge_ref[1].reshape(head_ref.shape).astype(BF16)
        zeros = jnp.zeros((8, width - band), BF16)
        total = flags_ref.shape[1]
        low_ref[band : band + 8, :band] = flags_ref[:, :band].astype(BF16)
        low_ref[band : band + 8, band:] = zeros
        high_ref[band : band + 8, :band] = flags_ref[:, total - band :].astype(BF16)
        high_ref[band : band + 8, band:] = zeros


def embed(stamps, count, visible, pixels, w, b, gain, shift, wave):
    tokens, depth = pixels.shape
    width = w.shape[1]
    frames, tile_rows, tile_cols = visible.shape
    line = frames * tile_cols
    band = HALO * line
    side = HALO * tile_rows * 8
    smem = pl.BlockSpec(memory_space=pltpu.SMEM)
    block = pl.BlockSpec((line, width), lambda r: (r, 0))
    return pl.pallas_call(
        embed_kernel,
        grid=(tile_rows,),
        in_specs=[
            smem,
            smem,
            whole(visible.shape),
            pl.BlockSpec((line, depth), lambda r: (r, 0)),
            held(w.shape),
            whole((width,)),
            whole((width,)),
            whole((width,)),
            whole((1, width)),
        ],
        out_specs=[
            block,
            block,
            whole((band + 8, width)),
            whole((band + 8, width)),
            whole((side + 8, width)),
            whole((side + 8, width)),
            whole((8, tokens)),
        ],
        out_shape=[
            jax.ShapeDtypeStruct((tokens, width), F32),
            jax.ShapeDtypeStruct((tokens, width), BF16),
            jax.ShapeDtypeStruct((band + 8, width), BF16),
            jax.ShapeDtypeStruct((band + 8, width), BF16),
            jax.ShapeDtypeStruct((side + 8, width), BF16),
            jax.ShapeDtypeStruct((side + 8, width), BF16),
            jax.ShapeDtypeStruct((8, tokens), F32),
        ],
        scratch_shapes=[
            pltpu.VMEM((2, side // 8 + 1, 8, width), F32),
            pltpu.VMEM((8, width), F32),
            pltpu.VMEM((tile_cols, width), F32),
            pltpu.VMEM((line, width), F32),
        ],
        compiler_params=params(60),
        cost_estimate=cost(2 * tokens * depth * width, 10 << 20),
        name="embed",
    )(stamps, count, visible, pixels, w, b, gain, shift, wave)


def decode_back_kernel(
    cot_ref, w_pix_ref, w_dec_ref, dec_ref, out_ref, mlp_ref, sum_pix, sum_dec, sum_down
):
    @pl.when(pl.program_id(0) == 0)
    def _():
        sum_pix[...] = jnp.zeros_like(sum_pix)
        sum_dec[...] = jnp.zeros_like(sum_dec)
        sum_down[...] = jnp.zeros_like(sum_down)

    grad_dec = dot_last(cot_ref[...], w_pix_ref[...]).astype(BF16)
    dec_ref[...] = grad_dec
    grad_out = dot_last(grad_dec, w_dec_ref[...])
    out_ref[...] = grad_out
    low = grad_out.astype(BF16)
    mlp_ref[...] = low
    sum_pix[...] += jnp.sum(cot_ref[...].astype(F32), 0, keepdims=True)
    sum_dec[...] += jnp.sum(grad_dec.astype(F32), 0, keepdims=True)
    sum_down[...] += jnp.sum(low.astype(F32), 0, keepdims=True)


def decode_back(cot, w_pix, w_dec):
    tokens, pix = cot.shape
    width, dec = w_dec.shape

    def block(size):
        return pl.BlockSpec((BLOCK, size), lambda i: (i, 0))

    return pl.pallas_call(
        decode_back_kernel,
        grid=(tokens // BLOCK,),
        in_specs=[block(pix), held(w_pix.shape), held(w_dec.shape)],
        out_specs=[
            block(dec),
            block(width),
            block(width),
            whole((1, pix)),
            whole((1, dec)),
            whole((1, width)),
        ],
        out_shape=[
            jax.ShapeDtypeStruct((tokens, dec), BF16),
            jax.ShapeDtypeStruct((tokens, width), F32),
            jax.ShapeDtypeStruct((tokens, width), BF16),
            jax.ShapeDtypeStruct((1, pix), F32),
            jax.ShapeDtypeStruct((1, dec), F32),
            jax.ShapeDtypeStruct((1, width), F32),
        ],
        compiler_params=params(16),
        cost_estimate=cost(2 * tokens * dec * (pix + width), 10 << 20),
        name="decode_back",
    )(cot, w_pix, w_dec)


def own_qkv_kernel(x_ref, w_ref, bq_ref, bv_ref, q_ref, k_ref, v_ref):
    width = x_ref.shape[1]
    x = x_ref[...]
    q_ref[...] = (dot_plain(x, w_ref[:, :width]) + row_of(bq_ref)).astype(BF16)
    k_ref[...] = dot_plain(x, w_ref[:, width : 2 * width]).astype(BF16)
    v_ref[...] = (dot_plain(x, w_ref[:, 2 * width :]) + row_of(bv_ref)).astype(BF16)


def own_qkv(x, w, bq, bv):
    tokens, width = x.shape
    block = pl.BlockSpec((BLOCK, width), lambda i: (i, 0))
    return pl.pallas_call(
        own_qkv_kernel,
        grid=(tokens // BLOCK,),
        in_specs=[block, held(w.shape), whole((width,)), whole((width,))],
        out_specs=[block] * 3,
        out_shape=[jax.ShapeDtypeStruct((tokens, width), BF16)] * 3,
        compiler_params=params(16),
        cost_estimate=cost(6 * tokens * width * width, 8 << 20),
        name="own_qkv",
    )(x, w, bq, bv)


def strip_kv_kernel(
    reach_ref, upper_ref, lower_ref, left_ref, right_ref, flags_ref, w_ref, bv_ref,
    k_ref, v_ref, rows_ref, bias_ref,
):
    band = upper_ref.shape[0] - 8
    side = left_ref.shape[0] - 8
    tokens = flags_ref.shape[1]
    total = rows_ref.shape[0]
    at = pl.program_id(0)

    @pl.when(at == 0)
    def _():
        rows_ref[:band, :] = upper_ref[:band, :]
        rows_ref[band : 2 * band, :] = lower_ref[:band, :]
        rows_ref[2 * band : 2 * band + side, :] = left_ref[:side, :]
        rows_ref[2 * band + side : 2 * (band + side), :] = right_ref[:side, :]
        if total > 2 * (band + side):
            rows_ref[2 * (band + side) :, :] = jnp.zeros(
                (total - 2 * (band + side), rows_ref.shape[1]), BF16
            )
        reach = reach_ref[0]
        line = band // HALO
        where = lax.broadcasted_iota(jnp.int32, (1, band), 1) // line
        near = (reach >= where + 1).astype(F32)
        far = (reach >= HALO - where).astype(F32)
        upper_ok = upper_ref[band : band + 1, :band].astype(F32) * far
        lower_ok = lower_ref[band : band + 1, :band].astype(F32) * near
        chunk = side // HALO
        spare = total - 2 * band
        source = lax.broadcasted_iota(jnp.int32, (LANES, spare), 0)
        target = lax.broadcasted_iota(jnp.int32, (LANES, spare), 1)
        sides = jnp.zeros((8, spare), F32)
        for j in range(HALO):
            for part, ref, need in ((0, left_ref, HALO - j), (1, right_ref, j + 1)):
                place = (target == source + part * side + j * chunk) & (source < chunk)
                line_ok = jnp.broadcast_to(
                    ref[side : side + 8, :LANES].astype(F32)[j : j + 1], (8, LANES)
                )
                moved = dot_plain(line_ok.astype(BF16), place.astype(BF16))
                sides = sides + jnp.where(reach >= need, moved, 0.0)
        bias_ref[:, :tokens] = jnp.where(flags_ref[...] > 0.5, 0.0, NEG_FILL)
        bias_ref[:, tokens : tokens + band] = jnp.broadcast_to(
            jnp.where(upper_ok > 0.5, 0.0, NEG_FILL), (8, band)
        )
        bias_ref[:, tokens + band : tokens + 2 * band] = jnp.broadcast_to(
            jnp.where(lower_ok > 0.5, 0.0, NEG_FILL), (8, band)
        )
        bias_ref[:, tokens + 2 * band :] = jnp.where(sides > 0.5, 0.0, NEG_FILL)
        k_ref[...] = dot_plain(rows_ref[...], w_ref[...]).astype(BF16)

    @pl.when(at == 1)
    def _():
        v_ref[...] = (dot_plain(rows_ref[...], w_ref[...]) + row_of(bv_ref)).astype(BF16)


def strip_kv(reach, upper, lower, left, right, flags, w, bv):
    width = w.shape[0]
    tokens = flags.shape[1]
    keys = 2 * (upper.shape[0] - 8) + 2 * (left.shape[0] - 8)
    total = -(-(tokens + keys) // LANES) * LANES - tokens
    strip = jax.ShapeDtypeStruct((total, width), BF16)
    return pl.pallas_call(
        strip_kv_kernel,
        grid=(2,),
        in_specs=[
            pl.BlockSpec(memory_space=pltpu.SMEM),
            whole(upper.shape),
            whole(lower.shape),
            whole(left.shape),
            whole(right.shape),
            whole(flags.shape),
            pl.BlockSpec((width, width), lambda i: (0, i + 1)),
            whole((width,)),
        ],
        out_specs=[whole((total, width))] * 3 + [whole((8, tokens + total))],
        out_shape=[strip] * 3 + [jax.ShapeDtypeStruct((8, tokens + total), F32)],
        compiler_params=params(16),
        cost_estimate=cost(4 * total * width * width, 8 << 20),
        name="strip_kv",
    )(reach, upper, lower, left, right, flags, w, bv)


def attend_kernel(
    q_ref, k_ref, v_ref, ks_ref, vs_ref, bias_ref, out_ref, log_ref, s_ref, keys_ref, values_ref
):
    tokens = q_ref.shape[0]
    keys_ref[:tokens, :] = k_ref[...]
    keys_ref[tokens:, :] = ks_ref[...]
    values_ref[:tokens, :] = v_ref[...]
    values_ref[tokens:, :] = vs_ref[...]
    eye = diagonal(BLOCK)
    lane = lax.broadcasted_iota(jnp.int32, (BLOCK, LANES), 1)

    def step(i, carry):
        at = pl.multiple_of(i * BLOCK, BLOCK)
        q = q_ref[pl.ds(at, BLOCK), :]
        mixed = []
        for head in range(2):
            q_head = one_head(q, head)
            s_ref[head] = dot_last(q_head, keys_ref[...]) + bias_ref[0:1, :]
            own = dot_last(q_head, keys_ref[pl.ds(at, BLOCK), :])
            s_ref[head, :, pl.ds(at, BLOCK)] = jnp.where(
                eye, own, own + bias_ref[0:1, pl.ds(at, BLOCK)]
            )
            scores = s_ref[head]
            top = jnp.max(scores, axis=1, keepdims=True)
            weights = jnp.exp2(scores * LOG_SCALE - top * LOG_SCALE)
            total = jnp.sum(weights, axis=1, keepdims=True)
            mixed.append(dot_plain(weights.astype(BF16), values_ref[...]) / total)
            log_ref[0, head, pl.ds(at, BLOCK)] = (top * LOG_SCALE + jnp.log2(total))[:, 0]
        out_ref[pl.ds(at, BLOCK), :] = jnp.where(lane < HEAD_WIDTH, mixed[0], mixed[1]).astype(
            out_ref.dtype
        )
        return carry

    lax.fori_loop(0, tokens // BLOCK, step, 0)


def attend(q, k, v, ks, vs, bias):
    tokens, width = q.shape
    keys = tokens + ks.shape[0]
    pairs = width // LANES
    own = pl.BlockSpec((tokens, LANES), lambda p: (0, p))
    strip = pl.BlockSpec((keys - tokens, LANES), lambda p: (0, p))
    return pl.pallas_call(
        attend_kernel,
        grid=(pairs,),
        in_specs=[own, own, own, strip, strip, whole((8, keys))],
        out_specs=[own, pl.BlockSpec((1, 2, tokens), lambda p: (p, 0, 0))],
        out_shape=[
            jax.ShapeDtypeStruct((tokens, width), F32),
            jax.ShapeDtypeStruct((pairs, 2, tokens), F32),
        ],
        scratch_shapes=[
            pltpu.VMEM((2, BLOCK, keys), F32),
            pltpu.VMEM((keys, LANES), BF16),
            pltpu.VMEM((keys, LANES), BF16),
        ],
        compiler_params=params(24),
        cost_estimate=cost(16 * tokens * keys * width, 8 << 20),
        name="attend",
    )(q, k, v, ks, vs, bias)


def attend_back_kernel(
    q_ref, k_ref, v_ref, ks_ref, vs_ref, do_ref, o_ref, log_ref, bias_ref,
    dq_ref, dk_ref, dv_ref, dks_ref, dvs_ref, sum_q, sum_v,
    keys_ref, values_ref, kt_ref, dk_sum, dv_sum, mask_ref,
):
    tokens = q_ref.shape[0]
    keys_ref[:tokens, :] = k_ref[...]
    keys_ref[tokens:, :] = ks_ref[...]
    values_ref[:tokens, :] = v_ref[...]
    values_ref[tokens:, :] = vs_ref[...]
    kt_ref[...] = keys_ref[...].T

    @pl.when(pl.program_id(0) == 0)
    def _():
        mask_ref[...] = bias_ref[...].T[:, 0:1]

    eye = diagonal(BLOCK)
    dk_sum[...] = jnp.zeros_like(dk_sum)
    dv_sum[...] = jnp.zeros_like(dv_sum)

    def step(i, carry):
        at = pl.multiple_of(i * BLOCK, BLOCK)
        q = q_ref[pl.ds(at, BLOCK), :]
        do = do_ref[pl.ds(at, BLOCK), :]
        product = (do.astype(F32) * o_ref[pl.ds(at, BLOCK), :]).T
        parts = []
        for head in range(2):
            delta = jnp.sum(
                product[head * HEAD_WIDTH : (head + 1) * HEAD_WIDTH], axis=0, keepdims=True
            )
            q_head = one_head(q, head)
            do_head = one_head(do, head)
            log_total = log_ref[0, pl.ds(head, 1), pl.ds(at, BLOCK)]
            scores = dot_last(keys_ref[...], q_head) + mask_ref[...]
            weights = jnp.exp2(scores * LOG_SCALE - log_total)
            back = dot_last(values_ref[...], do_head)
            grad = (weights * (back - delta)).astype(BF16)
            own_scores = dot_last(keys_ref[pl.ds(at, BLOCK), :], q_head)
            own = jnp.where(
                eye & (mask_ref[pl.ds(at, BLOCK), :] < 0),
                jnp.exp2(own_scores * LOG_SCALE - log_total),
                0.0,
            )
            own_back = dot_last(values_ref[pl.ds(at, BLOCK), :], do_head)
            own_grad = (own * (own_back - delta)).astype(BF16)
            dv_sum[...] += dot_plain(weights.astype(BF16), do_head)
            dv_sum[pl.ds(at, BLOCK), :] += dot_plain(own.astype(BF16), do_head)
            dk_sum[...] += dot_plain(grad, q_head)
            dk_sum[pl.ds(at, BLOCK), :] += dot_plain(own_grad, q_head)
            parts.append(
                dot_plain(kt_ref[...], grad) + dot_plain(kt_ref[:, pl.ds(at, BLOCK)], own_grad)
            )
        joined = jnp.concatenate([parts[0][:HEAD_WIDTH], parts[1][HEAD_WIDTH:]], axis=0)
        dq_ref[pl.ds(at, BLOCK), :] = (joined.T * SCALE).astype(BF16)
        return carry

    lax.fori_loop(0, tokens // BLOCK, step, 0)
    dk = (dk_sum[...] * SCALE).astype(BF16)
    dv = dv_sum[...].astype(BF16)
    dk_ref[...] = dk[:tokens]
    dks_ref[...] = dk[tokens:]
    dv_ref[...] = dv[:tokens]
    dvs_ref[...] = dv[tokens:]
    sum_q[...] = jnp.sum(dq_ref[...].astype(F32), 0, keepdims=True)
    sum_v[...] = jnp.sum(dv.astype(F32), 0, keepdims=True)


def attend_back(q, k, v, ks, vs, do, o, log_total, bias, first, count, before, after):
    tokens, width = q.shape
    keys = tokens + ks.shape[0]
    own = pl.BlockSpec((tokens, LANES), lambda p: (0, p + first))
    strip = pl.BlockSpec((keys - tokens, LANES), lambda p: (0, p + first))
    line = pl.BlockSpec((1, LANES), lambda p: (0, p + first))
    return run(
        attend_back_kernel, "attend_back", (q, k, v, ks, vs, do, o, log_total, bias),
        [jax.ShapeDtypeStruct((tokens, width), BF16)] * 3
        + [jax.ShapeDtypeStruct((keys - tokens, width), BF16)] * 2
        + [jax.ShapeDtypeStruct((1, width), F32)] * 2,
        [
            own, own, own, strip, strip, own, own,
            pl.BlockSpec((1, 2, tokens), lambda p: (p + first, 0, 0)),
            whole((8, keys)),
        ],
        [own, own, own, strip, strip, line, line], grid=(count,), after=tuple(before) + tuple(after),
        aliases={9 + i: i for i in range(len(before))},
        estimate=cost(24 * tokens * keys * LANES * count, 3 * count << 20),
        scratch=[
            pltpu.VMEM((keys, LANES), BF16),
            pltpu.VMEM((keys, LANES), BF16),
            pltpu.VMEM((LANES, keys), BF16),
            pltpu.VMEM((keys, LANES), F32),
            pltpu.VMEM((keys, LANES), F32),
            pltpu.VMEM((keys, 1), F32),
        ],
    )


def dot_first(a, b):
    return lax.dot_general(a, b, (((0,), (0,)), ((), ())), preferred_element_type=F32)


def mlp_kernel(
    one_ref, att_ref, gout_ref, w_out_ref, b_out_ref, gain_ref, shift_ref, w_up_ref, b_up_ref,
    w_down_ref, b_down_ref, w_dec_ref, b_dec_ref, w_pix_ref, b_pix_ref,
    pix_ref, normed_ref, act_ref, gup_ref, low_ref, decoded_ref, attended_ref,
    gtwo_ref, gatt_ref, gattended_ref, sum_up, sum_out, sum_gain, sum_shift,
):
    @pl.when(pl.program_id(0) == 0)
    def _():
        for ref in (sum_up, sum_out, sum_gain, sum_shift):
            ref[...] = jnp.zeros_like(ref)

    ff = w_up_ref.shape[1]
    attended = att_ref[...].astype(BF16)
    attended_ref[...] = attended
    two = one_ref[...] + dot_plain(attended, w_out_ref[...]) + row_of(b_out_ref)
    centre = two - jnp.mean(two, -1, keepdims=True)
    inverse = lax.rsqrt(jnp.mean(centre * centre, -1, keepdims=True) + EPS)
    gain = row_of(gain_ref)
    normed = (centre * inverse * gain + row_of(shift_ref)).astype(BF16)
    normed_ref[...] = normed
    gout = gout_ref[...]
    gmlp = gout.astype(BF16)
    out = two + row_of(b_down_ref)
    gnormed = jnp.zeros_like(two)
    for at in range(0, ff, FF_BLOCK):
        cols = slice(at, at + FF_BLOCK)
        up = dot_plain(normed, w_up_ref[:, cols]) + b_up_ref[cols].astype(F32).reshape(1, -1)
        bell = 0.5 * (1.0 + lax.erf(up * math.sqrt(0.5)))
        act = (up * bell).astype(BF16)
        slope = bell + up * (jnp.exp2(up * up * (-0.5 * math.log2(math.e))) * (2 * math.pi) ** -0.5)
        act_ref[:, cols] = act
        out = out + dot_plain(act, w_down_ref[cols, :])
        gup = (dot_last(gmlp, w_down_ref[cols, :]) * slope).astype(BF16)
        gup_ref[:, cols] = gup
        sum_up[:, cols] += jnp.sum(gup.astype(F32), 0, keepdims=True)
        gnormed = gnormed + dot_last(gup, w_up_ref[:, cols])
    low = out.astype(BF16)
    low_ref[...] = low
    decoded = (dot_plain(low, w_dec_ref[...]) + row_of(b_dec_ref)).astype(BF16)
    decoded_ref[...] = decoded
    pix_ref[...] = (dot_plain(decoded, w_pix_ref[...]) + row_of(b_pix_ref)).astype(BF16)
    hat = centre * inverse
    sum_gain[...] += jnp.sum(gnormed * hat, 0, keepdims=True)
    sum_shift[...] += jnp.sum(gnormed, 0, keepdims=True)
    scaled = gnormed * gain
    back = inverse * (
        scaled
        - jnp.mean(scaled, -1, keepdims=True)
        - hat * jnp.mean(scaled * hat, -1, keepdims=True)
    )
    gtwo = gout + back
    gtwo_ref[...] = gtwo
    gatt = gtwo.astype(BF16)
    gatt_ref[...] = gatt
    sum_out[...] += jnp.sum(gatt.astype(F32), 0, keepdims=True)
    gattended_ref[...] = dot_last(gatt, w_out_ref[...]).astype(BF16)


def mlp(one, att, gout, w_out, b_out, gain, shift, w_up, b_up, w_down, b_down, w_dec, b_dec, w_pix, b_pix):
    tokens, width = one.shape
    ff, dec, pix = w_up.shape[1], w_dec.shape[1], w_pix.shape[1]

    def block(size):
        return pl.BlockSpec((BLOCK, size), lambda i: (i, 0))

    def out(size, kind=BF16):
        return jax.ShapeDtypeStruct((tokens, size), kind)

    def vector(size):
        return jax.ShapeDtypeStruct((1, size), F32)

    weights = [w_out, b_out, gain, shift, w_up, b_up, w_down, b_down, w_dec, b_dec, w_pix, b_pix]
    return pl.pallas_call(
        mlp_kernel,
        grid=(tokens // BLOCK,),
        in_specs=[block(width)] * 3 + [held(item.shape) for item in weights],
        out_specs=[
            block(pix), block(width), block(ff), block(ff), block(width), block(dec), block(width),
            block(width), block(width), block(width),
            whole((1, ff)), whole((1, width)), whole((1, width)), whole((1, width)),
        ],
        out_shape=[
            out(pix), out(width), out(ff), out(ff), out(width), out(dec), out(width),
            out(width, F32), out(width), out(width),
            vector(ff), vector(width), vector(width), vector(width),
        ],
        compiler_params=params(48),
        cost_estimate=cost(2 * tokens * width * (2 * width + 4 * ff + dec) + 2 * tokens * dec * pix, 40 << 20),
        name="mlp",
    )(one, att, gout, *weights)


def quarter_at(step, core):
    return 2 * (step % 2) + jnp.where(step < 2, 1 - core, core)


def lay_columns(ref, at, values, width):
    rows, cols = values.shape
    for i in range(cols // width):
        ref[0, at + i * rows : at + (i + 1) * rows, :] = values[:, i * width : (i + 1) * width]


def padded(rows):
    granule = 8 * lax.axis_size("col")
    return -(-rows // granule) * granule


def blank(ref, at):
    if at < ref.shape[1]:
        ref[0, at:, :] = jnp.zeros((ref.shape[1] - at, ref.shape[2]), BF16)


def pair_specs(rows, width):
    return [
        pl.BlockSpec((1, rows, width), lambda s, c: (jnp.minimum(s, 1), 0, 0)),
        pl.BlockSpec((1, rows, width), lambda s, c: (jnp.maximum(s - 2, 0), 0, 0)),
    ]


def grads_down_kernel(
    places, act_ref, gmlp_ref, decoded_ref, cot_ref, low_ref, gdec_ref, send_ref, keep_ref, lt_ref
):
    step = pl.program_id(0)

    @pl.when(step == 0)
    def _():
        lt_ref[...] = low_ref[...].T

    width = gmlp_ref.shape[1]
    part = width // 4
    rows = pl.ds(pl.multiple_of(quarter_at(step, places[0]) * part, part), part)
    down = dot_first(act_ref[...], gmlp_ref[...]).astype(BF16)
    pix = dot_first(decoded_ref[...], cot_ref[...]).astype(BF16)
    dec = dot_plain(lt_ref[rows, :], gdec_ref[...]).astype(BF16)
    at = down.shape[0] + pix.size // width
    cut, side = part * 2 // 3, dec.shape[1]
    rest = width - side
    for is_sent, ref in ((True, send_ref), (False, keep_ref)):

        @pl.when((step < 2) == is_sent)
        def _():
            ref[0, : down.shape[0], :] = down
            lay_columns(ref, down.shape[0], pix, width)
            ref[0, at : at + cut, :side] = dec[:cut]
            ref[0, at : at + part - cut, side:] = dec[cut:, :rest]
            ref[0, at + part - cut : at + cut, side:] = dec[cut:, rest:]
            blank(ref, at + cut)


def grads_down(places, act, gmlp, decoded, cot, low, gdec):
    tokens, ff = act.shape
    width, dec, pix = gmlp.shape[1], decoded.shape[1], cot.shape[1]
    rows = padded(ff // 4 + (dec // 4) * (pix // width) + dec // 4)
    return run(
        grads_down_kernel, "grads_down", (act, gmlp, decoded, cot, low, gdec),
        [jax.ShapeDtypeStruct((2, rows, width), BF16)] * 2,
        [
            pl.BlockSpec((tokens, ff // 4), lambda s, c: (0, quarter_at(s, c[0]))),
            held(gmlp.shape),
            pl.BlockSpec((tokens, dec // 4), lambda s, c: (0, quarter_at(s, c[0]))),
            held(cot.shape),
            held(low.shape),
            held(gdec.shape),
        ],
        pair_specs(rows, width), grid=(4,), places=places,
        estimate=cost(2 * tokens * (ff * width + dec * (pix + width)), 20 << 20),
        megabytes=32, scratch=[pltpu.VMEM((width, tokens), BF16)],
    )


def grads_up_kernel(
    places, normed_ref, gup_ref, att_ref, gatt_ref, send_ref, keep_ref, nt_ref, at_ref
):
    step = pl.program_id(0)

    @pl.when(step == 0)
    def _():
        nt_ref[...] = normed_ref[...].T
        at_ref[...] = att_ref[...].T

    width = normed_ref.shape[1]
    part = width // 4
    rows = pl.ds(pl.multiple_of(quarter_at(step, places[0]) * part, part), part)
    up = dot_plain(nt_ref[rows, :], gup_ref[...]).astype(BF16)
    out = dot_plain(at_ref[rows, :], gatt_ref[...]).astype(BF16)
    at = up.size // width
    for is_sent, ref in ((True, send_ref), (False, keep_ref)):

        @pl.when((step < 2) == is_sent)
        def _():
            lay_columns(ref, 0, up, width)
            ref[0, at : at + part, :] = out
            blank(ref, at + part)


def grads_up(places, normed, gup, attended, gatt, after):
    tokens, width = normed.shape
    ff = gup.shape[1]
    rows = padded(ff // 4 + width // 4)
    operands = (normed, gup, attended, gatt)
    return run(
        grads_up_kernel, "grads_up", operands, [jax.ShapeDtypeStruct((2, rows, width), BF16)] * 2,
        [held(item.shape) for item in operands], pair_specs(rows, width), grid=(4,), places=places,
        after=after, estimate=cost(2 * tokens * width * (ff + width), 16 << 20),
        scratch=[pltpu.VMEM((width, tokens), BF16)] * 2,
    )


def strip_back_kernel(dk_ref, dv_ref, w_ref, upper_ref, lower_ref, left_ref, right_ref):
    width = w_ref.shape[0]
    band, side = upper_ref.shape[0], left_ref.shape[0]
    back = (
        dot_last(dk_ref[...], w_ref[:, width : 2 * width]) + dot_last(dv_ref[...], w_ref[:, 2 * width :])
    ).astype(BF16)
    upper_ref[...] = back[:band]
    lower_ref[...] = back[band : 2 * band]
    left_ref[...] = back[2 * band : 2 * band + side]
    right_ref[...] = back[2 * band + side : 2 * (band + side)]


def strip_back(dk, dv, w, band, side, after):
    total, width = dk.shape
    sizes = (band, band, side, side)
    return run(
        strip_back_kernel, "strip_back", (dk, dv, w),
        [jax.ShapeDtypeStruct((rows, width), BF16) for rows in sizes],
        [whole(item.shape) for item in (dk, dv, w)], [whole((rows, width)) for rows in sizes],
        after=after, estimate=cost(4 * total * width * width, 8 << 20), megabytes=24,
    )


def grads_qkv_kernel(
    core_ref, normed_ref, rows_ref, dq_ref, dk_ref, dv_ref, dks_ref, dvs_ref,
    send_ref, keep_ref, nt_ref, st_ref,
):
    step = pl.program_id(0)

    @pl.when(step == 0)
    def _():
        nt_ref[...] = normed_ref[...].T
        st_ref[...] = rows_ref[...].T

    width = normed_ref.shape[1]
    part = width // 4
    rows = pl.ds(pl.multiple_of(quarter_at(step, core_ref[0]) * part, part), part)
    own, strip = nt_ref[rows, :], st_ref[rows, :]
    parts = (
        dot_plain(own, dq_ref[...]),
        dot_plain(own, dk_ref[...]) + dot_plain(strip, dks_ref[...]),
        dot_plain(own, dv_ref[...]) + dot_plain(strip, dvs_ref[...]),
    )
    for is_sent, ref in ((True, send_ref), (False, keep_ref)):

        @pl.when((step < 2) == is_sent)
        def _():
            for i, values in enumerate(parts):
                ref[0, i * part : (i + 1) * part, :] = values.astype(BF16)
            blank(ref, len(parts) * part)


def grads_qkv(places, normed, rows, dq, dk, dv, dks, dvs, after):
    tokens, width = normed.shape
    total = rows.shape[0]
    operands = (normed, rows, dq, dk, dv, dks, dvs)
    size = padded(3 * width // 4)
    return run(
        grads_qkv_kernel, "grads_qkv", operands, [jax.ShapeDtypeStruct((2, size, width), BF16)] * 2,
        [held(item.shape) for item in operands], pair_specs(size, width), grid=(4,), places=places,
        after=after, estimate=cost(2 * width * width * (3 * tokens + 2 * total), 20 << 20),
        scratch=[
            pltpu.VMEM((width, tokens), BF16),
            pltpu.VMEM((width, total), BF16),
        ],
    )


def embed_back_kernel(
    frames, stream_ref, dq_ref, dk_ref, dv_ref, w_ref, gtwo_ref, gain_ref, above_ref, below_ref, left_ref,
    right_ref, emb_ref, sum_patch, sum_gain, sum_shift, g_ref, side_ref,
):
    at_row = pl.program_id(0)
    width = stream_ref.shape[1]
    line = stream_ref.shape[0]
    tile_rows = left_ref.shape[0] // (8 * HALO)
    tile_cols = line // frames

    @pl.when(at_row == 0)
    def _():
        side_ref[0] = left_ref[...].astype(F32).reshape(side_ref.shape[1:])
        side_ref[1] = right_ref[...].astype(F32).reshape(side_ref.shape[1:])
        for ref in (sum_patch, sum_gain, sum_shift):
            ref[...] = jnp.zeros_like(ref)

    g_ref[...] = (
        dot_last(dq_ref[...], w_ref[:, :width])
        + dot_last(dk_ref[...], w_ref[:, width : 2 * width])
        + dot_last(dv_ref[...], w_ref[:, 2 * width :])
    )

    @pl.when(at_row < HALO)
    def _():
        g_ref[...] += above_ref[pl.ds(pl.multiple_of(at_row * line, line), line), :].astype(F32)

    @pl.when(at_row >= tile_rows - HALO)
    def _():
        start = (at_row - (tile_rows - HALO)) * line
        g_ref[...] += below_ref[pl.ds(pl.multiple_of(start, line), line), :].astype(F32)

    for j in range(HALO):
        source = j * tile_rows + at_row
        for f in range(frames):
            near = f * tile_cols + j
            far = near + tile_cols - HALO
            g_ref[near : near + 1, :] += side_ref[0, source, f : f + 1, :]
            g_ref[far : far + 1, :] += side_ref[1, source, f : f + 1, :]
    stream = stream_ref[...]
    grad = g_ref[...]
    centre = stream - jnp.mean(stream, -1, keepdims=True)
    inverse = lax.rsqrt(jnp.mean(centre * centre, -1, keepdims=True) + EPS)
    hat = centre * inverse
    sum_gain[...] += jnp.sum(grad * hat, 0, keepdims=True)
    sum_shift[...] += jnp.sum(grad, 0, keepdims=True)
    scaled = grad * row_of(gain_ref)
    one = gtwo_ref[...] + inverse * (
        scaled
        - jnp.mean(scaled, -1, keepdims=True)
        - hat * jnp.mean(scaled * hat, -1, keepdims=True)
    )
    sum_patch[...] += jnp.sum(one, 0, keepdims=True)
    emb_ref[...] = one.astype(BF16)


def embed_back(stream, dq, dk, dv, w, gtwo, gain, above, below, left, right, tile_rows, frames, hold):
    tokens, width = stream.shape
    line = tokens // tile_rows
    block = pl.BlockSpec((line, width), lambda r: (r, 0))
    vector = jax.ShapeDtypeStruct((1, width), F32)
    return run(
        functools.partial(embed_back_kernel, frames), "embed_back",
        (stream, dq, dk, dv, w, gtwo, gain, above, below, left, right),
        [jax.ShapeDtypeStruct((tokens, width), BF16)] + [vector] * 3,
        [
            block, block, block, block, held(w.shape), block, whole((width,)),
            whole(above.shape), whole(below.shape), whole(left.shape), whole(right.shape),
        ],
        [block] + [whole((1, width))] * 3, grid=(tile_rows,), hold=hold,
        estimate=cost(6 * tokens * width * width, 16 << 20),
        scratch=[pltpu.VMEM((line, width), F32), pltpu.VMEM((2, left.shape[0] // 8, 8, width), F32)],
    )


def lay_vectors(ref, at, vectors, quarter):
    width = ref.shape[2]
    ref[0, at:, :] = jnp.zeros((ref.shape[1] - at, width), BF16)
    lines = []
    for item in vectors:
        part = item.shape[1] // 4
        mine = jnp.zeros((1, part), F32)
        for q in range(4):
            mine = jnp.where(quarter == q, item[:, q * part : (q + 1) * part], mine)
        if part < width:
            mine = jnp.concatenate([mine, jnp.zeros((1, width - part), F32)], 1)
        lines.append(mine)
    pad = -(-len(lines) // 16) * 16 - len(lines)
    block = jnp.concatenate(lines + [jnp.zeros((pad, width), F32)], 0)
    high = block.astype(BF16)
    ref[0, at : at + block.shape[0], :] = high
    ref[0, at + block.shape[0] : at + 2 * block.shape[0], :] = (block - high.astype(F32)).astype(BF16)


def grads_patch_kernel(core_ref, pixels_ref, emb_ref, *refs):
    vectors, (send_ref, keep_ref) = refs[:-2], refs[-2:]
    step = pl.program_id(0)
    quarter = quarter_at(step, core_ref[0])
    patch = dot_first(pixels_ref[...], emb_ref[...]).astype(BF16)
    for is_sent, ref in ((True, send_ref), (False, keep_ref)):

        @pl.when((step < 2) == is_sent)
        def _():
            ref[0, : patch.shape[0], :] = patch
            lay_vectors(ref, patch.shape[0], [item[...] for item in vectors], quarter)


def grads_patch(places, pixels, emb, vectors, after):
    tokens, pix = pixels.shape
    width = emb.shape[1]
    rows = padded(pix // 4 + 64)
    return run(
        grads_patch_kernel, "grads_patch", (pixels, emb, *vectors),
        [jax.ShapeDtypeStruct((2, rows, width), BF16)] * 2,
        [
            pl.BlockSpec((tokens, pix // 4), lambda s, c: (0, quarter_at(s, c[0]))),
            held(emb.shape),
        ]
        + [whole(item.shape) for item in vectors],
        pair_specs(rows, width), grid=(4,), places=places, after=after,
        estimate=cost(2 * tokens * pix * width, 8 << 20),
    )


def pixel_back_kernel(emb_ref, w_ref, out_ref):
    out_ref[...] = dot_last(emb_ref[...], w_ref[...]).astype(BF16)


def pixel_back(emb, w, after):
    tokens, width = emb.shape
    pix = w.shape[0]
    return run(
        pixel_back_kernel, "pixel_back", (emb, w), jax.ShapeDtypeStruct((tokens, pix), BF16),
        [pl.BlockSpec((BLOCK, width), lambda i: (i, 0)), held(w.shape)],
        pl.BlockSpec((BLOCK, pix), lambda i: (i, 0)), grid=(tokens // BLOCK,), after=after,
        estimate=cost(2 * tokens * pix * width, 8 << 20),
    )


def swap(value, axis, stride):
    count = lax.axis_size(axis)
    return lax.ppermute(value, axis, [(i, i ^ stride) for i in range(count)])


def rotate(value, axis, steps):
    count = lax.axis_size(axis)
    return lax.ppermute(value, axis, [(i, (i + steps) % count) for i in range(count)])


def run(
    kernel, name, operands, out_shape, in_specs, out_specs, *, grid=(1,), places=None, after=(), hold=(),
    estimate=None, scratch=(), megabytes=28, aliases=None,
):
    scalars = () if places is None else (places,)
    count = len(scalars) + len(operands)
    extra = tuple(after) + tuple(hold)
    any_space = pl.BlockSpec(memory_space=pl.ANY)
    shapes = list(out_shape) if isinstance(out_shape, (list, tuple)) else [out_shape]
    specs = list(out_specs) if isinstance(out_specs, (list, tuple)) else [out_specs]
    own = len(shapes)

    def body(*refs):
        results = refs[count + len(extra) :]
        kernel(*refs[:count], *results[:own], *results[own + len(hold) :])

    at = count + len(after)
    aliases = dict(aliases or {})
    aliases.update({at + i: own + i for i in range(len(hold))})
    results = pl.pallas_call(
        body,
        grid_spec=pltpu.PrefetchScalarGridSpec(
            num_scalar_prefetch=len(scalars),
            grid=grid,
            in_specs=list(in_specs) + [any_space] * len(extra),
            out_specs=specs + [any_space] * len(hold),
            scratch_shapes=list(scratch),
        ),
        out_shape=shapes + [jax.ShapeDtypeStruct(item.shape, item.dtype) for item in hold],
        input_output_aliases=aliases,
        compiler_params=params(megabytes),
        cost_estimate=estimate,
        name=name,
    )(*scalars, *operands, *extra)
    return results[0] if len(results) == 1 else results


def add_across_kernel(places, keep_ref, came_ref, out_ref):
    out_ref[...] = (keep_ref[0].astype(F32) + came_ref[0].astype(F32)).astype(BF16)


def add_across(places, keep, came, after):
    rows, width = keep.shape[1:]
    block = pl.BlockSpec((1, rows // 2, width), lambda i, p: (1 - p[1], i, 0))
    return run(
        add_across_kernel, "add_across", (keep, came), jax.ShapeDtypeStruct((rows, width), BF16),
        [block, block], pl.BlockSpec((rows // 2, width), lambda i, p: (i, 0)),
        grid=(2,), places=places, after=after, estimate=cost(rows * width, 6 * rows * width),
        megabytes=16,
    )


def add_down_kernel(places, *refs):
    terms, (sent_ref, mine_ref) = refs[:-2], refs[-2:]
    total = sum(ref[...].reshape(sent_ref.shape).astype(F32) for ref in terms).astype(BF16)

    @pl.when(pl.program_id(0) == 0)
    def _():
        sent_ref[...] = total

    @pl.when(pl.program_id(0) == 1)
    def _():
        mine_ref[...] = total


def add_down(places, bit, terms, after, hold=()):
    rows, width = terms[-1].shape
    half = rows // 2

    def which(h, p):
        return jnp.where(h == 0, 1 - p[bit], p[bit])

    flat = pl.BlockSpec((half, width), lambda h, p: (which(h, p), 0))
    pair = pl.BlockSpec((1, half, width), lambda h, p: (p[1], which(h, p), 0))
    out = pl.BlockSpec((half, width), lambda h, p: (0, 0))
    return run(
        add_down_kernel, "add_down", terms, [jax.ShapeDtypeStruct((half, width), BF16)] * 2,
        [pair if item.ndim == 3 else flat for item in terms], [out, out],
        grid=(2,), places=places, after=after, hold=hold,
        estimate=cost(rows * width, 6 * rows * width), megabytes=16,
    )


def add_whole_kernel(a_ref, b_ref, out_ref):
    out_ref[...] = (a_ref[...].astype(F32) + b_ref[...].astype(F32)).astype(BF16)


def add_whole(a, b, after):
    return run(
        add_whole_kernel, "add_whole", (a, b), jax.ShapeDtypeStruct(a.shape, BF16),
        [whole(a.shape)] * 2, whole(a.shape), after=after, estimate=cost(a.size, 6 * a.size),
        megabytes=16,
    )


def join_kernel(bit, places, own_ref, other_ref, out_ref):
    rows = own_ref.shape[0]
    first = places[bit] == 0
    own, other = own_ref[...], other_ref[...]
    out_ref[:rows, :] = jnp.where(first, own, other)
    out_ref[rows:, :] = jnp.where(first, other, own)


def join(places, bit, own, other, after):
    rows, width = own.shape
    return run(
        functools.partial(join_kernel, bit), "join", (own, other),
        jax.ShapeDtypeStruct((2 * rows, width), BF16), [whole(own.shape)] * 2,
        whole((2 * rows, width)), places=places, after=after,
        estimate=cost(own.size, 8 * own.size), megabytes=16,
    )


def wide(full_ref, at, rows, cols, out_ref):
    width = full_ref.shape[1]
    for i in range(cols // width):
        out_ref[:, i * width : (i + 1) * width] = full_ref[at + i * rows : at + (i + 1) * rows, :]


def unfold_kernel(lay_out, ref, *refs):
    outs, full_ref = refs[:-1], refs[-1]
    full_ref[...] = ref[...].astype(F32)
    lay_out(full_ref, *outs)


def unfold(packed, lay_out, shapes):
    return run(
        functools.partial(unfold_kernel, lay_out), "unfold", (packed,),
        [jax.ShapeDtypeStruct(shape, F32) for shape in shapes], [whole(packed.shape)],
        [whole(shape) for shape in shapes], estimate=cost(packed.size, 10 * packed.size),
        megabytes=24, scratch=[pltpu.VMEM(packed.shape, F32)],
    )


def finish_kernel(bit, lay_out, places, own_ref, other_ref, *refs):
    outs, full_ref = refs[:-1], refs[-1]
    rows = own_ref.shape[0]
    first = places[bit] == 0
    own, other = own_ref[...].astype(F32), other_ref[...].astype(F32)
    full_ref[:rows, :] = jnp.where(first, own, other)
    full_ref[rows:, :] = jnp.where(first, other, own)
    lay_out(full_ref, *outs)


def finish(places, bit, own, other, lay_out, shapes, after):
    rows, width = own.shape
    return run(
        functools.partial(finish_kernel, bit, lay_out), "finish", (own, other),
        [jax.ShapeDtypeStruct(shape, F32) for shape in shapes], [whole(own.shape)] * 2,
        [whole(shape) for shape in shapes], places=places, after=after,
        estimate=cost(own.size, 16 * own.size), megabytes=16, scratch=[pltpu.VMEM((2 * rows, width), F32)],
    )


class Reduction:
    def __init__(self, order, places, pair, lay_out, shapes):
        send, self.keep = pair
        self.order, self.places = order, places
        self.lay_out, self.shapes = lay_out, shapes
        self.send = send
        bits = lax.axis_size("col").bit_length() - 1
        self.steps = ["across"] + [("down", i) for i in range(bits - 1)] + [("full", bits - 1)]
        self.steps += [("up", i) for i in reversed(range(bits - 1))] + ["end"]
        self.pending = None
        self.sent = self.result = None

    def after(self):
        return (self.order[-1].sent,) if self.order and self.order[-1] is not self else ()

    def advance(self, then=None):
        step = self.steps.pop(0)
        places, after = self.places, self.after()
        if step == "across":
            self.came = swap(self.send, "row", 1)
            self.sent = add_across(places, self.keep, self.came, after)
        else:
            if self.pending == "across":
                terms = (self.keep, self.came, swap(self.sent, "row", 2))
            else:
                terms = (self.mine, swap(self.sent, "col", 1 << self.pending[1]))
            if step == "end":
                bit = 2 + self.pending[1]
                result = finish(places, bit, *terms, self.lay_out, self.shapes, after)
                self.result = result if isinstance(result, (list, tuple)) else [result]
                self.sent = self.result[0]
            elif step[0] == "down":
                hold = () if then is None else (then.send,)
                self.sent, self.mine, *kept = add_down(places, 2 + step[1], terms, after, hold)
                if kept:
                    (then.send,) = kept
            elif self.pending[0] in ("down", "full"):
                self.sent = self.mine = add_whole(*terms, after)
            else:
                self.sent = self.mine = join(places, 2 + self.pending[1], *terms, after)
        self.pending = step
        self.order.append(self)


class Ready:
    def __init__(self, value):
        self.sent = value


def wave_numbers(width):
    def of(part):
        half = part // 2
        one = np.float32(1.0) / np.float32(10000.0) ** (
            np.arange(half, dtype=np.float32) / np.float32(half)
        )
        return [one, one]

    unit = width // 16
    return np.concatenate(of(4 * unit) + of(6 * unit) + of(6 * unit)).astype(np.float32)[None, :]


def per_device(
    pixels, timestamps, frame_count, visible, halo_reach, w_patch, b_patch, gain_one, shift_one,
    w_qkv, b_query, b_value, w_out, b_out, gain_two, shift_two, w_up, b_up, w_down, b_down,
    w_dec, b_dec, w_pix, b_pix, cotangent,
):
    tile_rows, tile_cols, frames, pix_width = pixels.shape
    model_width = w_patch.shape[1]
    tokens = tile_rows * tile_cols * frames
    ff = w_up.shape[1]
    grid_shape = (tile_rows, frames, tile_cols)
    side = tile_rows * 8 * HALO
    band = HALO * frames * tile_cols
    row_at, col_at = lax.axis_index("row"), lax.axis_index("col")
    col_bits = lax.axis_size("col").bit_length() - 1
    places = jnp.stack(
        [row_at % 2, row_at // 2] + [(col_at >> i) % 2 for i in range(col_bits)]
    ).astype(jnp.int32)

    flat_pixels = pixels.transpose(0, 2, 1, 3).reshape(tokens, pix_width)
    flat_cotangent = cotangent.transpose(0, 2, 1, 3).reshape(tokens, pix_width)
    stream_one, normed_one, high, low, tail, head, flags = embed(
        timestamps.reshape(-1), frame_count.reshape(-1), visible.transpose(2, 0, 1), flat_pixels,
        w_patch, b_patch, gain_one, shift_one, wave_numbers(model_width),
    )
    upper = rotate(high, "row", 1)
    lower = rotate(low, "row", -1)
    left = rotate(tail, "col", 1)
    right = rotate(head, "col", -1)
    query, key, value = own_qkv(normed_one, w_qkv, b_query, b_value)
    grad_dec, grad_stream, grad_mlp, sum_pix, sum_dec, sum_down = decode_back(
        flat_cotangent, w_pix, w_dec
    )
    strip_key, strip_value, strip_rows, bias = strip_kv(
        halo_reach.reshape(-1), upper, lower, left, right, flags, w_qkv, b_value
    )
    mixed, log_total = attend(query, key, value, strip_key, strip_value, bias)
    (
        pixel_out, normed_two, act, grad_pre, stream_low, decoded, attended,
        grad_two, grad_att, grad_attended, sum_up, sum_out, sum_gain_two, sum_shift_two,
    ) = mlp(
        stream_one, mixed, grad_stream, w_out, b_out, gain_two, shift_two,
        w_up, b_up, w_down, b_down, w_dec, b_dec, w_pix, b_pix,
    )
    fixed = (query, key, value, strip_key, strip_value)
    rest = (mixed, log_total, bias)
    pairs = model_width // LANES
    third = pairs // 3
    quarter = model_width // 4
    patch_rows, down_rows = pix_width // 4, ff // 4
    pix_rows, up_rows = w_dec.shape[1] // 4, quarter * (ff // model_width)
    dec_width = w_dec.shape[1]
    cut = quarter * 2 // 3
    order = []

    def lay_down(full, down_ref, pix_ref, dec_ref):
        down_ref[...] = full[:down_rows, :]
        wide(full, down_rows, pix_rows, pix_width, pix_ref)
        at, tall = down_rows + pix_rows * (pix_width // model_width), quarter - cut
        dec_ref[:cut, :] = full[at : at + cut, :dec_width]
        dec_ref[cut:, : model_width - dec_width] = full[at : at + tall, dec_width:]
        dec_ref[cut:, model_width - dec_width :] = full[at + tall : at + cut, dec_width:]

    def lay_up(full, up_ref, out_ref):
        wide(full, 0, quarter, ff, up_ref)
        out_ref[...] = full[up_rows : up_rows + quarter, :]

    def lay_middle(full, qkv_ref):
        wide(full, 0, quarter, 3 * model_width, qkv_ref)

    def lay_last(full, patch_ref, *refs):
        patch_ref[...] = full[:patch_rows, :]
        lines = -(-len(refs) // 16) * 16
        for i, ref in enumerate(refs):
            at = patch_rows + i
            size = ref.shape[1]
            ref[...] = full[at : at + 1, :size] + full[at + lines : at + lines + 1, :size]

    down = Reduction(
        order, places,
        grads_down(places, act, grad_mlp, decoded, flat_cotangent, stream_low, grad_dec), lay_down,
        [(down_rows, model_width), (pix_rows, pix_width), (quarter, dec_width)],
    )
    up = Reduction(
        order, places, grads_up(places, normed_two, grad_pre, attended, grad_att, (down.keep,)),
        lay_up, [(quarter, ff), (quarter, model_width)],
    )
    down.advance()
    back = attend_back(*fixed, grad_attended, *rest, 0, third, (), (down.sent, up.keep))
    back = attend_back(*fixed, grad_attended, *rest, third, third, back, ())
    order.append(Ready(back[0]))
    down.advance()
    up.advance()
    back = attend_back(
        *fixed, grad_attended, *rest, 2 * third, pairs - 2 * third, back, (up.sent, down.sent)
    )
    dq, dk, dv, dks, dvs, sum_query, sum_value = back
    order.append(Ready(dq))
    down.advance()
    upper_back, lower_back, left_back, right_back = strip_back(
        dks, dvs, w_qkv, band, side, (down.sent,)
    )
    from_right = rotate(left_back, "col", -1)
    from_left = rotate(right_back, "col", 1)
    from_below = rotate(upper_back, "row", -1)
    from_above = rotate(lower_back, "row", 1)
    middle = Reduction(
        order, places,
        grads_qkv(places, normed_one, strip_rows, dq, dk, dv, dks, dvs, (upper_back,)),
        lay_middle, [(quarter, 3 * model_width)],
    )
    grad_emb, sum_patch, sum_gain_one, sum_shift_one, down.sent = embed_back(
        stream_one, dq, dk, dv, w_qkv, grad_two, gain_one, from_above,
        from_below, from_left, from_right, tile_rows, frames, (down.sent,),
    )
    vectors = [
        sum_patch, sum_gain_one, sum_shift_one, sum_query, sum_value, sum_out, sum_gain_two,
        sum_shift_two, sum_up, sum_down, sum_dec, sum_pix,
    ]
    order.append(Ready(grad_emb))
    up.advance(middle)
    last = Reduction(
        order, places, grads_patch(places, flat_pixels, grad_emb, vectors, (up.sent,)),
        lay_last, [(patch_rows, model_width)] + [(1, item.shape[1] // 4) for item in vectors],
    )
    down.advance()
    middle.advance()
    last.advance()
    pixel_grad = pixel_back(grad_emb, w_patch, (last.sent,))
    order.append(Ready(pixel_grad))
    for each in (up, down, middle, last, up, down, middle, last, up, down, middle, last, up, down, middle, last, middle, last, last):
        if each.steps:
            each.advance()
    groups = (down, up, middle, last)
    while any(each.steps for each in groups):
        for each in groups:
            if each.steps:
                each.advance()
    share_down, share_pix, share_dec = down.result
    share_up, share_out = up.result
    (share_qkv,) = middle.result
    share_patch, *pieces = last.result
    pieces = [item.reshape(-1) for item in pieces]

    def to_scene(flat):
        return flat.reshape(grid_shape + (pix_width,)).transpose(0, 2, 1, 3)

    return (
        to_scene(pixel_out), to_scene(pixel_grad), share_patch, pieces[0], pieces[1], pieces[2],
        share_qkv, pieces[3], pieces[4], share_out, pieces[5], pieces[6], pieces[7], share_up,
        pieces[8], share_down, pieces[9], share_dec, pieces[10], share_pix, pieces[11],
    )


def solution(mesh):
    tiles = P("row", "col", None, None)
    return jax.shard_map(
        per_device,
        mesh=mesh,
        in_specs=(
            tiles,
            P("row", "col", None),
            P("row", "col"),
            P("row", "col", None),
            P("row", "col"),
        )
        + (P(),) * 19
        + (tiles,),
        out_specs=(
            tiles,
            tiles,
            P("row", None),
            P("row"),
            P("row"),
            P("row"),
            P("row", None),
            P("row"),
            P("row"),
            P("row", None),
            P("row"),
            P("row"),
            P("row"),
            P("row", None),
            P("row"),
            P("row", None),
            P("row"),
            P("row", None),
            P("row"),
            P("row", None),
            P("row"),
        ),
        check_vma=False,
    )
```

```python
import functools
import math

import jax
import jax.numpy as jnp
import numpy as np
from jax import lax
from jax.experimental import pallas as pl
from jax.experimental.pallas import tpu as pltpu
from jax.sharding import PartitionSpec as P

HEAD_WIDTH = 64
HALO = 2
EPS = 1e-06
NEG_FILL = -1e30
BLOCK = 256
LANES = 128
KEY_BLOCK = 512
FF_BLOCK = 1024
EVENTS = "mldudmpuldmulmlmdlmulml"
SCALE = HEAD_WIDTH**-0.5
LOG_SCALE = SCALE * math.log2(math.e)
F32 = jnp.float32
BF16 = jnp.bfloat16


def dot_last(a, b):
    return lax.dot_general(a, b, (((1,), (1,)), ((), ())), preferred_element_type=F32)


def dot_plain(a, b):
    return lax.dot_general(a, b, (((1,), (0,)), ((), ())), preferred_element_type=F32)


def one_head(pair, head):
    lane = lax.broadcasted_iota(jnp.int32, pair.shape, 1)
    keep = (lane < HEAD_WIDTH) if head == 0 else (lane >= HEAD_WIDTH)
    return jnp.where(keep, pair, jnp.zeros_like(pair))


def diagonal(size):
    rows = lax.broadcasted_iota(jnp.int32, (size, size), 0)
    return rows == lax.broadcasted_iota(jnp.int32, (size, size), 1)


def row_of(ref):
    return ref[...].astype(F32).reshape(1, -1)


def params(megabytes):
    return pltpu.CompilerParams(vmem_limit_bytes=megabytes << 20)


def cost(flops, moved):
    return pl.CostEstimate(flops=flops, bytes_accessed=moved, transcendentals=0)


def whole(shape):
    return pl.BlockSpec(shape, lambda *_: (0,) * len(shape))


def held(shape):
    return pl.BlockSpec(shape, lambda *_: (0,) * len(shape), pipeline_mode=pl.Buffered(1))


def embed_kernel(
    stamps_ref,
    count_ref,
    visible_ref,
    pixels_ref,
    w_ref,
    b_ref,
    gain_ref,
    shift_ref,
    wave_ref,
    stream_ref,
    normed_ref,
    high_ref,
    low_ref,
    tail_ref,
    head_ref,
    flags_ref,
    edge_ref,
    time_ref,
    col_ref,
    n_ref,
):
    at_row = pl.program_id(0)
    width = w_ref.shape[1]
    frames, tile_rows, tile_cols = visible_ref.shape
    line = frames * tile_cols
    band = HALO * line

    lane = lax.broadcasted_iota(jnp.int32, (1, width), 1)
    t_end, r_end = width // 4, width // 4 + width * 3 // 8
    t_mid, r_mid, c_mid = width // 8, t_end + width * 3 // 16, r_end + width * 3 // 16

    def waves(places):
        angles = places * wave_ref[...]
        is_sin = (lane < t_mid) | ((lane >= t_end) & (lane < r_mid)) | ((lane >= r_end) & (lane < c_mid))
        return jnp.where(is_sin, jnp.sin(angles), jnp.cos(angles))

    @pl.when(at_row == 0)
    def _():
        slot = lax.broadcasted_iota(jnp.int32, (8, 1), 0)
        stamps = jnp.zeros((8, 1), F32)
        for f in range(frames):
            stamps = jnp.where(slot == f, stamps_ref[f].astype(F32), stamps)
        time_ref[...] = jnp.where(lane < t_end, waves(stamps), 0.0)
        cols = lax.axis_index("col") * tile_cols + lax.broadcasted_iota(
            jnp.int32, (tile_cols, 1), 0
        )
        col_ref[...] = jnp.where(lane >= r_end, waves(cols.astype(F32)), 0.0)
        frame_at = lax.broadcasted_iota(jnp.int32, visible_ref.shape, 0)
        ok = ((frame_at < count_ref[0]) & (visible_ref[...] == 1)).astype(F32)
        pieces = [ok[f, r : r + 1, :] for r in range(tile_rows) for f in range(frames)]
        flat = jnp.concatenate(pieces, 1)
        flags_ref[...] = jnp.broadcast_to(flat, flags_ref.shape)
        edge_ref[...] = jnp.zeros_like(edge_ref)
        nothing = [jnp.zeros((8 - frames, tile_cols), F32)]
        stacked = jnp.concatenate(
            sum((pieces[r * frames : (r + 1) * frames] + nothing for r in range(tile_rows)), []), 0
        )
        slot = lax.broadcasted_iota(jnp.int32, (8, tile_cols), 0)
        col = lax.broadcasted_iota(jnp.int32, (8, tile_cols), 1)
        last = HALO * tile_rows
        chunk = 8 * tile_rows
        edge_ref[0, last, :, :chunk] = dot_last(
            (col == slot + tile_cols - HALO).astype(F32), stacked
        )
        edge_ref[1, last, :, :chunk] = dot_last((col == slot).astype(F32), stacked)

    places = (lax.axis_index("row") * tile_rows + at_row).astype(F32)
    row_part = jnp.where((lane >= t_end) & (lane < r_end), waves(jnp.full((1, 1), places)), 0.0)
    base = row_of(b_ref) + row_part
    stream = dot_plain(pixels_ref[...], w_ref[...])
    position = jnp.concatenate(
        [col_ref[...] + (time_ref[f : f + 1, :] + base) for f in range(frames)], 0
    )
    stream = stream + position
    stream_ref[...] = stream
    centre = stream - jnp.mean(stream, -1, keepdims=True)
    spread = jnp.mean(centre * centre, -1, keepdims=True)
    normed = centre * lax.rsqrt(spread + EPS) * row_of(gain_ref) + row_of(shift_ref)
    low = normed.astype(BF16)
    normed_ref[...] = low
    n_ref[...] = low.astype(F32)
    for j in range(HALO):
        target = j * tile_rows + at_row
        for f in range(frames):
            near = f * tile_cols + j
            far = near + tile_cols - HALO
            edge_ref[0, target, f : f + 1, :] = n_ref[far : far + 1, :]
            edge_ref[1, target, f : f + 1, :] = n_ref[near : near + 1, :]

    @pl.when(at_row < HALO)
    def _():
        low_ref[pl.ds(pl.multiple_of(at_row * line, line), line), :] = low

    @pl.when(at_row >= tile_rows - HALO)
    def _():
        start = (at_row - (tile_rows - HALO)) * line
        high_ref[pl.ds(pl.multiple_of(start, line), line), :] = low

    @pl.when(at_row == tile_rows - 1)
    def _():
        tail_ref[...] = edge_ref[0].reshape(tail_ref.shape).astype(BF16)
        head_ref[...] = edge_ref[1].reshape(head_ref.shape).astype(BF16)
        zeros = jnp.zeros((8, width - band), BF16)
        total = flags_ref.shape[1]
        low_ref[band : band + 8, :band] = flags_ref[:, :band].astype(BF16)
        low_ref[band : band + 8, band:] = zeros
        high_ref[band : band + 8, :band] = flags_ref[:, total - band :].astype(BF16)
        high_ref[band : band + 8, band:] = zeros


def embed(stamps, count, visible, pixels, w, b, gain, shift, wave):
    tokens, depth = pixels.shape
    width = w.shape[1]
    frames, tile_rows, tile_cols = visible.shape
    line = frames * tile_cols
    band = HALO * line
    side = HALO * tile_rows * 8
    smem = pl.BlockSpec(memory_space=pltpu.SMEM)
    block = pl.BlockSpec((line, width), lambda r: (r, 0))
    return pl.pallas_call(
        embed_kernel,
        grid=(tile_rows,),
        in_specs=[
            smem,
            smem,
            whole(visible.shape),
            pl.BlockSpec((line, depth), lambda r: (r, 0)),
            held(w.shape),
            whole((width,)),
            whole((width,)),
            whole((width,)),
            whole((1, width)),
        ],
        out_specs=[
            block,
            block,
            whole((band + 8, width)),
            whole((band + 8, width)),
            whole((side + 8, width)),
            whole((side + 8, width)),
            whole((8, tokens)),
        ],
        out_shape=[
            jax.ShapeDtypeStruct((tokens, width), F32),
            jax.ShapeDtypeStruct((tokens, width), BF16),
            jax.ShapeDtypeStruct((band + 8, width), BF16),
            jax.ShapeDtypeStruct((band + 8, width), BF16),
            jax.ShapeDtypeStruct((side + 8, width), BF16),
            jax.ShapeDtypeStruct((side + 8, width), BF16),
            jax.ShapeDtypeStruct((8, tokens), F32),
        ],
        scratch_shapes=[
            pltpu.VMEM((2, side // 8 + 1, 8, width), F32),
            pltpu.VMEM((8, width), F32),
            pltpu.VMEM((tile_cols, width), F32),
            pltpu.VMEM((line, width), F32),
        ],
        compiler_params=params(60),
        cost_estimate=cost(2 * tokens * depth * width, 10 << 20),
        name="embed",
    )(stamps, count, visible, pixels, w, b, gain, shift, wave)


def decode_back_kernel(
    cot_ref, w_pix_ref, w_dec_ref, dec_ref, out_ref, mlp_ref, sum_pix, sum_dec, sum_down
):
    @pl.when(pl.program_id(0) == 0)
    def _():
        sum_pix[...] = jnp.zeros_like(sum_pix)
        sum_dec[...] = jnp.zeros_like(sum_dec)
        sum_down[...] = jnp.zeros_like(sum_down)

    grad_dec = dot_last(cot_ref[...], w_pix_ref[...]).astype(BF16)
    dec_ref[...] = grad_dec
    grad_out = dot_last(grad_dec, w_dec_ref[...])
    out_ref[...] = grad_out
    low = grad_out.astype(BF16)
    mlp_ref[...] = low
    sum_pix[...] += jnp.sum(cot_ref[...].astype(F32), 0, keepdims=True)
    sum_dec[...] += jnp.sum(grad_dec.astype(F32), 0, keepdims=True)
    sum_down[...] += jnp.sum(low.astype(F32), 0, keepdims=True)


def decode_back(cot, w_pix, w_dec):
    tokens, pix = cot.shape
    width, dec = w_dec.shape

    def block(size):
        return pl.BlockSpec((BLOCK, size), lambda i: (i, 0))

    return pl.pallas_call(
        decode_back_kernel,
        grid=(tokens // BLOCK,),
        in_specs=[block(pix), held(w_pix.shape), held(w_dec.shape)],
        out_specs=[
            block(dec),
            block(width),
            block(width),
            whole((1, pix)),
            whole((1, dec)),
            whole((1, width)),
        ],
        out_shape=[
            jax.ShapeDtypeStruct((tokens, dec), BF16),
            jax.ShapeDtypeStruct((tokens, width), F32),
            jax.ShapeDtypeStruct((tokens, width), BF16),
            jax.ShapeDtypeStruct((1, pix), F32),
            jax.ShapeDtypeStruct((1, dec), F32),
            jax.ShapeDtypeStruct((1, width), F32),
        ],
        compiler_params=params(16),
        cost_estimate=cost(2 * tokens * dec * (pix + width), 10 << 20),
        name="decode_back",
    )(cot, w_pix, w_dec)


def own_qkv_kernel(x_ref, w_ref, bq_ref, bv_ref, q_ref, k_ref, v_ref):
    width = x_ref.shape[1]
    x = x_ref[...]
    q_ref[...] = (dot_plain(x, w_ref[:, :width]) + row_of(bq_ref)).astype(BF16)
    k_ref[...] = dot_plain(x, w_ref[:, width : 2 * width]).astype(BF16)
    v_ref[...] = (dot_plain(x, w_ref[:, 2 * width :]) + row_of(bv_ref)).astype(BF16)


def own_qkv(x, w, bq, bv):
    tokens, width = x.shape
    block = pl.BlockSpec((BLOCK, width), lambda i: (i, 0))
    return pl.pallas_call(
        own_qkv_kernel,
        grid=(tokens // BLOCK,),
        in_specs=[block, held(w.shape), whole((width,)), whole((width,))],
        out_specs=[block] * 3,
        out_shape=[jax.ShapeDtypeStruct((tokens, width), BF16)] * 3,
        compiler_params=params(16),
        cost_estimate=cost(6 * tokens * width * width, 8 << 20),
        name="own_qkv",
    )(x, w, bq, bv)


def strip_kv_kernel(
    reach_ref, upper_ref, lower_ref, left_ref, right_ref, flags_ref, w_ref, bv_ref,
    k_ref, v_ref, rows_ref, bias_ref,
):
    band = upper_ref.shape[0] - 8
    side = left_ref.shape[0] - 8
    tokens = flags_ref.shape[1]
    total = rows_ref.shape[0]
    at = pl.program_id(0)

    @pl.when(at == 0)
    def _():
        rows_ref[:band, :] = upper_ref[:band, :]
        rows_ref[band : 2 * band, :] = lower_ref[:band, :]
        rows_ref[2 * band : 2 * band + side, :] = left_ref[:side, :]
        rows_ref[2 * band + side : 2 * (band + side), :] = right_ref[:side, :]
        if total > 2 * (band + side):
            rows_ref[2 * (band + side) :, :] = jnp.zeros(
                (total - 2 * (band + side), rows_ref.shape[1]), BF16
            )
        reach = reach_ref[0]
        line = band // HALO
        where = lax.broadcasted_iota(jnp.int32, (1, band), 1) // line
        near = (reach >= where + 1).astype(F32)
        far = (reach >= HALO - where).astype(F32)
        upper_ok = upper_ref[band : band + 1, :band].astype(F32) * far
        lower_ok = lower_ref[band : band + 1, :band].astype(F32) * near
        chunk = side // HALO
        spare = total - 2 * band
        source = lax.broadcasted_iota(jnp.int32, (LANES, spare), 0)
        target = lax.broadcasted_iota(jnp.int32, (LANES, spare), 1)
        sides = jnp.zeros((8, spare), F32)
        for j in range(HALO):
            for part, ref, need in ((0, left_ref, HALO - j), (1, right_ref, j + 1)):
                place = (target == source + part * side + j * chunk) & (source < chunk)
                line_ok = jnp.broadcast_to(
                    ref[side : side + 8, :LANES].astype(F32)[j : j + 1], (8, LANES)
                )
                moved = dot_plain(line_ok.astype(BF16), place.astype(BF16))
                sides = sides + jnp.where(reach >= need, moved, 0.0)
        bias_ref[:, :tokens] = jnp.where(flags_ref[...] > 0.5, 0.0, NEG_FILL)
        bias_ref[:, tokens : tokens + band] = jnp.broadcast_to(
            jnp.where(upper_ok > 0.5, 0.0, NEG_FILL), (8, band)
        )
        bias_ref[:, tokens + band : tokens + 2 * band] = jnp.broadcast_to(
            jnp.where(lower_ok > 0.5, 0.0, NEG_FILL), (8, band)
        )
        bias_ref[:, tokens + 2 * band :] = jnp.where(sides > 0.5, 0.0, NEG_FILL)
        k_ref[...] = dot_plain(rows_ref[...], w_ref[...]).astype(BF16)

    @pl.when(at == 1)
    def _():
        v_ref[...] = (dot_plain(rows_ref[...], w_ref[...]) + row_of(bv_ref)).astype(BF16)


def strip_kv(reach, upper, lower, left, right, flags, w, bv):
    width = w.shape[0]
    tokens = flags.shape[1]
    keys = 2 * (upper.shape[0] - 8) + 2 * (left.shape[0] - 8)
    total = -(-(tokens + keys) // LANES) * LANES - tokens
    strip = jax.ShapeDtypeStruct((total, width), BF16)
    return pl.pallas_call(
        strip_kv_kernel,
        grid=(2,),
        in_specs=[
            pl.BlockSpec(memory_space=pltpu.SMEM),
            whole(upper.shape),
            whole(lower.shape),
            whole(left.shape),
            whole(right.shape),
            whole(flags.shape),
            pl.BlockSpec((width, width), lambda i: (0, i + 1)),
            whole((width,)),
        ],
        out_specs=[whole((total, width))] * 3 + [whole((8, tokens + total))],
        out_shape=[strip] * 3 + [jax.ShapeDtypeStruct((8, tokens + total), F32)],
        compiler_params=params(16),
        cost_estimate=cost(4 * total * width * width, 8 << 20),
        name="strip_kv",
    )(reach, upper, lower, left, right, flags, w, bv)


def attend_kernel(
    q_ref, k_ref, v_ref, ks_ref, vs_ref, bias_ref, out_ref, log_ref, s_ref, keys_ref, values_ref, own_ref
):
    tokens = q_ref.shape[0]
    keys = keys_ref.shape[0]
    keys_ref[:tokens, :] = k_ref[...]
    keys_ref[tokens:, :] = ks_ref[...]
    for ref, rows in ((v_ref, slice(0, tokens)), (vs_ref, slice(tokens, keys))):
        values = ref[...]
        lane = lax.broadcasted_iota(jnp.int32, values.shape, 1)
        values_ref[0, rows, :] = jnp.where(lane < HEAD_WIDTH, values, jnp.ones_like(values))
        values_ref[1, rows, :] = jnp.where(lane >= HEAD_WIDTH, values, jnp.ones_like(values))

    @pl.when(pl.program_id(0) == 0)
    def _():
        own_ref[...] = bias_ref[:, :tokens].T[:, 0:1]

    block = tokens // 2
    lane = lax.broadcasted_iota(jnp.int32, (block, LANES), 1)
    spans = [(at, min(KEY_BLOCK, keys - at)) for at in range(0, keys, KEY_BLOCK)]
    units = [(at, head) for at in range(0, tokens, block) for head in range(2)]

    def query(unit):
        at, head = unit
        return one_head(q_ref[at : at + block, :], head)

    def score(q_head, span, slot, top):
        at, size = span
        scores = dot_last(q_head, keys_ref[at : at + size, :]) + bias_ref[0:1, at : at + size]
        s_ref[slot, :, at : at + size] = scores
        for part in range(0, size, LANES):
            piece = scores[:, part : part + LANES]
            top = piece if top is None else jnp.maximum(top, piece)
        return top

    def own_term(unit, q_head, top):
        at = unit[0]
        own_keys = keys_ref[at : at + block, :].astype(F32)
        score_own = jnp.sum(q_head.astype(F32) * own_keys, 1, keepdims=True)
        score_own = jnp.where(own_ref[at : at + block, :] < 0, score_own, NEG_FILL)
        top = jnp.maximum(jnp.max(top, 1, keepdims=True), score_own) * LOG_SCALE
        return top, jnp.exp2(score_own * LOG_SCALE - top).astype(BF16).astype(F32)

    def weigh(unit, span, slot, top, mixed):
        at, size = span
        weights = jnp.exp2(s_ref[slot, :, at : at + size] * LOG_SCALE - top).astype(BF16)
        part = dot_plain(weights, values_ref[unit[1], at : at + size, :])
        return part if mixed is None else mixed + part

    q_head, best = query(units[0]), None
    for span in spans:
        best = score(q_head, span, 0, best)
    top, own = own_term(units[0], q_head, best)
    first = None
    for number, unit in enumerate(units):
        at, head = unit
        follows = units[number + 1] if number + 1 < len(units) else None
        q_head = query(follows) if follows else None
        best = mixed = None
        for span in spans:
            if follows:
                best = score(q_head, span, (number + 1) % 2, best)
            mixed = weigh(unit, span, number % 2, top, mixed)
        mixed = mixed + own * values_ref[head, at : at + block, :].astype(F32)
        total = mixed[:, HEAD_WIDTH : HEAD_WIDTH + 1] if head == 0 else mixed[:, 0:1]
        log_ref[0, head, at : at + block] = (top + jnp.log2(total))[:, 0]
        if head == 0:
            first = mixed / total
        else:
            out_ref[at : at + block, :] = jnp.where(lane < HEAD_WIDTH, first, mixed / total)
        if follows:
            top, own = own_term(follows, q_head, best)


def attend(q, k, v, ks, vs, bias):
    tokens, width = q.shape
    keys = tokens + ks.shape[0]
    pairs = width // LANES
    own = pl.BlockSpec((tokens, LANES), lambda p: (0, p))
    strip = pl.BlockSpec((keys - tokens, LANES), lambda p: (0, p))
    return pl.pallas_call(
        attend_kernel,
        grid=(pairs,),
        in_specs=[own, own, own, strip, strip, whole((8, keys))],
        out_specs=[own, pl.BlockSpec((1, 2, tokens), lambda p: (p, 0, 0))],
        out_shape=[
            jax.ShapeDtypeStruct((tokens, width), F32),
            jax.ShapeDtypeStruct((pairs, 2, tokens), F32),
        ],
        scratch_shapes=[
            pltpu.VMEM((2, tokens // 2, keys), F32),
            pltpu.VMEM((keys, LANES), BF16),
            pltpu.VMEM((2, keys, LANES), BF16),
            pltpu.VMEM((tokens, 1), F32),
        ],
        compiler_params=params(24),
        cost_estimate=cost(16 * tokens * keys * width, 8 << 20),
        name="attend",
    )(q, k, v, ks, vs, bias)


def attend_back_kernel(
    q_ref, k_ref, v_ref, ks_ref, vs_ref, do_ref, o_ref, log_ref, bias_ref,
    dq_ref, dk_ref, dv_ref, dks_ref, dvs_ref, sum_q, sum_v,
    keys_ref, values_ref, kt_ref, mask_ref,
):
    tokens = q_ref.shape[0]
    keys_ref[:tokens, :] = k_ref[...]
    keys_ref[tokens:, :] = ks_ref[...]
    values_ref[:tokens, :] = v_ref[...]
    values_ref[tokens:, :] = vs_ref[...]
    kt_ref[...] = keys_ref[...].T

    @pl.when(pl.program_id(0) == 0)
    def _():
        mask_ref[...] = bias_ref[...].T[:, 0:1]

    q, do = q_ref[...], do_ref[...]
    wide_q, wide_do, wide_k = q.astype(F32), do.astype(F32), k_ref[...].astype(F32)
    with_out = (wide_do * o_ref[...]).T
    with_key = (wide_q * wide_k).T
    with_value = (wide_do * v_ref[...].astype(F32)).T
    hidden = bias_ref[0:1, :tokens] < 0
    dk = dv = None
    dq, own_weights, own_grads = [], [], []
    for head in range(2):
        part = slice(head * HEAD_WIDTH, (head + 1) * HEAD_WIDTH)
        delta = jnp.sum(with_out[part], axis=0, keepdims=True)
        log_total = log_ref[0, head : head + 1, :]
        own = jnp.sum(with_key[part], axis=0, keepdims=True) * LOG_SCALE - log_total
        own = jnp.where(hidden, jnp.exp2(jnp.where(hidden, own, 0.0)), 0.0)
        own_grad = own * (jnp.sum(with_value[part], axis=0, keepdims=True) - delta)
        own_weights.append(own.astype(BF16).astype(F32))
        own_grads.append(own_grad.astype(BF16).astype(F32))
        q_head = one_head(q, head)
        do_head = one_head(do, head)
        scores = dot_last(keys_ref[...], q_head) + mask_ref[...]
        weights = jnp.exp2(scores * LOG_SCALE - log_total)
        back = dot_last(values_ref[...], do_head)
        grad = (weights * (back - delta)).astype(BF16)
        dv_part = dot_plain(weights.astype(BF16), do_head)
        dk_part = dot_plain(grad, q_head)
        dv = dv_part if dv is None else dv + dv_part
        dk = dk_part if dk is None else dk + dk_part
        dq.append(dot_plain(kt_ref[...], grad))

    def per_lane(rows):
        return jnp.concatenate([jnp.broadcast_to(row, (HEAD_WIDTH, tokens)) for row in rows], 0).T

    own, own_grad = per_lane(own_weights), per_lane(own_grads)
    dv_own = (dv[:tokens] + own * wide_do).astype(BF16)
    dv_strip = dv[tokens:].astype(BF16)
    dv_ref[...] = dv_own
    dvs_ref[...] = dv_strip
    dk_ref[...] = ((dk[:tokens] + own_grad * wide_q) * SCALE).astype(BF16)
    dks_ref[...] = (dk[tokens:] * SCALE).astype(BF16)
    joined = jnp.concatenate([dq[0][:HEAD_WIDTH], dq[1][HEAD_WIDTH:]], axis=0).T
    low = ((joined + own_grad * wide_k) * SCALE).astype(BF16)
    dq_ref[...] = low
    sum_q[...] = jnp.sum(low.astype(F32), 0, keepdims=True)
    sum_v[...] = jnp.sum(dv_own.astype(F32), 0, keepdims=True) + jnp.sum(
        dv_strip.astype(F32), 0, keepdims=True
    )


def attend_back(q, k, v, ks, vs, do, o, log_total, bias, first, count, before, after):
    tokens, width = q.shape
    keys = tokens + ks.shape[0]
    own = pl.BlockSpec((tokens, LANES), lambda p: (0, p + first))
    strip = pl.BlockSpec((keys - tokens, LANES), lambda p: (0, p + first))
    line = pl.BlockSpec((1, LANES), lambda p: (0, p + first))
    return run(
        attend_back_kernel, "attend_back", (q, k, v, ks, vs, do, o, log_total, bias),
        [jax.ShapeDtypeStruct((tokens, width), BF16)] * 3
        + [jax.ShapeDtypeStruct((keys - tokens, width), BF16)] * 2
        + [jax.ShapeDtypeStruct((1, width), F32)] * 2,
        [
            own, own, own, strip, strip, own, own,
            pl.BlockSpec((1, 2, tokens), lambda p: (p + first, 0, 0)),
            whole((8, keys)),
        ],
        [own, own, own, strip, strip, line, line], grid=(count,), after=tuple(before) + tuple(after),
        aliases={9 + i: i for i in range(len(before))},
        estimate=cost(24 * tokens * keys * LANES * count, 3 * count << 20), megabytes=40,
        scratch=[
            pltpu.VMEM((keys, LANES), BF16),
            pltpu.VMEM((keys, LANES), BF16),
            pltpu.VMEM((LANES, keys), BF16),
            pltpu.VMEM((keys, 1), F32),
        ],
    )


def dot_first(a, b):
    return lax.dot_general(a, b, (((0,), (0,)), ((), ())), preferred_element_type=F32)


def mlp_kernel(
    one_ref, att_ref, gout_ref, w_out_ref, b_out_ref, gain_ref, shift_ref, w_up_ref, b_up_ref,
    w_down_ref, b_down_ref, w_dec_ref, b_dec_ref, w_pix_ref, b_pix_ref,
    pix_ref, normed_ref, act_ref, gup_ref, low_ref, decoded_ref, attended_ref,
    gtwo_ref, gatt_ref, gattended_ref, sum_up, sum_out, sum_gain, sum_shift,
    bias_ref, out_ref, gnormed_ref,
):
    @pl.when(pl.program_id(0) == 0)
    def _():
        bias_ref[...] = row_of(b_up_ref)
        for ref in (sum_up, sum_out, sum_gain, sum_shift):
            ref[...] = jnp.zeros_like(ref)

    ff = w_up_ref.shape[1]
    attended = att_ref[...].astype(BF16)
    attended_ref[...] = attended
    two = one_ref[...] + dot_plain(attended, w_out_ref[...]) + row_of(b_out_ref)
    centre = two - jnp.mean(two, -1, keepdims=True)
    inverse = lax.rsqrt(jnp.mean(centre * centre, -1, keepdims=True) + EPS)
    gain = row_of(gain_ref)
    normed = (centre * inverse * gain + row_of(shift_ref)).astype(BF16)
    normed_ref[...] = normed
    gout = gout_ref[...]
    gmlp = gout.astype(BF16)
    out_ref[...] = two + row_of(b_down_ref)
    gnormed_ref[...] = jnp.zeros_like(two)

    def step(i, carry):
        cols = pl.ds(pl.multiple_of(i * FF_BLOCK, FF_BLOCK), FF_BLOCK)
        up = dot_plain(normed, w_up_ref[:, cols]) + bias_ref[:, cols]
        bell = 0.5 * (1.0 + lax.erf(up * math.sqrt(0.5)))
        act = (up * bell).astype(BF16)
        slope = bell + up * (jnp.exp2(up * up * (-0.5 * math.log2(math.e))) * (2 * math.pi) ** -0.5)
        act_ref[:, cols] = act
        out_ref[...] += dot_plain(act, w_down_ref[cols, :])
        gup = (dot_last(gmlp, w_down_ref[cols, :]) * slope).astype(BF16)
        gup_ref[:, cols] = gup
        sum_up[:, cols] += jnp.sum(gup.astype(F32), 0, keepdims=True)
        gnormed_ref[...] += dot_last(gup, w_up_ref[:, cols])
        return carry

    lax.fori_loop(0, ff // FF_BLOCK, step, 0)
    out = out_ref[...]
    gnormed = gnormed_ref[...]
    low = out.astype(BF16)
    low_ref[...] = low
    decoded = (dot_plain(low, w_dec_ref[...]) + row_of(b_dec_ref)).astype(BF16)
    decoded_ref[...] = decoded
    pix_ref[...] = (dot_plain(decoded, w_pix_ref[...]) + row_of(b_pix_ref)).astype(BF16)
    hat = centre * inverse
    sum_gain[...] += jnp.sum(gnormed * hat, 0, keepdims=True)
    sum_shift[...] += jnp.sum(gnormed, 0, keepdims=True)
    scaled = gnormed * gain
    back = inverse * (
        scaled
        - jnp.mean(scaled, -1, keepdims=True)
        - hat * jnp.mean(scaled * hat, -1, keepdims=True)
    )
    gtwo = gout + back
    gtwo_ref[...] = gtwo
    gatt = gtwo.astype(BF16)
    gatt_ref[...] = gatt
    sum_out[...] += jnp.sum(gatt.astype(F32), 0, keepdims=True)
    gattended_ref[...] = dot_last(gatt, w_out_ref[...]).astype(BF16)


def mlp(one, att, gout, w_out, b_out, gain, shift, w_up, b_up, w_down, b_down, w_dec, b_dec, w_pix, b_pix):
    tokens, width = one.shape
    ff, dec, pix = w_up.shape[1], w_dec.shape[1], w_pix.shape[1]

    def block(size):
        return pl.BlockSpec((BLOCK, size), lambda i: (i, 0))

    def out(size, kind=BF16):
        return jax.ShapeDtypeStruct((tokens, size), kind)

    def vector(size):
        return jax.ShapeDtypeStruct((1, size), F32)

    weights = [w_out, b_out, gain, shift, w_up, b_up, w_down, b_down, w_dec, b_dec, w_pix, b_pix]
    return pl.pallas_call(
        mlp_kernel,
        grid=(tokens // BLOCK,),
        in_specs=[block(width)] * 3 + [held(item.shape) for item in weights],
        out_specs=[
            block(pix), block(width), block(ff), block(ff), block(width), block(dec), block(width),
            block(width), block(width), block(width),
            whole((1, ff)), whole((1, width)), whole((1, width)), whole((1, width)),
        ],
        out_shape=[
            out(pix), out(width), out(ff), out(ff), out(width), out(dec), out(width),
            out(width, F32), out(width), out(width),
            vector(ff), vector(width), vector(width), vector(width),
        ],
        scratch_shapes=[
            pltpu.VMEM((1, ff), F32),
            pltpu.VMEM((BLOCK, width), F32),
            pltpu.VMEM((BLOCK, width), F32),
        ],
        compiler_params=params(48),
        cost_estimate=cost(2 * tokens * width * (2 * width + 4 * ff + dec) + 2 * tokens * dec * pix, 40 << 20),
        name="mlp",
    )(one, att, gout, *weights)


def quarter_at(step, core):
    return 2 * (step % 2) + jnp.where(step < 2, 1 - core, core)


def lay_columns(ref, at, values, width):
    rows, cols = values.shape
    for i in range(cols // width):
        ref[0, at + i * rows : at + (i + 1) * rows, :] = values[:, i * width : (i + 1) * width]


def padded(rows):
    granule = 8 * lax.axis_size("col")
    return -(-rows // granule) * granule


def blank(ref, at):
    if at < ref.shape[1]:
        ref[0, at:, :] = jnp.zeros((ref.shape[1] - at, ref.shape[2]), BF16)


def pair_specs(rows, width):
    return [
        pl.BlockSpec((1, rows, width), lambda s, c: (jnp.minimum(s, 1), 0, 0)),
        pl.BlockSpec((1, rows, width), lambda s, c: (jnp.maximum(s - 2, 0), 0, 0)),
    ]


def grads_down_kernel(
    places, act_ref, gmlp_ref, decoded_ref, cot_ref, low_ref, gdec_ref, send_ref, keep_ref, lt_ref
):
    step = pl.program_id(0)

    @pl.when(step == 0)
    def _():
        lt_ref[...] = low_ref[...].T

    width = gmlp_ref.shape[1]
    part = width // 4
    rows = pl.ds(pl.multiple_of(quarter_at(step, places[0]) * part, part), part)
    down = dot_first(act_ref[...], gmlp_ref[...]).astype(BF16)
    pix = dot_first(decoded_ref[...], cot_ref[...]).astype(BF16)
    dec = dot_plain(lt_ref[rows, :], gdec_ref[...]).astype(BF16)
    at = down.shape[0] + pix.size // width
    cut, side = part * 2 // 3, dec.shape[1]
    rest = width - side
    for is_sent, ref in ((True, send_ref), (False, keep_ref)):

        @pl.when((step < 2) == is_sent)
        def _():
            ref[0, : down.shape[0], :] = down
            lay_columns(ref, down.shape[0], pix, width)
            ref[0, at : at + cut, :side] = dec[:cut]
            ref[0, at : at + part - cut, side:] = dec[cut:, :rest]
            ref[0, at + part - cut : at + cut, side:] = dec[cut:, rest:]
            blank(ref, at + cut)


def grads_down(places, act, gmlp, decoded, cot, low, gdec):
    tokens, ff = act.shape
    width, dec, pix = gmlp.shape[1], decoded.shape[1], cot.shape[1]
    rows = padded(ff // 4 + (dec // 4) * (pix // width) + dec // 4)
    return run(
        grads_down_kernel, "grads_down", (act, gmlp, decoded, cot, low, gdec),
        [jax.ShapeDtypeStruct((2, rows, width), BF16)] * 2,
        [
            pl.BlockSpec((tokens, ff // 4), lambda s, c: (0, quarter_at(s, c[0]))),
            held(gmlp.shape),
            pl.BlockSpec((tokens, dec // 4), lambda s, c: (0, quarter_at(s, c[0]))),
            held(cot.shape),
            held(low.shape),
            held(gdec.shape),
        ],
        pair_specs(rows, width), grid=(4,), places=places,
        estimate=cost(2 * tokens * (ff * width + dec * (pix + width)), 20 << 20),
        megabytes=32, scratch=[pltpu.VMEM((width, tokens), BF16)],
    )


def grads_up_kernel(
    places, normed_ref, gup_ref, att_ref, gatt_ref, send_ref, keep_ref, nt_ref, at_ref
):
    step = pl.program_id(0)

    @pl.when(step == 0)
    def _():
        nt_ref[...] = normed_ref[...].T
        at_ref[...] = att_ref[...].T

    width = normed_ref.shape[1]
    part = width // 4
    rows = pl.ds(pl.multiple_of(quarter_at(step, places[0]) * part, part), part)
    up = dot_plain(nt_ref[rows, :], gup_ref[...]).astype(BF16)
    out = dot_plain(at_ref[rows, :], gatt_ref[...]).astype(BF16)
    at = up.size // width
    for is_sent, ref in ((True, send_ref), (False, keep_ref)):

        @pl.when((step < 2) == is_sent)
        def _():
            lay_columns(ref, 0, up, width)
            ref[0, at : at + part, :] = out
            blank(ref, at + part)


def grads_up(places, normed, gup, attended, gatt, after):
    tokens, width = normed.shape
    ff = gup.shape[1]
    rows = padded(ff // 4 + width // 4)
    operands = (normed, gup, attended, gatt)
    return run(
        grads_up_kernel, "grads_up", operands, [jax.ShapeDtypeStruct((2, rows, width), BF16)] * 2,
        [held(item.shape) for item in operands], pair_specs(rows, width), grid=(4,), places=places,
        after=after, estimate=cost(2 * tokens * width * (ff + width), 16 << 20),
        scratch=[pltpu.VMEM((width, tokens), BF16)] * 2,
    )


def strip_back_kernel(dk_ref, dv_ref, w_ref, upper_ref, lower_ref, left_ref, right_ref):
    width = w_ref.shape[0]
    band, side = upper_ref.shape[0], left_ref.shape[0]
    back = (
        dot_last(dk_ref[...], w_ref[:, width : 2 * width]) + dot_last(dv_ref[...], w_ref[:, 2 * width :])
    ).astype(BF16)
    upper_ref[...] = back[:band]
    lower_ref[...] = back[band : 2 * band]
    left_ref[...] = back[2 * band : 2 * band + side]
    right_ref[...] = back[2 * band + side : 2 * (band + side)]


def strip_back(dk, dv, w, band, side, after):
    total, width = dk.shape
    sizes = (band, band, side, side)
    return run(
        strip_back_kernel, "strip_back", (dk, dv, w),
        [jax.ShapeDtypeStruct((rows, width), BF16) for rows in sizes],
        [whole(item.shape) for item in (dk, dv, w)], [whole((rows, width)) for rows in sizes],
        after=after, estimate=cost(4 * total * width * width, 8 << 20), megabytes=24,
    )


def grads_qkv_kernel(
    core_ref, normed_ref, rows_ref, dq_ref, dk_ref, dv_ref, dks_ref, dvs_ref,
    send_ref, keep_ref, nt_ref, st_ref,
):
    step = pl.program_id(0)

    @pl.when(step == 0)
    def _():
        nt_ref[...] = normed_ref[...].T
        st_ref[...] = rows_ref[...].T

    width = normed_ref.shape[1]
    part = width // 4
    rows = pl.ds(pl.multiple_of(quarter_at(step, core_ref[0]) * part, part), part)
    own, strip = nt_ref[rows, :], st_ref[rows, :]
    parts = (
        dot_plain(own, dq_ref[...]),
        dot_plain(own, dk_ref[...]) + dot_plain(strip, dks_ref[...]),
        dot_plain(own, dv_ref[...]) + dot_plain(strip, dvs_ref[...]),
    )
    for is_sent, ref in ((True, send_ref), (False, keep_ref)):

        @pl.when((step < 2) == is_sent)
        def _():
            for i, values in enumerate(parts):
                ref[0, i * part : (i + 1) * part, :] = values.astype(BF16)
            blank(ref, len(parts) * part)


def grads_qkv(places, normed, rows, dq, dk, dv, dks, dvs, after):
    tokens, width = normed.shape
    total = rows.shape[0]
    operands = (normed, rows, dq, dk, dv, dks, dvs)
    size = padded(3 * width // 4)
    return run(
        grads_qkv_kernel, "grads_qkv", operands, [jax.ShapeDtypeStruct((2, size, width), BF16)] * 2,
        [held(item.shape) for item in operands], pair_specs(size, width), grid=(4,), places=places,
        after=after, estimate=cost(2 * width * width * (3 * tokens + 2 * total), 20 << 20),
        scratch=[
            pltpu.VMEM((width, tokens), BF16),
            pltpu.VMEM((width, total), BF16),
        ],
    )


def embed_back_kernel(
    frames, stream_ref, dq_ref, dk_ref, dv_ref, w_ref, gtwo_ref, gain_ref, above_ref, below_ref, left_ref,
    right_ref, emb_ref, sum_patch, sum_gain, sum_shift, g_ref, side_ref,
):
    at_row = pl.program_id(0)
    width = stream_ref.shape[1]
    line = stream_ref.shape[0]
    tile_rows = left_ref.shape[0] // (8 * HALO)
    tile_cols = line // frames

    @pl.when(at_row == 0)
    def _():
        side_ref[0] = left_ref[...].astype(F32).reshape(side_ref.shape[1:])
        side_ref[1] = right_ref[...].astype(F32).reshape(side_ref.shape[1:])
        for ref in (sum_patch, sum_gain, sum_shift):
            ref[...] = jnp.zeros_like(ref)

    g_ref[...] = (
        dot_last(dq_ref[...], w_ref[:, :width])
        + dot_last(dk_ref[...], w_ref[:, width : 2 * width])
        + dot_last(dv_ref[...], w_ref[:, 2 * width :])
    )

    @pl.when(at_row < HALO)
    def _():
        g_ref[...] += above_ref[pl.ds(pl.multiple_of(at_row * line, line), line), :].astype(F32)

    @pl.when(at_row >= tile_rows - HALO)
    def _():
        start = (at_row - (tile_rows - HALO)) * line
        g_ref[...] += below_ref[pl.ds(pl.multiple_of(start, line), line), :].astype(F32)

    for j in range(HALO):
        source = j * tile_rows + at_row
        for f in range(frames):
            near = f * tile_cols + j
            far = near + tile_cols - HALO
            g_ref[near : near + 1, :] += side_ref[0, source, f : f + 1, :]
            g_ref[far : far + 1, :] += side_ref[1, source, f : f + 1, :]
    stream = stream_ref[...]
    grad = g_ref[...]
    centre = stream - jnp.mean(stream, -1, keepdims=True)
    inverse = lax.rsqrt(jnp.mean(centre * centre, -1, keepdims=True) + EPS)
    hat = centre * inverse
    sum_gain[...] += jnp.sum(grad * hat, 0, keepdims=True)
    sum_shift[...] += jnp.sum(grad, 0, keepdims=True)
    scaled = grad * row_of(gain_ref)
    one = gtwo_ref[...] + inverse * (
        scaled
        - jnp.mean(scaled, -1, keepdims=True)
        - hat * jnp.mean(scaled * hat, -1, keepdims=True)
    )
    sum_patch[...] += jnp.sum(one, 0, keepdims=True)
    emb_ref[...] = one.astype(BF16)


def embed_back(stream, dq, dk, dv, w, gtwo, gain, above, below, left, right, tile_rows, frames, hold):
    tokens, width = stream.shape
    line = tokens // tile_rows
    block = pl.BlockSpec((line, width), lambda r: (r, 0))
    vector = jax.ShapeDtypeStruct((1, width), F32)
    return run(
        functools.partial(embed_back_kernel, frames), "embed_back",
        (stream, dq, dk, dv, w, gtwo, gain, above, below, left, right),
        [jax.ShapeDtypeStruct((tokens, width), BF16)] + [vector] * 3,
        [
            block, block, block, block, held(w.shape), block, whole((width,)),
            whole(above.shape), whole(below.shape), whole(left.shape), whole(right.shape),
        ],
        [block] + [whole((1, width))] * 3, grid=(tile_rows,), hold=hold,
        estimate=cost(6 * tokens * width * width, 16 << 20),
        scratch=[pltpu.VMEM((line, width), F32), pltpu.VMEM((2, left.shape[0] // 8, 8, width), F32)],
    )


def lay_vectors(ref, at, vectors, quarter):
    width = ref.shape[2]
    ref[0, at:, :] = jnp.zeros((ref.shape[1] - at, width), BF16)
    lines = []
    for item in vectors:
        part = item.shape[1] // 4
        mine = jnp.zeros((1, part), F32)
        for q in range(4):
            mine = jnp.where(quarter == q, item[:, q * part : (q + 1) * part], mine)
        if part < width:
            mine = jnp.concatenate([mine, jnp.zeros((1, width - part), F32)], 1)
        lines.append(mine)
    pad = -(-len(lines) // 16) * 16 - len(lines)
    block = jnp.concatenate(lines + [jnp.zeros((pad, width), F32)], 0)
    high = block.astype(BF16)
    ref[0, at : at + block.shape[0], :] = high
    ref[0, at + block.shape[0] : at + 2 * block.shape[0], :] = (block - high.astype(F32)).astype(BF16)


def grads_patch_kernel(core_ref, pixels_ref, emb_ref, *refs):
    vectors, (send_ref, keep_ref) = refs[:-2], refs[-2:]
    step = pl.program_id(0)
    quarter = quarter_at(step, core_ref[0])
    patch = dot_first(pixels_ref[...], emb_ref[...]).astype(BF16)
    for is_sent, ref in ((True, send_ref), (False, keep_ref)):

        @pl.when((step < 2) == is_sent)
        def _():
            ref[0, : patch.shape[0], :] = patch
            lay_vectors(ref, patch.shape[0], [item[...] for item in vectors], quarter)


def grads_patch(places, pixels, emb, vectors, after):
    tokens, pix = pixels.shape
    width = emb.shape[1]
    rows = padded(pix // 4 + 64)
    return run(
        grads_patch_kernel, "grads_patch", (pixels, emb, *vectors),
        [jax.ShapeDtypeStruct((2, rows, width), BF16)] * 2,
        [
            pl.BlockSpec((tokens, pix // 4), lambda s, c: (0, quarter_at(s, c[0]))),
            held(emb.shape),
        ]
        + [whole(item.shape) for item in vectors],
        pair_specs(rows, width), grid=(4,), places=places, after=after,
        estimate=cost(2 * tokens * pix * width, 8 << 20),
    )


def pixel_back_kernel(emb_ref, w_ref, out_ref):
    out_ref[...] = dot_last(emb_ref[...], w_ref[...]).astype(BF16)


def pixel_back(emb, w, after):
    tokens, width = emb.shape
    pix = w.shape[0]
    return run(
        pixel_back_kernel, "pixel_back", (emb, w), jax.ShapeDtypeStruct((tokens, pix), BF16),
        [pl.BlockSpec((BLOCK, width), lambda i: (i, 0)), held(w.shape)],
        pl.BlockSpec((BLOCK, pix), lambda i: (i, 0)), grid=(tokens // BLOCK,), after=after,
        estimate=cost(2 * tokens * pix * width, 8 << 20),
    )


def swap(value, axis, stride):
    count = lax.axis_size(axis)
    return lax.ppermute(value, axis, [(i, i ^ stride) for i in range(count)])


def rotate(value, axis, steps):
    count = lax.axis_size(axis)
    return lax.ppermute(value, axis, [(i, (i + steps) % count) for i in range(count)])


def run(
    kernel, name, operands, out_shape, in_specs, out_specs, *, grid=(1,), places=None, after=(), hold=(),
    estimate=None, scratch=(), megabytes=28, aliases=None,
):
    scalars = () if places is None else (places,)
    count = len(scalars) + len(operands)
    extra = tuple(after) + tuple(hold)
    any_space = pl.BlockSpec(memory_space=pl.ANY)
    shapes = list(out_shape) if isinstance(out_shape, (list, tuple)) else [out_shape]
    specs = list(out_specs) if isinstance(out_specs, (list, tuple)) else [out_specs]
    own = len(shapes)

    def body(*refs):
        results = refs[count + len(extra) :]
        kernel(*refs[:count], *results[:own], *results[own + len(hold) :])

    at = count + len(after)
    aliases = dict(aliases or {})
    aliases.update({at + i: own + i for i in range(len(hold))})
    results = pl.pallas_call(
        body,
        grid_spec=pltpu.PrefetchScalarGridSpec(
            num_scalar_prefetch=len(scalars),
            grid=grid,
            in_specs=list(in_specs) + [any_space] * len(extra),
            out_specs=specs + [any_space] * len(hold),
            scratch_shapes=list(scratch),
        ),
        out_shape=shapes + [jax.ShapeDtypeStruct(item.shape, item.dtype) for item in hold],
        input_output_aliases=aliases,
        compiler_params=params(megabytes),
        cost_estimate=estimate,
        name=name,
    )(*scalars, *operands, *extra)
    return results[0] if len(results) == 1 else results


def by_rows(rows, body):
    size = next(n for n in (96, 80, 72, 64, 56, 48, 40, 32, 24, 16, 8) if rows % n == 0)

    def step(i, carry):
        body(pl.ds(pl.multiple_of(i * size, 8), size))
        return carry

    lax.fori_loop(0, rows // size, step, 0)


def add_across_kernel(places, keep_ref, came_ref, out_ref):
    def body(at):
        total = keep_ref[0, at, :].astype(F32) + came_ref[0, at, :].astype(F32)
        out_ref[at, :] = total.astype(BF16)

    by_rows(out_ref.shape[0], body)


def add_across(places, keep, came, after):
    rows, width = keep.shape[1:]
    block = pl.BlockSpec((1, rows // 2, width), lambda i, p: (1 - p[1], i, 0))
    return run(
        add_across_kernel, "add_across", (keep, came), jax.ShapeDtypeStruct((rows, width), BF16),
        [block, block], pl.BlockSpec((rows // 2, width), lambda i, p: (i, 0)),
        grid=(2,), places=places, after=after, estimate=cost(rows * width, 6 * rows * width),
        megabytes=16,
    )


def add_down_kernel(places, *refs):
    terms, outs = refs[:-2], refs[-2:]
    lead = outs[0].shape[:-2]

    for half, out_ref in enumerate(outs):

        @pl.when(pl.program_id(0) == half)
        def _():
            for i in range(lead[0] if lead else 1):

                def body(at):
                    total = sum(
                        (ref[i if lead else 0, at, :] if len(ref.shape) == 3 else ref[at, :]).astype(F32)
                        for ref in terms
                    ).astype(BF16)
                    if lead:
                        out_ref[i, at, :] = total
                    else:
                        out_ref[at, :] = total

                by_rows(out_ref.shape[-2], body)


def add_down(places, bit, terms, after, hold=()):
    shape = terms[-1].shape
    lead = shape[:-2]
    half, width = shape[-2] // 2, shape[-1]

    def which(h, p):
        return jnp.where(h == 0, 1 - p[bit], p[bit])

    same = pl.BlockSpec(lead + (half, width), lambda h, p: (0,) * len(lead) + (which(h, p), 0))
    pair = pl.BlockSpec((1, half, width), lambda h, p: (p[1], which(h, p), 0))
    out = pl.BlockSpec(lead + (half, width), lambda h, p: (0,) * len(lead) + (0, 0))
    return run(
        add_down_kernel, "add_down", terms,
        [jax.ShapeDtypeStruct(lead + (half, width), BF16)] * 2,
        [same if item.ndim == len(shape) else pair for item in terms], [out, out],
        grid=(2,), places=places, after=after, hold=hold,
        estimate=cost(half * width, 6 * half * width), megabytes=24,
    )


def add_x(places, terms, after, hold=()):
    rows, width = terms[0].shape[1:]
    block = pl.BlockSpec(
        (1, rows, width), lambda h, p: (jnp.where(h == 0, 1 - p[1], p[1]), 0, 0)
    )
    out = pl.BlockSpec((rows, width), lambda h, p: (0, 0))
    return run(
        add_down_kernel, "add_x", terms, [jax.ShapeDtypeStruct((rows, width), BF16)] * 2,
        [block] * len(terms), [out, out], grid=(2,), places=places, after=after, hold=hold,
        estimate=cost(rows * width, 6 * rows * width), megabytes=16,
    )


def add_whole_kernel(a_ref, b_ref, out_ref):
    def body(at):
        out_ref[at, :] = (a_ref[at, :].astype(F32) + b_ref[at, :].astype(F32)).astype(BF16)

    by_rows(out_ref.shape[0], body)


def add_whole(a, b, after):
    return run(
        add_whole_kernel, "add_whole", (a, b), jax.ShapeDtypeStruct(a.shape, BF16),
        [whole(a.shape)] * 2, whole(a.shape), after=after, estimate=cost(a.size, 6 * a.size),
        megabytes=16,
    )


def join_kernel(bit, places, own_ref, other_ref, out_ref):
    rows = own_ref.shape[0]
    mine = pl.multiple_of(places[bit] * rows, 8)
    theirs = pl.multiple_of((1 - places[bit]) * rows, 8)

    def body(at):
        out_ref[pl.ds(pl.multiple_of(mine + at.start, 8), at.size), :] = own_ref[at, :]
        out_ref[pl.ds(pl.multiple_of(theirs + at.start, 8), at.size), :] = other_ref[at, :]

    by_rows(rows, body)


def join(places, bit, own, other, after):
    rows, width = own.shape
    return run(
        functools.partial(join_kernel, bit), "join", (own, other),
        jax.ShapeDtypeStruct((2 * rows, width), BF16), [whole(own.shape)] * 2,
        whole((2 * rows, width)), places=places, after=after,
        estimate=cost(own.size, 8 * own.size), megabytes=16,
    )


def wide(full_ref, at, rows, cols, out_ref):
    width = full_ref.shape[1]
    for i in range(cols // width):

        def body(to):
            source = pl.ds(pl.multiple_of(at + i * rows + to.start, 8), to.size)
            out_ref[to, i * width : (i + 1) * width] = full_ref[source, :]

        by_rows(rows, body)


def finish_kernel(bit, lay_out, places, own_ref, other_ref, *refs):
    outs, full_ref = refs[:-1], refs[-1]
    rows = own_ref.shape[0]
    mine = pl.multiple_of(places[bit] * rows, 8)
    theirs = pl.multiple_of((1 - places[bit]) * rows, 8)

    def body(at):
        full_ref[pl.ds(pl.multiple_of(mine + at.start, 8), at.size), :] = own_ref[at, :].astype(F32)
        full_ref[pl.ds(pl.multiple_of(theirs + at.start, 8), at.size), :] = other_ref[at, :].astype(F32)

    by_rows(rows, body)
    lay_out(full_ref, *outs)


def finish(places, bit, own, other, lay_out, shapes, after):
    rows, width = own.shape
    return run(
        functools.partial(finish_kernel, bit, lay_out), "finish", (own, other),
        [jax.ShapeDtypeStruct(shape, F32) for shape in shapes], [whole(own.shape)] * 2,
        [whole(shape) for shape in shapes], places=places, after=after,
        estimate=cost(own.size, 16 * own.size), megabytes=16, scratch=[pltpu.VMEM((2 * rows, width), F32)],
    )


class Reduction:
    def __init__(self, order, places, pair, lay_out, shapes, late_x=False):
        self.send, self.keep = pair
        self.order, self.places = order, places
        self.lay_out, self.shapes = lay_out, shapes
        last = lax.axis_size("col").bit_length() - 2
        self.steps = [("down", i) for i in range(last)]
        if late_x:
            self.steps += [("down", last), ("x", 0), ("up", last)]
        else:
            self.steps = [("across", 0)] + self.steps + [("full", last)]
        self.steps += [("up", i) for i in reversed(range(last))] + [("end", 0)]
        self.pending = (None, 0)
        self.sent = self.result = None

    def after(self):
        return (self.order[-1].sent,) if self.order and self.order[-1] is not self else ()

    def terms(self):
        kind, bit = self.pending
        if kind is None:
            self.came = swap(self.send, "row", 1)
            return self.keep, self.came
        if kind == "across":
            return self.keep, self.came, swap(self.sent, "row", 2)
        if kind == "x":
            return self.mine, swap(self.sent, "row", 2)
        return self.mine, swap(self.sent, "col", 1 << bit)

    def advance(self, then=None):
        kind, bit = self.steps.pop(0)
        places, after = self.places, self.after()
        terms = self.terms()
        hold = () if then is None else (then.send,)
        kept = ()
        if kind == "across":
            self.sent = add_across(places, *terms, after)
        elif kind == "down":
            self.sent, self.mine, *kept = add_down(places, 2 + bit, terms, after, hold)
        elif kind == "x":
            self.sent, self.mine, *kept = add_x(places, terms, after, hold)
        elif kind == "end":
            result = finish(places, 2 + self.pending[1], *terms, self.lay_out, self.shapes, after)
            self.result = result if isinstance(result, (list, tuple)) else [result]
            self.sent = self.result[0]
        elif self.pending[0] == "up":
            self.sent = self.mine = join(places, 2 + self.pending[1], *terms, after)
        else:
            self.sent = self.mine = add_whole(*terms, after)
        if kept:
            (then.send,) = kept
        self.pending = (kind, bit)
        self.order.append(self)


class Ready:
    def __init__(self, value):
        self.sent = value


def wave_numbers(width):
    def of(part):
        half = part // 2
        one = np.float32(1.0) / np.float32(10000.0) ** (
            np.arange(half, dtype=np.float32) / np.float32(half)
        )
        return [one, one]

    unit = width // 16
    return np.concatenate(of(4 * unit) + of(6 * unit) + of(6 * unit)).astype(np.float32)[None, :]


def per_device(
    pixels, timestamps, frame_count, visible, halo_reach, w_patch, b_patch, gain_one, shift_one,
    w_qkv, b_query, b_value, w_out, b_out, gain_two, shift_two, w_up, b_up, w_down, b_down,
    w_dec, b_dec, w_pix, b_pix, cotangent,
):
    tile_rows, tile_cols, frames, pix_width = pixels.shape
    model_width = w_patch.shape[1]
    tokens = tile_rows * tile_cols * frames
    ff = w_up.shape[1]
    grid_shape = (tile_rows, frames, tile_cols)
    side = tile_rows * 8 * HALO
    band = HALO * frames * tile_cols
    row_at, col_at = lax.axis_index("row"), lax.axis_index("col")
    col_bits = lax.axis_size("col").bit_length() - 1
    places = jnp.stack(
        [row_at % 2, row_at // 2] + [(col_at >> i) % 2 for i in range(col_bits)]
    ).astype(jnp.int32)

    flat_pixels = pixels.transpose(0, 2, 1, 3).reshape(tokens, pix_width)
    flat_cotangent = cotangent.transpose(0, 2, 1, 3).reshape(tokens, pix_width)
    stream_one, normed_one, high, low, tail, head, flags = embed(
        timestamps.reshape(-1), frame_count.reshape(-1), visible.transpose(2, 0, 1), flat_pixels,
        w_patch, b_patch, gain_one, shift_one, wave_numbers(model_width),
    )
    upper = rotate(high, "row", 1)
    lower = rotate(low, "row", -1)
    left = rotate(tail, "col", 1)
    right = rotate(head, "col", -1)
    query, key, value = own_qkv(normed_one, w_qkv, b_query, b_value)
    grad_dec, grad_stream, grad_mlp, sum_pix, sum_dec, sum_down = decode_back(
        flat_cotangent, w_pix, w_dec
    )
    strip_key, strip_value, strip_rows, bias = strip_kv(
        halo_reach.reshape(-1), upper, lower, left, right, flags, w_qkv, b_value
    )
    mixed, log_total = attend(query, key, value, strip_key, strip_value, bias)
    (
        pixel_out, normed_two, act, grad_pre, stream_low, decoded, attended,
        grad_two, grad_att, grad_attended, sum_up, sum_out, sum_gain_two, sum_shift_two,
    ) = mlp(
        stream_one, mixed, grad_stream, w_out, b_out, gain_two, shift_two,
        w_up, b_up, w_down, b_down, w_dec, b_dec, w_pix, b_pix,
    )
    fixed = (query, key, value, strip_key, strip_value)
    rest = (mixed, log_total, bias)
    pairs = model_width // LANES
    third = pairs // 3
    quarter = model_width // 4
    patch_rows, down_rows = pix_width // 4, ff // 4
    pix_rows, up_rows = w_dec.shape[1] // 4, quarter * (ff // model_width)
    dec_width = w_dec.shape[1]
    cut = quarter * 2 // 3
    order = []

    def lay_down(full, down_ref, pix_ref, dec_ref):
        wide(full, 0, down_rows, model_width, down_ref)
        wide(full, down_rows, pix_rows, pix_width, pix_ref)
        at, tall = down_rows + pix_rows * (pix_width // model_width), quarter - cut
        dec_ref[:cut, :] = full[at : at + cut, :dec_width]
        dec_ref[cut:, : model_width - dec_width] = full[at : at + tall, dec_width:]
        dec_ref[cut:, model_width - dec_width :] = full[at + tall : at + cut, dec_width:]

    def lay_up(full, up_ref, out_ref):
        wide(full, 0, quarter, ff, up_ref)
        wide(full, up_rows, quarter, model_width, out_ref)

    def lay_middle(full, qkv_ref):
        wide(full, 0, quarter, 3 * model_width, qkv_ref)

    def lay_last(full, patch_ref, *refs):
        wide(full, 0, patch_rows, model_width, patch_ref)
        lines = -(-len(refs) // 16) * 16
        for i, ref in enumerate(refs):
            at = patch_rows + i
            size = ref.shape[1]
            ref[...] = full[at : at + 1, :size] + full[at + lines : at + lines + 1, :size]

    down = Reduction(
        order, places,
        grads_down(places, act, grad_mlp, decoded, flat_cotangent, stream_low, grad_dec), lay_down,
        [(down_rows, model_width), (pix_rows, pix_width), (quarter, dec_width)], late_x=True,
    )
    up = Reduction(
        order, places, grads_up(places, normed_two, grad_pre, attended, grad_att, (down.keep,)),
        lay_up, [(quarter, ff), (quarter, model_width)],
    )
    down.advance()
    up.advance()
    most = pairs * 2 // 3
    back = attend_back(*fixed, grad_attended, *rest, 0, most, (), (down.sent, up.sent))
    order.append(Ready(back[0]))
    down.advance()
    up.advance()
    back = attend_back(
        *fixed, grad_attended, *rest, most, pairs - most, back, (up.sent, down.sent)
    )
    dq, dk, dv, dks, dvs, sum_query, sum_value = back
    order.append(Ready(dq))
    down.advance()
    up.advance()
    upper_back, lower_back, left_back, right_back = strip_back(
        dks, dvs, w_qkv, band, side, (up.sent,)
    )
    from_right = rotate(left_back, "col", -1)
    from_left = rotate(right_back, "col", 1)
    from_below = rotate(upper_back, "row", -1)
    from_above = rotate(lower_back, "row", 1)
    middle = Reduction(
        order, places,
        grads_qkv(places, normed_one, strip_rows, dq, dk, dv, dks, dvs, (upper_back,)),
        lay_middle, [(quarter, 3 * model_width)],
    )
    grad_emb, sum_patch, sum_gain_one, sum_shift_one, up.sent = embed_back(
        stream_one, dq, dk, dv, w_qkv, grad_two, gain_one, from_above,
        from_below, from_left, from_right, tile_rows, frames, (up.sent,),
    )
    vectors = [
        sum_patch, sum_gain_one, sum_shift_one, sum_query, sum_value, sum_out, sum_gain_two,
        sum_shift_two, sum_up, sum_down, sum_dec, sum_pix,
    ]
    order.append(Ready(grad_emb))
    down.advance(middle)
    last = Reduction(
        order, places, grads_patch(places, flat_pixels, grad_emb, vectors, (down.sent,)),
        lay_last, [(patch_rows, model_width)] + [(1, item.shape[1] // 4) for item in vectors],
    )
    groups = {"d": down, "u": up, "m": middle, "l": last}
    for turn in EVENTS:
        if turn == "p":
            pixel_grad = pixel_back(grad_emb, w_patch, (order[-1].sent,))
            order.append(Ready(pixel_grad))
        elif groups[turn].steps:
            groups[turn].advance()
    while any(each.steps for each in groups.values()):
        for each in groups.values():
            if each.steps:
                each.advance()
    share_down, share_pix, share_dec = down.result
    share_up, share_out = up.result
    (share_qkv,) = middle.result
    share_patch, *pieces = last.result
    pieces = [item.reshape(-1) for item in pieces]

    def to_scene(flat):
        return flat.reshape(grid_shape + (pix_width,)).transpose(0, 2, 1, 3)

    return (
        to_scene(pixel_out), to_scene(pixel_grad), share_patch, pieces[0], pieces[1], pieces[2],
        share_qkv, pieces[3], pieces[4], share_out, pieces[5], pieces[6], pieces[7], share_up,
        pieces[8], share_down, pieces[9], share_dec, pieces[10], share_pix, pieces[11],
    )


def solution(mesh):
    tiles = P("row", "col", None, None)
    return jax.shard_map(
        per_device,
        mesh=mesh,
        in_specs=(
            tiles,
            P("row", "col", None),
            P("row", "col"),
            P("row", "col", None),
            P("row", "col"),
        )
        + (P(),) * 19
        + (tiles,),
        out_specs=(
            tiles,
            tiles,
            P("row", None),
            P("row"),
            P("row"),
            P("row"),
            P("row", None),
            P("row"),
            P("row"),
            P("row", None),
            P("row"),
            P("row"),
            P("row"),
            P("row", None),
            P("row"),
            P("row", None),
            P("row"),
            P("row", None),
            P("row"),
            P("row", None),
            P("row"),
        ),
        check_vma=False,
    )
```

```python
import functools
import math

import jax
import jax.numpy as jnp
import numpy as np
from jax import lax
from jax.experimental import pallas as pl
from jax.experimental.pallas import tpu as pltpu
from jax.sharding import PartitionSpec as P

HEAD_WIDTH = 64
HALO = 2
EPS = 1e-06
NEG_FILL = -1e30
BLOCK = 256
LANES = 128
KEY_BLOCK = 512
FF_BLOCK = 1024
EVENTS = "mldumulmulmdmudlmldlmpl"
SCALE = HEAD_WIDTH**-0.5
LOG_SCALE = SCALE * math.log2(math.e)
F32 = jnp.float32
BF16 = jnp.bfloat16


def dot_last(a, b):
    return lax.dot_general(a, b, (((1,), (1,)), ((), ())), preferred_element_type=F32)


def dot_plain(a, b):
    return lax.dot_general(a, b, (((1,), (0,)), ((), ())), preferred_element_type=F32)


def one_head(pair, head):
    lane = lax.broadcasted_iota(jnp.int32, pair.shape, 1)
    keep = (lane < HEAD_WIDTH) if head == 0 else (lane >= HEAD_WIDTH)
    return jnp.where(keep, pair, jnp.zeros_like(pair))


def diagonal(size):
    rows = lax.broadcasted_iota(jnp.int32, (size, size), 0)
    return rows == lax.broadcasted_iota(jnp.int32, (size, size), 1)


def row_of(ref):
    return ref[...].astype(F32).reshape(1, -1)


def params(megabytes):
    return pltpu.CompilerParams(vmem_limit_bytes=megabytes << 20)


def cost(flops, moved):
    return pl.CostEstimate(flops=flops, bytes_accessed=moved, transcendentals=0)


def whole(shape):
    return pl.BlockSpec(shape, lambda *_: (0,) * len(shape))


def held(shape):
    return pl.BlockSpec(shape, lambda *_: (0,) * len(shape), pipeline_mode=pl.Buffered(1))


def embed_kernel(
    stamps_ref,
    count_ref,
    visible_ref,
    pixels_ref,
    w_ref,
    b_ref,
    gain_ref,
    shift_ref,
    wave_ref,
    stream_ref,
    normed_ref,
    high_ref,
    low_ref,
    tail_ref,
    head_ref,
    flags_ref,
    edge_ref,
    time_ref,
    col_ref,
    n_ref,
):
    at_row = pl.program_id(0)
    width = w_ref.shape[1]
    frames, tile_rows, tile_cols = visible_ref.shape
    line = frames * tile_cols
    band = HALO * line

    lane = lax.broadcasted_iota(jnp.int32, (1, width), 1)
    t_end, r_end = width // 4, width // 4 + width * 3 // 8
    t_mid, r_mid, c_mid = width // 8, t_end + width * 3 // 16, r_end + width * 3 // 16

    def waves(places):
        angles = places * wave_ref[...]
        is_sin = (lane < t_mid) | ((lane >= t_end) & (lane < r_mid)) | ((lane >= r_end) & (lane < c_mid))
        return jnp.where(is_sin, jnp.sin(angles), jnp.cos(angles))

    @pl.when(at_row == 0)
    def _():
        slot = lax.broadcasted_iota(jnp.int32, (8, 1), 0)
        stamps = jnp.zeros((8, 1), F32)
        for f in range(frames):
            stamps = jnp.where(slot == f, stamps_ref[f].astype(F32), stamps)
        time_ref[...] = jnp.where(lane < t_end, waves(stamps), 0.0)
        cols = lax.axis_index("col") * tile_cols + lax.broadcasted_iota(
            jnp.int32, (tile_cols, 1), 0
        )
        col_ref[...] = jnp.where(lane >= r_end, waves(cols.astype(F32)), 0.0)
        frame_at = lax.broadcasted_iota(jnp.int32, visible_ref.shape, 0)
        ok = ((frame_at < count_ref[0]) & (visible_ref[...] == 1)).astype(F32)
        pieces = [ok[f, r : r + 1, :] for r in range(tile_rows) for f in range(frames)]
        flat = jnp.concatenate(pieces, 1)
        flags_ref[...] = jnp.broadcast_to(flat, flags_ref.shape)
        edge_ref[...] = jnp.zeros_like(edge_ref)
        nothing = [jnp.zeros((8 - frames, tile_cols), F32)]
        stacked = jnp.concatenate(
            sum((pieces[r * frames : (r + 1) * frames] + nothing for r in range(tile_rows)), []), 0
        )
        slot = lax.broadcasted_iota(jnp.int32, (8, tile_cols), 0)
        col = lax.broadcasted_iota(jnp.int32, (8, tile_cols), 1)
        last = HALO * tile_rows
        chunk = 8 * tile_rows
        edge_ref[0, last, :, :chunk] = dot_last(
            (col == slot + tile_cols - HALO).astype(F32), stacked
        )
        edge_ref[1, last, :, :chunk] = dot_last((col == slot).astype(F32), stacked)

    places = (lax.axis_index("row") * tile_rows + at_row).astype(F32)
    row_part = jnp.where((lane >= t_end) & (lane < r_end), waves(jnp.full((1, 1), places)), 0.0)
    base = row_of(b_ref) + row_part
    stream = dot_plain(pixels_ref[...], w_ref[...])
    position = jnp.concatenate(
        [col_ref[...] + (time_ref[f : f + 1, :] + base) for f in range(frames)], 0
    )
    stream = stream + position
    stream_ref[...] = stream
    centre = stream - jnp.mean(stream, -1, keepdims=True)
    spread = jnp.mean(centre * centre, -1, keepdims=True)
    normed = centre * lax.rsqrt(spread + EPS) * row_of(gain_ref) + row_of(shift_ref)
    low = normed.astype(BF16)
    normed_ref[...] = low
    n_ref[...] = low.astype(F32)
    for j in range(HALO):
        target = j * tile_rows + at_row
        for f in range(frames):
            near = f * tile_cols + j
            far = near + tile_cols - HALO
            edge_ref[0, target, f : f + 1, :] = n_ref[far : far + 1, :]
            edge_ref[1, target, f : f + 1, :] = n_ref[near : near + 1, :]

    @pl.when(at_row < HALO)
    def _():
        low_ref[pl.ds(pl.multiple_of(at_row * line, line), line), :] = low

    @pl.when(at_row >= tile_rows - HALO)
    def _():
        start = (at_row - (tile_rows - HALO)) * line
        high_ref[pl.ds(pl.multiple_of(start, line), line), :] = low

    @pl.when(at_row == tile_rows - 1)
    def _():
        tail_ref[...] = edge_ref[0].reshape(tail_ref.shape).astype(BF16)
        head_ref[...] = edge_ref[1].reshape(head_ref.shape).astype(BF16)
        zeros = jnp.zeros((8, width - band), BF16)
        total = flags_ref.shape[1]
        low_ref[band : band + 8, :band] = flags_ref[:, :band].astype(BF16)
        low_ref[band : band + 8, band:] = zeros
        high_ref[band : band + 8, :band] = flags_ref[:, total - band :].astype(BF16)
        high_ref[band : band + 8, band:] = zeros


def embed(stamps, count, visible, pixels, w, b, gain, shift, wave):
    tokens, depth = pixels.shape
    width = w.shape[1]
    frames, tile_rows, tile_cols = visible.shape
    line = frames * tile_cols
    band = HALO * line
    side = HALO * tile_rows * 8
    smem = pl.BlockSpec(memory_space=pltpu.SMEM)
    block = pl.BlockSpec((line, width), lambda r: (r, 0))
    return pl.pallas_call(
        embed_kernel,
        grid=(tile_rows,),
        in_specs=[
            smem,
            smem,
            whole(visible.shape),
            pl.BlockSpec((line, depth), lambda r: (r, 0)),
            held(w.shape),
            whole((width,)),
            whole((width,)),
            whole((width,)),
            whole((1, width)),
        ],
        out_specs=[
            block,
            block,
            whole((band + 8, width)),
            whole((band + 8, width)),
            whole((side + 8, width)),
            whole((side + 8, width)),
            whole((8, tokens)),
        ],
        out_shape=[
            jax.ShapeDtypeStruct((tokens, width), F32),
            jax.ShapeDtypeStruct((tokens, width), BF16),
            jax.ShapeDtypeStruct((band + 8, width), BF16),
            jax.ShapeDtypeStruct((band + 8, width), BF16),
            jax.ShapeDtypeStruct((side + 8, width), BF16),
            jax.ShapeDtypeStruct((side + 8, width), BF16),
            jax.ShapeDtypeStruct((8, tokens), F32),
        ],
        scratch_shapes=[
            pltpu.VMEM((2, side // 8 + 1, 8, width), F32),
            pltpu.VMEM((8, width), F32),
            pltpu.VMEM((tile_cols, width), F32),
            pltpu.VMEM((line, width), F32),
        ],
        compiler_params=params(60),
        cost_estimate=cost(2 * tokens * depth * width, 10 << 20),
        name="embed",
    )(stamps, count, visible, pixels, w, b, gain, shift, wave)


def decode_back_kernel(
    cot_ref, w_pix_ref, w_dec_ref, dec_ref, out_ref, mlp_ref, sum_pix, sum_dec, sum_down
):
    @pl.when(pl.program_id(0) == 0)
    def _():
        sum_pix[...] = jnp.zeros_like(sum_pix)
        sum_dec[...] = jnp.zeros_like(sum_dec)
        sum_down[...] = jnp.zeros_like(sum_down)

    grad_dec = dot_last(cot_ref[...], w_pix_ref[...]).astype(BF16)
    dec_ref[...] = grad_dec
    grad_out = dot_last(grad_dec, w_dec_ref[...])
    out_ref[...] = grad_out
    low = grad_out.astype(BF16)
    mlp_ref[...] = low
    sum_pix[...] += jnp.sum(cot_ref[...].astype(F32), 0, keepdims=True)
    sum_dec[...] += jnp.sum(grad_dec.astype(F32), 0, keepdims=True)
    sum_down[...] += jnp.sum(low.astype(F32), 0, keepdims=True)


def decode_back(cot, w_pix, w_dec):
    tokens, pix = cot.shape
    width, dec = w_dec.shape

    def block(size):
        return pl.BlockSpec((BLOCK, size), lambda i: (i, 0))

    return pl.pallas_call(
        decode_back_kernel,
        grid=(tokens // BLOCK,),
        in_specs=[block(pix), held(w_pix.shape), held(w_dec.shape)],
        out_specs=[
            block(dec),
            block(width),
            block(width),
            whole((1, pix)),
            whole((1, dec)),
            whole((1, width)),
        ],
        out_shape=[
            jax.ShapeDtypeStruct((tokens, dec), BF16),
            jax.ShapeDtypeStruct((tokens, width), F32),
            jax.ShapeDtypeStruct((tokens, width), BF16),
            jax.ShapeDtypeStruct((1, pix), F32),
            jax.ShapeDtypeStruct((1, dec), F32),
            jax.ShapeDtypeStruct((1, width), F32),
        ],
        compiler_params=params(16),
        cost_estimate=cost(2 * tokens * dec * (pix + width), 10 << 20),
        name="decode_back",
    )(cot, w_pix, w_dec)


def own_qkv_kernel(x_ref, w_ref, bq_ref, bv_ref, q_ref, k_ref, v_ref):
    width = x_ref.shape[1]
    x = x_ref[...]
    q_ref[...] = (dot_plain(x, w_ref[:, :width]) + row_of(bq_ref)).astype(BF16)
    k_ref[...] = dot_plain(x, w_ref[:, width : 2 * width]).astype(BF16)
    v_ref[...] = (dot_plain(x, w_ref[:, 2 * width :]) + row_of(bv_ref)).astype(BF16)


def own_qkv(x, w, bq, bv):
    tokens, width = x.shape
    block = pl.BlockSpec((BLOCK, width), lambda i: (i, 0))
    return pl.pallas_call(
        own_qkv_kernel,
        grid=(tokens // BLOCK,),
        in_specs=[block, held(w.shape), whole((width,)), whole((width,))],
        out_specs=[block] * 3,
        out_shape=[jax.ShapeDtypeStruct((tokens, width), BF16)] * 3,
        compiler_params=params(16),
        cost_estimate=cost(6 * tokens * width * width, 8 << 20),
        name="own_qkv",
    )(x, w, bq, bv)


def strip_kv_kernel(
    reach_ref, upper_ref, lower_ref, left_ref, right_ref, flags_ref, w_ref, bv_ref,
    k_ref, v_ref, rows_ref, bias_ref,
):
    band = upper_ref.shape[0] - 8
    side = left_ref.shape[0] - 8
    tokens = flags_ref.shape[1]
    total = rows_ref.shape[0]
    at = pl.program_id(0)

    @pl.when(at == 0)
    def _():
        rows_ref[:band, :] = upper_ref[:band, :]
        rows_ref[band : 2 * band, :] = lower_ref[:band, :]
        rows_ref[2 * band : 2 * band + side, :] = left_ref[:side, :]
        rows_ref[2 * band + side : 2 * (band + side), :] = right_ref[:side, :]
        if total > 2 * (band + side):
            rows_ref[2 * (band + side) :, :] = jnp.zeros(
                (total - 2 * (band + side), rows_ref.shape[1]), BF16
            )
        reach = reach_ref[0]
        line = band // HALO
        where = lax.broadcasted_iota(jnp.int32, (1, band), 1) // line
        near = (reach >= where + 1).astype(F32)
        far = (reach >= HALO - where).astype(F32)
        upper_ok = upper_ref[band : band + 1, :band].astype(F32) * far
        lower_ok = lower_ref[band : band + 1, :band].astype(F32) * near
        chunk = side // HALO
        spare = total - 2 * band
        source = lax.broadcasted_iota(jnp.int32, (LANES, spare), 0)
        target = lax.broadcasted_iota(jnp.int32, (LANES, spare), 1)
        sides = jnp.zeros((8, spare), F32)
        for j in range(HALO):
            for part, ref, need in ((0, left_ref, HALO - j), (1, right_ref, j + 1)):
                place = (target == source + part * side + j * chunk) & (source < chunk)
                line_ok = jnp.broadcast_to(
                    ref[side : side + 8, :LANES].astype(F32)[j : j + 1], (8, LANES)
                )
                moved = dot_plain(line_ok.astype(BF16), place.astype(BF16))
                sides = sides + jnp.where(reach >= need, moved, 0.0)
        bias_ref[:, :tokens] = jnp.where(flags_ref[...] > 0.5, 0.0, NEG_FILL)
        bias_ref[:, tokens : tokens + band] = jnp.broadcast_to(
            jnp.where(upper_ok > 0.5, 0.0, NEG_FILL), (8, band)
        )
        bias_ref[:, tokens + band : tokens + 2 * band] = jnp.broadcast_to(
            jnp.where(lower_ok > 0.5, 0.0, NEG_FILL), (8, band)
        )
        bias_ref[:, tokens + 2 * band :] = jnp.where(sides > 0.5, 0.0, NEG_FILL)
        k_ref[...] = dot_plain(rows_ref[...], w_ref[...]).astype(BF16)

    @pl.when(at == 1)
    def _():
        v_ref[...] = (dot_plain(rows_ref[...], w_ref[...]) + row_of(bv_ref)).astype(BF16)


def strip_kv(reach, upper, lower, left, right, flags, w, bv):
    width = w.shape[0]
    tokens = flags.shape[1]
    keys = 2 * (upper.shape[0] - 8) + 2 * (left.shape[0] - 8)
    total = -(-(tokens + keys) // LANES) * LANES - tokens
    strip = jax.ShapeDtypeStruct((total, width), BF16)
    return pl.pallas_call(
        strip_kv_kernel,
        grid=(2,),
        in_specs=[
            pl.BlockSpec(memory_space=pltpu.SMEM),
            whole(upper.shape),
            whole(lower.shape),
            whole(left.shape),
            whole(right.shape),
            whole(flags.shape),
            pl.BlockSpec((width, width), lambda i: (0, i + 1)),
            whole((width,)),
        ],
        out_specs=[whole((total, width))] * 3 + [whole((8, tokens + total))],
        out_shape=[strip] * 3 + [jax.ShapeDtypeStruct((8, tokens + total), F32)],
        compiler_params=params(16),
        cost_estimate=cost(4 * total * width * width, 8 << 20),
        name="strip_kv",
    )(reach, upper, lower, left, right, flags, w, bv)


def attend_kernel(
    q_ref, k_ref, v_ref, ks_ref, vs_ref, bias_ref, out_ref, log_ref, s_ref, keys_ref, values_ref, own_ref
):
    tokens = q_ref.shape[0]
    keys = keys_ref.shape[0]
    keys_ref[:tokens, :] = k_ref[...]
    keys_ref[tokens:, :] = ks_ref[...]
    for ref, rows in ((v_ref, slice(0, tokens)), (vs_ref, slice(tokens, keys))):
        values = ref[...]
        lane = lax.broadcasted_iota(jnp.int32, values.shape, 1)
        values_ref[0, rows, :] = jnp.where(lane < HEAD_WIDTH, values, jnp.ones_like(values))
        values_ref[1, rows, :] = jnp.where(lane >= HEAD_WIDTH, values, jnp.ones_like(values))

    @pl.when(pl.program_id(0) == 0)
    def _():
        own_ref[...] = bias_ref[:, :tokens].T[:, 0:1]

    block = tokens // 2
    lane = lax.broadcasted_iota(jnp.int32, (block, LANES), 1)
    spans = [(at, min(KEY_BLOCK, keys - at)) for at in range(0, keys, KEY_BLOCK)]
    units = [(at, head) for at in range(0, tokens, block) for head in range(2)]

    def query(unit):
        at, head = unit
        return one_head(q_ref[at : at + block, :], head)

    def score(q_head, span, slot, top):
        at, size = span
        scores = dot_last(q_head, keys_ref[at : at + size, :]) + bias_ref[0:1, at : at + size]
        s_ref[slot, :, at : at + size] = scores
        for part in range(0, size, LANES):
            piece = scores[:, part : part + LANES]
            top = piece if top is None else jnp.maximum(top, piece)
        return top

    def own_term(unit, q_head, top):
        at = unit[0]
        own_keys = keys_ref[at : at + block, :].astype(F32)
        score_own = jnp.sum(q_head.astype(F32) * own_keys, 1, keepdims=True)
        score_own = jnp.where(own_ref[at : at + block, :] < 0, score_own, NEG_FILL)
        top = jnp.maximum(jnp.max(top, 1, keepdims=True), score_own) * LOG_SCALE
        return top, jnp.exp2(score_own * LOG_SCALE - top).astype(BF16).astype(F32)

    def weigh(unit, span, slot, top, mixed):
        at, size = span
        weights = jnp.exp2(s_ref[slot, :, at : at + size] * LOG_SCALE - top).astype(BF16)
        part = dot_plain(weights, values_ref[unit[1], at : at + size, :])
        return part if mixed is None else mixed + part

    q_head, best = query(units[0]), None
    for span in spans:
        best = score(q_head, span, 0, best)
    top, own = own_term(units[0], q_head, best)
    first = None
    for number, unit in enumerate(units):
        at, head = unit
        follows = units[number + 1] if number + 1 < len(units) else None
        q_head = query(follows) if follows else None
        best = mixed = None
        for span in spans:
            if follows:
                best = score(q_head, span, (number + 1) % 2, best)
            mixed = weigh(unit, span, number % 2, top, mixed)
        mixed = mixed + own * values_ref[head, at : at + block, :].astype(F32)
        total = mixed[:, HEAD_WIDTH : HEAD_WIDTH + 1] if head == 0 else mixed[:, 0:1]
        log_ref[0, head, at : at + block] = (top + jnp.log2(total))[:, 0]
        if head == 0:
            first = mixed / total
        else:
            out_ref[at : at + block, :] = jnp.where(lane < HEAD_WIDTH, first, mixed / total)
        if follows:
            top, own = own_term(follows, q_head, best)


def attend(q, k, v, ks, vs, bias):
    tokens, width = q.shape
    keys = tokens + ks.shape[0]
    pairs = width // LANES
    own = pl.BlockSpec((tokens, LANES), lambda p: (0, p))
    strip = pl.BlockSpec((keys - tokens, LANES), lambda p: (0, p))
    return pl.pallas_call(
        attend_kernel,
        grid=(pairs,),
        in_specs=[own, own, own, strip, strip, whole((8, keys))],
        out_specs=[own, pl.BlockSpec((1, 2, tokens), lambda p: (p, 0, 0))],
        out_shape=[
            jax.ShapeDtypeStruct((tokens, width), F32),
            jax.ShapeDtypeStruct((pairs, 2, tokens), F32),
        ],
        scratch_shapes=[
            pltpu.VMEM((2, tokens // 2, keys), F32),
            pltpu.VMEM((keys, LANES), BF16),
            pltpu.VMEM((2, keys, LANES), BF16),
            pltpu.VMEM((tokens, 1), F32),
        ],
        compiler_params=params(24),
        cost_estimate=cost(16 * tokens * keys * width, 8 << 20),
        name="attend",
    )(q, k, v, ks, vs, bias)


def attend_back_kernel(
    q_ref, k_ref, v_ref, ks_ref, vs_ref, do_ref, o_ref, log_ref, bias_ref,
    dq_ref, dk_ref, dv_ref, dks_ref, dvs_ref, sum_q, sum_v,
    keys_ref, values_ref, kt_ref, mask_ref,
):
    tokens = q_ref.shape[0]
    keys_ref[:tokens, :] = k_ref[...]
    keys_ref[tokens:, :] = ks_ref[...]
    values_ref[:tokens, :] = v_ref[...]
    values_ref[tokens:, :] = vs_ref[...]
    kt_ref[...] = keys_ref[...].T

    @pl.when(pl.program_id(0) == 0)
    def _():
        mask_ref[...] = bias_ref[...].T[:, 0:1]

    q, do = q_ref[...], do_ref[...]
    wide_q, wide_do, wide_k = q.astype(F32), do.astype(F32), k_ref[...].astype(F32)
    with_out = (wide_do * o_ref[...]).T
    with_key = (wide_q * wide_k).T
    with_value = (wide_do * v_ref[...].astype(F32)).T
    hidden = bias_ref[0:1, :tokens] < 0
    dk = dv = None
    dq, own_weights, own_grads = [], [], []
    for head in range(2):
        part = slice(head * HEAD_WIDTH, (head + 1) * HEAD_WIDTH)
        delta = jnp.sum(with_out[part], axis=0, keepdims=True)
        log_total = log_ref[0, head : head + 1, :]
        own = jnp.sum(with_key[part], axis=0, keepdims=True) * LOG_SCALE - log_total
        own = jnp.where(hidden, jnp.exp2(jnp.where(hidden, own, 0.0)), 0.0)
        own_grad = own * (jnp.sum(with_value[part], axis=0, keepdims=True) - delta)
        own_weights.append(own.astype(BF16).astype(F32))
        own_grads.append(own_grad.astype(BF16).astype(F32))
        q_head = one_head(q, head)
        do_head = one_head(do, head)
        scores = dot_last(keys_ref[...], q_head) + mask_ref[...]
        weights = jnp.exp2(scores * LOG_SCALE - log_total)
        back = dot_last(values_ref[...], do_head)
        grad = (weights * (back - delta)).astype(BF16)
        dv_part = dot_plain(weights.astype(BF16), do_head)
        dk_part = dot_plain(grad, q_head)
        dv = dv_part if dv is None else dv + dv_part
        dk = dk_part if dk is None else dk + dk_part
        dq.append(dot_plain(kt_ref[...], grad))

    def per_lane(rows):
        return jnp.concatenate([jnp.broadcast_to(row, (HEAD_WIDTH, tokens)) for row in rows], 0).T

    own, own_grad = per_lane(own_weights), per_lane(own_grads)
    dv_own = (dv[:tokens] + own * wide_do).astype(BF16)
    dv_strip = dv[tokens:].astype(BF16)
    dv_ref[...] = dv_own
    dvs_ref[...] = dv_strip
    dk_ref[...] = ((dk[:tokens] + own_grad * wide_q) * SCALE).astype(BF16)
    dks_ref[...] = (dk[tokens:] * SCALE).astype(BF16)
    joined = jnp.concatenate([dq[0][:HEAD_WIDTH], dq[1][HEAD_WIDTH:]], axis=0).T
    low = ((joined + own_grad * wide_k) * SCALE).astype(BF16)
    dq_ref[...] = low
    sum_q[...] = jnp.sum(low.astype(F32), 0, keepdims=True)
    sum_v[...] = jnp.sum(dv_own.astype(F32), 0, keepdims=True) + jnp.sum(
        dv_strip.astype(F32), 0, keepdims=True
    )


def attend_back(q, k, v, ks, vs, do, o, log_total, bias, first, count, before, after):
    tokens, width = q.shape
    keys = tokens + ks.shape[0]
    own = pl.BlockSpec((tokens, LANES), lambda p: (0, p + first))
    strip = pl.BlockSpec((keys - tokens, LANES), lambda p: (0, p + first))
    line = pl.BlockSpec((1, LANES), lambda p: (0, p + first))
    return run(
        attend_back_kernel, "attend_back", (q, k, v, ks, vs, do, o, log_total, bias),
        [jax.ShapeDtypeStruct((tokens, width), BF16)] * 3
        + [jax.ShapeDtypeStruct((keys - tokens, width), BF16)] * 2
        + [jax.ShapeDtypeStruct((1, width), F32)] * 2,
        [
            own, own, own, strip, strip, own, own,
            pl.BlockSpec((1, 2, tokens), lambda p: (p + first, 0, 0)),
            whole((8, keys)),
        ],
        [own, own, own, strip, strip, line, line], grid=(count,), after=tuple(before) + tuple(after),
        aliases={9 + i: i for i in range(len(before))},
        estimate=cost(24 * tokens * keys * LANES * count, 3 * count << 20), megabytes=40,
        scratch=[
            pltpu.VMEM((keys, LANES), BF16),
            pltpu.VMEM((keys, LANES), BF16),
            pltpu.VMEM((LANES, keys), BF16),
            pltpu.VMEM((keys, 1), F32),
        ],
    )


def dot_first(a, b):
    return lax.dot_general(a, b, (((0,), (0,)), ((), ())), preferred_element_type=F32)


def mlp_kernel(
    one_ref, att_ref, gout_ref, w_out_ref, b_out_ref, gain_ref, shift_ref, w_up_ref, b_up_ref,
    w_down_ref, b_down_ref, w_dec_ref, b_dec_ref, w_pix_ref, b_pix_ref,
    pix_ref, normed_ref, act_ref, gup_ref, low_ref, decoded_ref, attended_ref,
    gtwo_ref, gatt_ref, gattended_ref, sum_up, sum_out, sum_gain, sum_shift,
    bias_ref, out_ref, gnormed_ref,
):
    @pl.when(pl.program_id(0) == 0)
    def _():
        bias_ref[...] = row_of(b_up_ref)
        for ref in (sum_up, sum_out, sum_gain, sum_shift):
            ref[...] = jnp.zeros_like(ref)

    ff = w_up_ref.shape[1]
    attended = att_ref[...].astype(BF16)
    attended_ref[...] = attended
    two = one_ref[...] + dot_plain(attended, w_out_ref[...]) + row_of(b_out_ref)
    centre = two - jnp.mean(two, -1, keepdims=True)
    inverse = lax.rsqrt(jnp.mean(centre * centre, -1, keepdims=True) + EPS)
    gain = row_of(gain_ref)
    normed = (centre * inverse * gain + row_of(shift_ref)).astype(BF16)
    normed_ref[...] = normed
    gout = gout_ref[...]
    gmlp = gout.astype(BF16)
    out_ref[...] = two + row_of(b_down_ref)
    gnormed_ref[...] = jnp.zeros_like(two)

    def step(i, carry):
        cols = pl.ds(pl.multiple_of(i * FF_BLOCK, FF_BLOCK), FF_BLOCK)
        up = dot_plain(normed, w_up_ref[:, cols]) + bias_ref[:, cols]
        bell = 0.5 * (1.0 + lax.erf(up * math.sqrt(0.5)))
        act = (up * bell).astype(BF16)
        slope = bell + up * (jnp.exp2(up * up * (-0.5 * math.log2(math.e))) * (2 * math.pi) ** -0.5)
        act_ref[:, cols] = act
        out_ref[...] += dot_plain(act, w_down_ref[cols, :])
        gup = (dot_last(gmlp, w_down_ref[cols, :]) * slope).astype(BF16)
        gup_ref[:, cols] = gup
        sum_up[:, cols] += jnp.sum(gup.astype(F32), 0, keepdims=True)
        gnormed_ref[...] += dot_last(gup, w_up_ref[:, cols])
        return carry

    lax.fori_loop(0, ff // FF_BLOCK, step, 0)
    out = out_ref[...]
    gnormed = gnormed_ref[...]
    low = out.astype(BF16)
    low_ref[...] = low
    decoded = (dot_plain(low, w_dec_ref[...]) + row_of(b_dec_ref)).astype(BF16)
    decoded_ref[...] = decoded
    pix_ref[...] = (dot_plain(decoded, w_pix_ref[...]) + row_of(b_pix_ref)).astype(BF16)
    hat = centre * inverse
    sum_gain[...] += jnp.sum(gnormed * hat, 0, keepdims=True)
    sum_shift[...] += jnp.sum(gnormed, 0, keepdims=True)
    scaled = gnormed * gain
    back = inverse * (
        scaled
        - jnp.mean(scaled, -1, keepdims=True)
        - hat * jnp.mean(scaled * hat, -1, keepdims=True)
    )
    gtwo = gout + back
    gtwo_ref[...] = gtwo
    gatt = gtwo.astype(BF16)
    gatt_ref[...] = gatt
    sum_out[...] += jnp.sum(gatt.astype(F32), 0, keepdims=True)
    gattended_ref[...] = dot_last(gatt, w_out_ref[...]).astype(BF16)


def mlp(one, att, gout, w_out, b_out, gain, shift, w_up, b_up, w_down, b_down, w_dec, b_dec, w_pix, b_pix):
    tokens, width = one.shape
    ff, dec, pix = w_up.shape[1], w_dec.shape[1], w_pix.shape[1]

    def block(size):
        return pl.BlockSpec((BLOCK, size), lambda i: (i, 0))

    def out(size, kind=BF16):
        return jax.ShapeDtypeStruct((tokens, size), kind)

    def vector(size):
        return jax.ShapeDtypeStruct((1, size), F32)

    weights = [w_out, b_out, gain, shift, w_up, b_up, w_down, b_down, w_dec, b_dec, w_pix, b_pix]
    return pl.pallas_call(
        mlp_kernel,
        grid=(tokens // BLOCK,),
        in_specs=[block(width)] * 3 + [held(item.shape) for item in weights],
        out_specs=[
            block(pix), block(width), block(ff), block(ff), block(width), block(dec), block(width),
            block(width), block(width), block(width),
            whole((1, ff)), whole((1, width)), whole((1, width)), whole((1, width)),
        ],
        out_shape=[
            out(pix), out(width), out(ff), out(ff), out(width), out(dec), out(width),
            out(width, F32), out(width), out(width),
            vector(ff), vector(width), vector(width), vector(width),
        ],
        scratch_shapes=[
            pltpu.VMEM((1, ff), F32),
            pltpu.VMEM((BLOCK, width), F32),
            pltpu.VMEM((BLOCK, width), F32),
        ],
        compiler_params=params(48),
        cost_estimate=cost(2 * tokens * width * (2 * width + 4 * ff + dec) + 2 * tokens * dec * pix, 40 << 20),
        name="mlp",
    )(one, att, gout, *weights)


def quarter_at(step, core):
    return 2 * (step % 2) + jnp.where(step < 2, 1 - core, core)


def lay_columns(ref, at, values, width):
    rows, cols = values.shape
    for i in range(cols // width):
        ref[0, at + i * rows : at + (i + 1) * rows, :] = values[:, i * width : (i + 1) * width]


def padded(rows):
    granule = 8 * lax.axis_size("col")
    return -(-rows // granule) * granule


def blank(ref, at):
    if at < ref.shape[1]:
        ref[0, at:, :] = jnp.zeros((ref.shape[1] - at, ref.shape[2]), BF16)


def pair_specs(rows, width):
    return [
        pl.BlockSpec((1, rows, width), lambda s, c: (jnp.minimum(s, 1), 0, 0)),
        pl.BlockSpec((1, rows, width), lambda s, c: (jnp.maximum(s - 2, 0), 0, 0)),
    ]


def grads_down_kernel(
    places, act_ref, gmlp_ref, decoded_ref, cot_ref, low_ref, gdec_ref, send_ref, keep_ref, lt_ref
):
    step = pl.program_id(0)

    @pl.when(step == 0)
    def _():
        lt_ref[...] = low_ref[...].T

    width = gmlp_ref.shape[1]
    part = width // 4
    rows = pl.ds(pl.multiple_of(quarter_at(step, places[0]) * part, part), part)
    down = dot_first(act_ref[...], gmlp_ref[...]).astype(BF16)
    pix = dot_first(decoded_ref[...], cot_ref[...]).astype(BF16)
    dec = dot_plain(lt_ref[rows, :], gdec_ref[...]).astype(BF16)
    at = down.shape[0] + pix.size // width
    cut, side = part * 2 // 3, dec.shape[1]
    rest = width - side
    for is_sent, ref in ((True, send_ref), (False, keep_ref)):

        @pl.when((step < 2) == is_sent)
        def _():
            ref[0, : down.shape[0], :] = down
            lay_columns(ref, down.shape[0], pix, width)
            ref[0, at : at + cut, :side] = dec[:cut]
            ref[0, at : at + part - cut, side:] = dec[cut:, :rest]
            ref[0, at + part - cut : at + cut, side:] = dec[cut:, rest:]
            blank(ref, at + cut)


def grads_down(places, act, gmlp, decoded, cot, low, gdec):
    tokens, ff = act.shape
    width, dec, pix = gmlp.shape[1], decoded.shape[1], cot.shape[1]
    rows = padded(ff // 4 + (dec // 4) * (pix // width) + dec // 4)
    return run(
        grads_down_kernel, "grads_down", (act, gmlp, decoded, cot, low, gdec),
        [jax.ShapeDtypeStruct((2, rows, width), BF16)] * 2,
        [
            pl.BlockSpec((tokens, ff // 4), lambda s, c: (0, quarter_at(s, c[0]))),
            held(gmlp.shape),
            pl.BlockSpec((tokens, dec // 4), lambda s, c: (0, quarter_at(s, c[0]))),
            held(cot.shape),
            held(low.shape),
            held(gdec.shape),
        ],
        pair_specs(rows, width), grid=(4,), places=places,
        estimate=cost(2 * tokens * (ff * width + dec * (pix + width)), 20 << 20),
        megabytes=32, scratch=[pltpu.VMEM((width, tokens), BF16)],
    )


def grads_up_kernel(
    places, normed_ref, gup_ref, att_ref, gatt_ref, send_ref, keep_ref, nt_ref, at_ref
):
    step = pl.program_id(0)

    @pl.when(step == 0)
    def _():
        nt_ref[...] = normed_ref[...].T
        at_ref[...] = att_ref[...].T

    width = normed_ref.shape[1]
    part = width // 4
    rows = pl.ds(pl.multiple_of(quarter_at(step, places[0]) * part, part), part)
    up = dot_plain(nt_ref[rows, :], gup_ref[...]).astype(BF16)
    out = dot_plain(at_ref[rows, :], gatt_ref[...]).astype(BF16)
    at = up.size // width
    for is_sent, ref in ((True, send_ref), (False, keep_ref)):

        @pl.when((step < 2) == is_sent)
        def _():
            lay_columns(ref, 0, up, width)
            ref[0, at : at + part, :] = out
            blank(ref, at + part)


def grads_up(places, normed, gup, attended, gatt, after):
    tokens, width = normed.shape
    ff = gup.shape[1]
    rows = padded(ff // 4 + width // 4)
    operands = (normed, gup, attended, gatt)
    return run(
        grads_up_kernel, "grads_up", operands, [jax.ShapeDtypeStruct((2, rows, width), BF16)] * 2,
        [held(item.shape) for item in operands], pair_specs(rows, width), grid=(4,), places=places,
        after=after, estimate=cost(2 * tokens * width * (ff + width), 16 << 20),
        scratch=[pltpu.VMEM((width, tokens), BF16)] * 2,
    )


def strip_back_kernel(dk_ref, dv_ref, w_ref, upper_ref, lower_ref, left_ref, right_ref):
    width = w_ref.shape[0]
    band, side = upper_ref.shape[0], left_ref.shape[0]
    back = (
        dot_last(dk_ref[...], w_ref[:, width : 2 * width]) + dot_last(dv_ref[...], w_ref[:, 2 * width :])
    ).astype(BF16)
    upper_ref[...] = back[:band]
    lower_ref[...] = back[band : 2 * band]
    left_ref[...] = back[2 * band : 2 * band + side]
    right_ref[...] = back[2 * band + side : 2 * (band + side)]


def strip_back(dk, dv, w, band, side, after):
    total, width = dk.shape
    sizes = (band, band, side, side)
    return run(
        strip_back_kernel, "strip_back", (dk, dv, w),
        [jax.ShapeDtypeStruct((rows, width), BF16) for rows in sizes],
        [whole(item.shape) for item in (dk, dv, w)], [whole((rows, width)) for rows in sizes],
        after=after, estimate=cost(4 * total * width * width, 8 << 20), megabytes=24,
    )


def grads_qkv_kernel(
    core_ref, normed_ref, rows_ref, dq_ref, dk_ref, dv_ref, dks_ref, dvs_ref,
    send_ref, keep_ref, nt_ref, st_ref,
):
    step = pl.program_id(0)

    @pl.when(step == 0)
    def _():
        nt_ref[...] = normed_ref[...].T
        st_ref[...] = rows_ref[...].T

    width = normed_ref.shape[1]
    part = width // 4
    rows = pl.ds(pl.multiple_of(quarter_at(step, core_ref[0]) * part, part), part)
    own, strip = nt_ref[rows, :], st_ref[rows, :]
    parts = (
        dot_plain(own, dq_ref[...]),
        dot_plain(own, dk_ref[...]) + dot_plain(strip, dks_ref[...]),
        dot_plain(own, dv_ref[...]) + dot_plain(strip, dvs_ref[...]),
    )
    for is_sent, ref in ((True, send_ref), (False, keep_ref)):

        @pl.when((step < 2) == is_sent)
        def _():
            for i, values in enumerate(parts):
                ref[0, i * part : (i + 1) * part, :] = values.astype(BF16)
            blank(ref, len(parts) * part)


def grads_qkv(places, normed, rows, dq, dk, dv, dks, dvs, after):
    tokens, width = normed.shape
    total = rows.shape[0]
    operands = (normed, rows, dq, dk, dv, dks, dvs)
    size = padded(3 * width // 4)
    return run(
        grads_qkv_kernel, "grads_qkv", operands, [jax.ShapeDtypeStruct((2, size, width), BF16)] * 2,
        [held(item.shape) for item in operands], pair_specs(size, width), grid=(4,), places=places,
        after=after, estimate=cost(2 * width * width * (3 * tokens + 2 * total), 20 << 20),
        scratch=[
            pltpu.VMEM((width, tokens), BF16),
            pltpu.VMEM((width, total), BF16),
        ],
    )


def embed_back_kernel(
    frames, stream_ref, dq_ref, dk_ref, dv_ref, w_ref, gtwo_ref, gain_ref, above_ref, below_ref, left_ref,
    right_ref, emb_ref, sum_patch, sum_gain, sum_shift, g_ref, side_ref,
):
    at_row = pl.program_id(0)
    width = stream_ref.shape[1]
    line = stream_ref.shape[0]
    tile_rows = left_ref.shape[0] // (8 * HALO)
    tile_cols = line // frames

    @pl.when(at_row == 0)
    def _():
        side_ref[0] = left_ref[...].astype(F32).reshape(side_ref.shape[1:])
        side_ref[1] = right_ref[...].astype(F32).reshape(side_ref.shape[1:])
        for ref in (sum_patch, sum_gain, sum_shift):
            ref[...] = jnp.zeros_like(ref)

    g_ref[...] = (
        dot_last(dq_ref[...], w_ref[:, :width])
        + dot_last(dk_ref[...], w_ref[:, width : 2 * width])
        + dot_last(dv_ref[...], w_ref[:, 2 * width :])
    )

    @pl.when(at_row < HALO)
    def _():
        g_ref[...] += above_ref[pl.ds(pl.multiple_of(at_row * line, line), line), :].astype(F32)

    @pl.when(at_row >= tile_rows - HALO)
    def _():
        start = (at_row - (tile_rows - HALO)) * line
        g_ref[...] += below_ref[pl.ds(pl.multiple_of(start, line), line), :].astype(F32)

    for j in range(HALO):
        source = j * tile_rows + at_row
        for f in range(frames):
            near = f * tile_cols + j
            far = near + tile_cols - HALO
            g_ref[near : near + 1, :] += side_ref[0, source, f : f + 1, :]
            g_ref[far : far + 1, :] += side_ref[1, source, f : f + 1, :]
    stream = stream_ref[...]
    grad = g_ref[...]
    centre = stream - jnp.mean(stream, -1, keepdims=True)
    inverse = lax.rsqrt(jnp.mean(centre * centre, -1, keepdims=True) + EPS)
    hat = centre * inverse
    sum_gain[...] += jnp.sum(grad * hat, 0, keepdims=True)
    sum_shift[...] += jnp.sum(grad, 0, keepdims=True)
    scaled = grad * row_of(gain_ref)
    one = gtwo_ref[...] + inverse * (
        scaled
        - jnp.mean(scaled, -1, keepdims=True)
        - hat * jnp.mean(scaled * hat, -1, keepdims=True)
    )
    sum_patch[...] += jnp.sum(one, 0, keepdims=True)
    emb_ref[...] = one.astype(BF16)


def embed_back(stream, dq, dk, dv, w, gtwo, gain, above, below, left, right, tile_rows, frames, hold):
    tokens, width = stream.shape
    line = tokens // tile_rows
    block = pl.BlockSpec((line, width), lambda r: (r, 0))
    vector = jax.ShapeDtypeStruct((1, width), F32)
    return run(
        functools.partial(embed_back_kernel, frames), "embed_back",
        (stream, dq, dk, dv, w, gtwo, gain, above, below, left, right),
        [jax.ShapeDtypeStruct((tokens, width), BF16)] + [vector] * 3,
        [
            block, block, block, block, held(w.shape), block, whole((width,)),
            whole(above.shape), whole(below.shape), whole(left.shape), whole(right.shape),
        ],
        [block] + [whole((1, width))] * 3, grid=(tile_rows,), hold=hold,
        estimate=cost(6 * tokens * width * width, 16 << 20),
        scratch=[pltpu.VMEM((line, width), F32), pltpu.VMEM((2, left.shape[0] // 8, 8, width), F32)],
    )


def lay_vectors(ref, at, vectors, quarter):
    width = ref.shape[2]
    ref[0, at:, :] = jnp.zeros((ref.shape[1] - at, width), BF16)
    lines = []
    for item in vectors:
        part = item.shape[1] // 4
        mine = jnp.zeros((1, part), F32)
        for q in range(4):
            mine = jnp.where(quarter == q, item[:, q * part : (q + 1) * part], mine)
        if part < width:
            mine = jnp.concatenate([mine, jnp.zeros((1, width - part), F32)], 1)
        lines.append(mine)
    pad = -(-len(lines) // 16) * 16 - len(lines)
    block = jnp.concatenate(lines + [jnp.zeros((pad, width), F32)], 0)
    high = block.astype(BF16)
    ref[0, at : at + block.shape[0], :] = high
    ref[0, at + block.shape[0] : at + 2 * block.shape[0], :] = (block - high.astype(F32)).astype(BF16)


def grads_patch_kernel(core_ref, pixels_ref, emb_ref, *refs):
    vectors, (send_ref, keep_ref) = refs[:-2], refs[-2:]
    step = pl.program_id(0)
    quarter = quarter_at(step, core_ref[0])
    patch = dot_first(pixels_ref[...], emb_ref[...]).astype(BF16)
    for is_sent, ref in ((True, send_ref), (False, keep_ref)):

        @pl.when((step < 2) == is_sent)
        def _():
            ref[0, : patch.shape[0], :] = patch
            lay_vectors(ref, patch.shape[0], [item[...] for item in vectors], quarter)


def grads_patch(places, pixels, emb, vectors, after):
    tokens, pix = pixels.shape
    width = emb.shape[1]
    rows = padded(pix // 4 + 64)
    return run(
        grads_patch_kernel, "grads_patch", (pixels, emb, *vectors),
        [jax.ShapeDtypeStruct((2, rows, width), BF16)] * 2,
        [
            pl.BlockSpec((tokens, pix // 4), lambda s, c: (0, quarter_at(s, c[0]))),
            held(emb.shape),
        ]
        + [whole(item.shape) for item in vectors],
        pair_specs(rows, width), grid=(4,), places=places, after=after,
        estimate=cost(2 * tokens * pix * width, 8 << 20),
    )


def pixel_back_kernel(emb_ref, w_ref, out_ref):
    out_ref[...] = dot_last(emb_ref[...], w_ref[...]).astype(BF16)


def pixel_back(emb, w, after):
    tokens, width = emb.shape
    pix = w.shape[0]
    return run(
        pixel_back_kernel, "pixel_back", (emb, w), jax.ShapeDtypeStruct((tokens, pix), BF16),
        [pl.BlockSpec((BLOCK, width), lambda i: (i, 0)), held(w.shape)],
        pl.BlockSpec((BLOCK, pix), lambda i: (i, 0)), grid=(tokens // BLOCK,), after=after,
        estimate=cost(2 * tokens * pix * width, 8 << 20),
    )


def swap(value, axis, stride):
    count = lax.axis_size(axis)
    return lax.ppermute(value, axis, [(i, i ^ stride) for i in range(count)])


def rotate(value, axis, steps):
    count = lax.axis_size(axis)
    return lax.ppermute(value, axis, [(i, (i + steps) % count) for i in range(count)])


def run(
    kernel, name, operands, out_shape, in_specs, out_specs, *, grid=(1,), places=None, after=(), hold=(),
    estimate=None, scratch=(), megabytes=28, aliases=None,
):
    scalars = () if places is None else (places,)
    count = len(scalars) + len(operands)
    extra = tuple(after) + tuple(hold)
    any_space = pl.BlockSpec(memory_space=pl.ANY)
    shapes = list(out_shape) if isinstance(out_shape, (list, tuple)) else [out_shape]
    specs = list(out_specs) if isinstance(out_specs, (list, tuple)) else [out_specs]
    own = len(shapes)

    def body(*refs):
        results = refs[count + len(extra) :]
        kernel(*refs[:count], *results[:own], *results[own + len(hold) :])

    at = count + len(after)
    aliases = dict(aliases or {})
    aliases.update({at + i: own + i for i in range(len(hold))})
    results = pl.pallas_call(
        body,
        grid_spec=pltpu.PrefetchScalarGridSpec(
            num_scalar_prefetch=len(scalars),
            grid=grid,
            in_specs=list(in_specs) + [any_space] * len(extra),
            out_specs=specs + [any_space] * len(hold),
            scratch_shapes=list(scratch),
        ),
        out_shape=shapes + [jax.ShapeDtypeStruct(item.shape, item.dtype) for item in hold],
        input_output_aliases=aliases,
        compiler_params=params(megabytes),
        cost_estimate=estimate,
        name=name,
    )(*scalars, *operands, *extra)
    return results[0] if len(results) == 1 else results


def by_rows(rows, body):
    size = next(n for n in (96, 80, 72, 64, 56, 48, 40, 32, 24, 16, 8) if rows % n == 0)

    def step(i, carry):
        body(pl.ds(pl.multiple_of(i * size, 8), size))
        return carry

    lax.fori_loop(0, rows // size, step, 0)


def add_across_kernel(places, keep_ref, came_ref, out_ref):
    def body(at):
        total = keep_ref[0, at, :].astype(F32) + came_ref[0, at, :].astype(F32)
        out_ref[at, :] = total.astype(BF16)

    by_rows(out_ref.shape[0], body)


def add_across(places, keep, came, after):
    rows, width = keep.shape[1:]
    block = pl.BlockSpec((1, rows // 2, width), lambda i, p: (1 - p[1], i, 0))
    return run(
        add_across_kernel, "add_across", (keep, came), jax.ShapeDtypeStruct((rows, width), BF16),
        [block, block], pl.BlockSpec((rows // 2, width), lambda i, p: (i, 0)),
        grid=(2,), places=places, after=after, estimate=cost(rows * width, 6 * rows * width),
        megabytes=16,
    )


def add_down_kernel(places, *refs):
    terms, outs = refs[:-2], refs[-2:]
    lead = outs[0].shape[:-2]

    for half, out_ref in enumerate(outs):

        @pl.when(pl.program_id(0) == half)
        def _():
            for i in range(lead[0] if lead else 1):

                def body(at):
                    total = sum(
                        (ref[i if lead else 0, at, :] if len(ref.shape) == 3 else ref[at, :]).astype(F32)
                        for ref in terms
                    ).astype(BF16)
                    if lead:
                        out_ref[i, at, :] = total
                    else:
                        out_ref[at, :] = total

                by_rows(out_ref.shape[-2], body)


def add_down(places, bit, terms, after, hold=()):
    shape = terms[-1].shape
    lead = shape[:-2]
    half, width = shape[-2] // 2, shape[-1]

    def which(h, p):
        return jnp.where(h == 0, 1 - p[bit], p[bit])

    same = pl.BlockSpec(lead + (half, width), lambda h, p: (0,) * len(lead) + (which(h, p), 0))
    pair = pl.BlockSpec((1, half, width), lambda h, p: (p[1], which(h, p), 0))
    out = pl.BlockSpec(lead + (half, width), lambda h, p: (0,) * len(lead) + (0, 0))
    return run(
        add_down_kernel, "add_down", terms,
        [jax.ShapeDtypeStruct(lead + (half, width), BF16)] * 2,
        [same if item.ndim == len(shape) else pair for item in terms], [out, out],
        grid=(2,), places=places, after=after, hold=hold,
        estimate=cost(half * width, 6 * half * width), megabytes=24,
    )


def add_x(places, terms, after, hold=()):
    rows, width = terms[0].shape[1:]
    block = pl.BlockSpec(
        (1, rows, width), lambda h, p: (jnp.where(h == 0, 1 - p[1], p[1]), 0, 0)
    )
    out = pl.BlockSpec((rows, width), lambda h, p: (0, 0))
    return run(
        add_down_kernel, "add_x", terms, [jax.ShapeDtypeStruct((rows, width), BF16)] * 2,
        [block] * len(terms), [out, out], grid=(2,), places=places, after=after, hold=hold,
        estimate=cost(rows * width, 6 * rows * width), megabytes=16,
    )


def add_whole_kernel(a_ref, b_ref, out_ref):
    def body(at):
        out_ref[at, :] = (a_ref[at, :].astype(F32) + b_ref[at, :].astype(F32)).astype(BF16)

    by_rows(out_ref.shape[0], body)


def add_whole(a, b, after):
    return run(
        add_whole_kernel, "add_whole", (a, b), jax.ShapeDtypeStruct(a.shape, BF16),
        [whole(a.shape)] * 2, whole(a.shape), after=after, estimate=cost(a.size, 6 * a.size),
        megabytes=16,
    )


def join_kernel(bit, places, own_ref, other_ref, out_ref):
    rows = own_ref.shape[0]
    mine = pl.multiple_of(places[bit] * rows, 8)
    theirs = pl.multiple_of((1 - places[bit]) * rows, 8)

    def body(at):
        out_ref[pl.ds(pl.multiple_of(mine + at.start, 8), at.size), :] = own_ref[at, :]
        out_ref[pl.ds(pl.multiple_of(theirs + at.start, 8), at.size), :] = other_ref[at, :]

    by_rows(rows, body)


def join(places, bit, own, other, after):
    rows, width = own.shape
    return run(
        functools.partial(join_kernel, bit), "join", (own, other),
        jax.ShapeDtypeStruct((2 * rows, width), BF16), [whole(own.shape)] * 2,
        whole((2 * rows, width)), places=places, after=after,
        estimate=cost(own.size, 8 * own.size), megabytes=16,
    )


def wide(full_ref, at, rows, cols, out_ref):
    width = full_ref.shape[1]
    for i in range(cols // width):

        def body(to):
            source = pl.ds(pl.multiple_of(at + i * rows + to.start, 8), to.size)
            out_ref[to, i * width : (i + 1) * width] = full_ref[source, :]

        by_rows(rows, body)


def finish_kernel(bit, lay_out, places, own_ref, other_ref, *refs):
    outs, full_ref = refs[:-1], refs[-1]
    rows = own_ref.shape[0]
    mine = pl.multiple_of(places[bit] * rows, 8)
    theirs = pl.multiple_of((1 - places[bit]) * rows, 8)

    def body(at):
        full_ref[pl.ds(pl.multiple_of(mine + at.start, 8), at.size), :] = own_ref[at, :].astype(F32)
        full_ref[pl.ds(pl.multiple_of(theirs + at.start, 8), at.size), :] = other_ref[at, :].astype(F32)

    by_rows(rows, body)
    lay_out(full_ref, *outs)


def finish(places, bit, own, other, lay_out, shapes, after):
    rows, width = own.shape
    return run(
        functools.partial(finish_kernel, bit, lay_out), "finish", (own, other),
        [jax.ShapeDtypeStruct(shape, F32) for shape in shapes], [whole(own.shape)] * 2,
        [whole(shape) for shape in shapes], places=places, after=after,
        estimate=cost(own.size, 16 * own.size), megabytes=16, scratch=[pltpu.VMEM((2 * rows, width), F32)],
    )


class Reduction:
    def __init__(self, order, places, pair, lay_out, shapes, late_x=False):
        self.send, self.keep = pair
        self.order, self.places = order, places
        self.lay_out, self.shapes = lay_out, shapes
        last = lax.axis_size("col").bit_length() - 2
        self.steps = [("down", i) for i in range(last)]
        if late_x:
            self.steps += [("down", last), ("x", 0), ("up", last)]
        else:
            self.steps = [("across", 0)] + self.steps + [("full", last)]
        self.steps += [("up", i) for i in reversed(range(last))] + [("end", 0)]
        self.pending = (None, 0)
        self.sent = self.result = None

    def after(self):
        return (self.order[-1].sent,) if self.order and self.order[-1] is not self else ()

    def terms(self):
        kind, bit = self.pending
        if kind is None:
            self.came = swap(self.send, "row", 1)
            return self.keep, self.came
        if kind == "across":
            return self.keep, self.came, swap(self.sent, "row", 2)
        if kind == "x":
            return self.mine, swap(self.sent, "row", 2)
        return self.mine, swap(self.sent, "col", 1 << bit)

    def advance(self, then=None):
        kind, bit = self.steps.pop(0)
        places, after = self.places, self.after()
        terms = self.terms()
        hold = () if then is None else (then.send,)
        kept = ()
        if kind == "across":
            self.sent = add_across(places, *terms, after)
        elif kind == "down":
            self.sent, self.mine, *kept = add_down(places, 2 + bit, terms, after, hold)
        elif kind == "x":
            self.sent, self.mine, *kept = add_x(places, terms, after, hold)
        elif kind == "end":
            result = finish(places, 2 + self.pending[1], *terms, self.lay_out, self.shapes, after)
            self.result = result if isinstance(result, (list, tuple)) else [result]
            self.sent = self.result[0]
        elif self.pending[0] == "up":
            self.sent = self.mine = join(places, 2 + self.pending[1], *terms, after)
        else:
            self.sent = self.mine = add_whole(*terms, after)
        if kept:
            (then.send,) = kept
        self.pending = (kind, bit)
        self.order.append(self)


class Ready:
    def __init__(self, value):
        self.sent = value


def wave_numbers(width):
    def of(part):
        half = part // 2
        one = np.float32(1.0) / np.float32(10000.0) ** (
            np.arange(half, dtype=np.float32) / np.float32(half)
        )
        return [one, one]

    unit = width // 16
    return np.concatenate(of(4 * unit) + of(6 * unit) + of(6 * unit)).astype(np.float32)[None, :]


def per_device(
    pixels, timestamps, frame_count, visible, halo_reach, w_patch, b_patch, gain_one, shift_one,
    w_qkv, b_query, b_value, w_out, b_out, gain_two, shift_two, w_up, b_up, w_down, b_down,
    w_dec, b_dec, w_pix, b_pix, cotangent,
):
    tile_rows, tile_cols, frames, pix_width = pixels.shape
    model_width = w_patch.shape[1]
    tokens = tile_rows * tile_cols * frames
    ff = w_up.shape[1]
    grid_shape = (tile_rows, frames, tile_cols)
    side = tile_rows * 8 * HALO
    band = HALO * frames * tile_cols
    row_at, col_at = lax.axis_index("row"), lax.axis_index("col")
    col_bits = lax.axis_size("col").bit_length() - 1
    places = jnp.stack(
        [row_at % 2, row_at // 2] + [(col_at >> i) % 2 for i in range(col_bits)]
    ).astype(jnp.int32)

    flat_pixels = pixels.transpose(0, 2, 1, 3).reshape(tokens, pix_width)
    flat_cotangent = cotangent.transpose(0, 2, 1, 3).reshape(tokens, pix_width)
    stream_one, normed_one, high, low, tail, head, flags = embed(
        timestamps.reshape(-1), frame_count.reshape(-1), visible.transpose(2, 0, 1), flat_pixels,
        w_patch, b_patch, gain_one, shift_one, wave_numbers(model_width),
    )
    upper = rotate(high, "row", 1)
    lower = rotate(low, "row", -1)
    left = rotate(tail, "col", 1)
    right = rotate(head, "col", -1)
    query, key, value = own_qkv(normed_one, w_qkv, b_query, b_value)
    grad_dec, grad_stream, grad_mlp, sum_pix, sum_dec, sum_down = decode_back(
        flat_cotangent, w_pix, w_dec
    )
    strip_key, strip_value, strip_rows, bias = strip_kv(
        halo_reach.reshape(-1), upper, lower, left, right, flags, w_qkv, b_value
    )
    mixed, log_total = attend(query, key, value, strip_key, strip_value, bias)
    (
        pixel_out, normed_two, act, grad_pre, stream_low, decoded, attended,
        grad_two, grad_att, grad_attended, sum_up, sum_out, sum_gain_two, sum_shift_two,
    ) = mlp(
        stream_one, mixed, grad_stream, w_out, b_out, gain_two, shift_two,
        w_up, b_up, w_down, b_down, w_dec, b_dec, w_pix, b_pix,
    )
    fixed = (query, key, value, strip_key, strip_value)
    rest = (mixed, log_total, bias)
    pairs = model_width // LANES
    third = pairs // 3
    quarter = model_width // 4
    patch_rows, down_rows = pix_width // 4, ff // 4
    pix_rows, up_rows = w_dec.shape[1] // 4, quarter * (ff // model_width)
    dec_width = w_dec.shape[1]
    cut = quarter * 2 // 3
    order = []

    def lay_down(full, down_ref, pix_ref, dec_ref):
        wide(full, 0, down_rows, model_width, down_ref)
        wide(full, down_rows, pix_rows, pix_width, pix_ref)
        at, tall = down_rows + pix_rows * (pix_width // model_width), quarter - cut
        dec_ref[:cut, :] = full[at : at + cut, :dec_width]
        dec_ref[cut:, : model_width - dec_width] = full[at : at + tall, dec_width:]
        dec_ref[cut:, model_width - dec_width :] = full[at + tall : at + cut, dec_width:]

    def lay_up(full, up_ref, out_ref):
        wide(full, 0, quarter, ff, up_ref)
        wide(full, up_rows, quarter, model_width, out_ref)

    def lay_middle(full, qkv_ref):
        wide(full, 0, quarter, 3 * model_width, qkv_ref)

    def lay_last(full, patch_ref, *refs):
        wide(full, 0, patch_rows, model_width, patch_ref)
        lines = -(-len(refs) // 16) * 16
        for i, ref in enumerate(refs):
            at = patch_rows + i
            size = ref.shape[1]
            ref[...] = full[at : at + 1, :size] + full[at + lines : at + lines + 1, :size]

    down = Reduction(
        order, places,
        grads_down(places, act, grad_mlp, decoded, flat_cotangent, stream_low, grad_dec), lay_down,
        [(down_rows, model_width), (pix_rows, pix_width), (quarter, dec_width)], late_x=True,
    )
    up = Reduction(
        order, places, grads_up(places, normed_two, grad_pre, attended, grad_att, (down.keep,)),
        lay_up, [(quarter, ff), (quarter, model_width)],
    )
    down.advance()
    up.advance()
    most = pairs * 2 // 3
    back = attend_back(*fixed, grad_attended, *rest, 0, most, (), (down.sent, up.sent))
    order.append(Ready(back[0]))
    down.advance()
    up.advance()
    back = attend_back(
        *fixed, grad_attended, *rest, most, pairs - most, back, (up.sent, down.sent)
    )
    dq, dk, dv, dks, dvs, sum_query, sum_value = back
    order.append(Ready(dq))
    down.advance()
    up.advance()
    upper_back, lower_back, left_back, right_back = strip_back(
        dks, dvs, w_qkv, band, side, (up.sent,)
    )
    from_right = rotate(left_back, "col", -1)
    from_left = rotate(right_back, "col", 1)
    from_below = rotate(upper_back, "row", -1)
    from_above = rotate(lower_back, "row", 1)
    middle = Reduction(
        order, places,
        grads_qkv(places, normed_one, strip_rows, dq, dk, dv, dks, dvs, (upper_back,)),
        lay_middle, [(quarter, 3 * model_width)],
    )
    grad_emb, sum_patch, sum_gain_one, sum_shift_one, up.sent = embed_back(
        stream_one, dq, dk, dv, w_qkv, grad_two, gain_one, from_above,
        from_below, from_left, from_right, tile_rows, frames, (up.sent,),
    )
    vectors = [
        sum_patch, sum_gain_one, sum_shift_one, sum_query, sum_value, sum_out, sum_gain_two,
        sum_shift_two, sum_up, sum_down, sum_dec, sum_pix,
    ]
    order.append(Ready(grad_emb))
    down.advance(middle)
    last = Reduction(
        order, places, grads_patch(places, flat_pixels, grad_emb, vectors, (down.sent,)),
        lay_last, [(patch_rows, model_width)] + [(1, item.shape[1] // 4) for item in vectors],
    )
    groups = {"d": down, "u": up, "m": middle, "l": last}
    for turn in EVENTS:
        if turn == "p":
            pixel_grad = pixel_back(grad_emb, w_patch, (order[-1].sent,))
            order.append(Ready(pixel_grad))
        elif groups[turn].steps:
            groups[turn].advance()
    while any(each.steps for each in groups.values()):
        for each in groups.values():
            if each.steps:
                each.advance()
    share_down, share_pix, share_dec = down.result
    share_up, share_out = up.result
    (share_qkv,) = middle.result
    share_patch, *pieces = last.result
    pieces = [item.reshape(-1) for item in pieces]

    def to_scene(flat):
        return flat.reshape(grid_shape + (pix_width,)).transpose(0, 2, 1, 3)

    return (
        to_scene(pixel_out), to_scene(pixel_grad), share_patch, pieces[0], pieces[1], pieces[2],
        share_qkv, pieces[3], pieces[4], share_out, pieces[5], pieces[6], pieces[7], share_up,
        pieces[8], share_down, pieces[9], share_dec, pieces[10], share_pix, pieces[11],
    )


def solution(mesh):
    tiles = P("row", "col", None, None)
    return jax.shard_map(
        per_device,
        mesh=mesh,
        in_specs=(
            tiles,
            P("row", "col", None),
            P("row", "col"),
            P("row", "col", None),
            P("row", "col"),
        )
        + (P(),) * 19
        + (tiles,),
        out_specs=(
            tiles,
            tiles,
            P("row", None),
            P("row"),
            P("row"),
            P("row"),
            P("row", None),
            P("row"),
            P("row"),
            P("row", None),
            P("row"),
            P("row"),
            P("row"),
            P("row", None),
            P("row"),
            P("row", None),
            P("row"),
            P("row", None),
            P("row"),
            P("row", None),
            P("row"),
        ),
        check_vma=False,
    )
```

```python
import functools
import math

import jax
import jax.numpy as jnp
import numpy as np
from jax import lax
from jax.experimental import pallas as pl
from jax.experimental.pallas import tpu as pltpu
from jax.sharding import PartitionSpec as P

HEAD_WIDTH = 64
HALO = 2
EPS = 1e-06
NEG_FILL = -1e30
BLOCK = 256
LANES = 128
KEY_BLOCK = 512
FF_BLOCK = 1024
EVENTS = "mldumulmulmdmudlmlpdlml"
SCALE = HEAD_WIDTH**-0.5
LOG_SCALE = SCALE * math.log2(math.e)
F32 = jnp.float32
BF16 = jnp.bfloat16


def dot_last(a, b):
    return lax.dot_general(a, b, (((1,), (1,)), ((), ())), preferred_element_type=F32)


def dot_plain(a, b):
    return lax.dot_general(a, b, (((1,), (0,)), ((), ())), preferred_element_type=F32)


def one_head(pair, head):
    lane = lax.broadcasted_iota(jnp.int32, pair.shape, 1)
    keep = (lane < HEAD_WIDTH) if head == 0 else (lane >= HEAD_WIDTH)
    return jnp.where(keep, pair, jnp.zeros_like(pair))


def diagonal(size):
    rows = lax.broadcasted_iota(jnp.int32, (size, size), 0)
    return rows == lax.broadcasted_iota(jnp.int32, (size, size), 1)


def row_of(ref):
    return ref[...].astype(F32).reshape(1, -1)


def params(megabytes):
    return pltpu.CompilerParams(vmem_limit_bytes=megabytes << 20)


def cost(flops, moved):
    return pl.CostEstimate(flops=flops, bytes_accessed=moved, transcendentals=0)


def whole(shape):
    return pl.BlockSpec(shape, lambda *_: (0,) * len(shape))


def held(shape):
    return pl.BlockSpec(shape, lambda *_: (0,) * len(shape), pipeline_mode=pl.Buffered(1))


def embed_kernel(
    stamps_ref,
    count_ref,
    visible_ref,
    pixels_ref,
    w_ref,
    b_ref,
    gain_ref,
    shift_ref,
    wave_ref,
    stream_ref,
    normed_ref,
    high_ref,
    low_ref,
    tail_ref,
    head_ref,
    flags_ref,
    edge_ref,
    time_ref,
    col_ref,
    n_ref,
):
    at_row = pl.program_id(0)
    width = w_ref.shape[1]
    frames, tile_rows, tile_cols = visible_ref.shape
    line = frames * tile_cols
    band = HALO * line

    lane = lax.broadcasted_iota(jnp.int32, (1, width), 1)
    t_end, r_end = width // 4, width // 4 + width * 3 // 8
    t_mid, r_mid, c_mid = width // 8, t_end + width * 3 // 16, r_end + width * 3 // 16

    def waves(places):
        angles = places * wave_ref[...]
        is_sin = (lane < t_mid) | ((lane >= t_end) & (lane < r_mid)) | ((lane >= r_end) & (lane < c_mid))
        return jnp.where(is_sin, jnp.sin(angles), jnp.cos(angles))

    @pl.when(at_row == 0)
    def _():
        slot = lax.broadcasted_iota(jnp.int32, (8, 1), 0)
        stamps = jnp.zeros((8, 1), F32)
        for f in range(frames):
            stamps = jnp.where(slot == f, stamps_ref[f].astype(F32), stamps)
        time_ref[...] = jnp.where(lane < t_end, waves(stamps), 0.0)
        cols = lax.axis_index("col") * tile_cols + lax.broadcasted_iota(
            jnp.int32, (tile_cols, 1), 0
        )
        col_ref[...] = jnp.where(lane >= r_end, waves(cols.astype(F32)), 0.0)
        frame_at = lax.broadcasted_iota(jnp.int32, visible_ref.shape, 0)
        ok = ((frame_at < count_ref[0]) & (visible_ref[...] == 1)).astype(F32)
        pieces = [ok[f, r : r + 1, :] for r in range(tile_rows) for f in range(frames)]
        flat = jnp.concatenate(pieces, 1)
        flags_ref[...] = jnp.broadcast_to(flat, flags_ref.shape)
        edge_ref[...] = jnp.zeros_like(edge_ref)
        nothing = [jnp.zeros((8 - frames, tile_cols), F32)]
        stacked = jnp.concatenate(
            sum((pieces[r * frames : (r + 1) * frames] + nothing for r in range(tile_rows)), []), 0
        )
        slot = lax.broadcasted_iota(jnp.int32, (8, tile_cols), 0)
        col = lax.broadcasted_iota(jnp.int32, (8, tile_cols), 1)
        last = HALO * tile_rows
        chunk = 8 * tile_rows
        edge_ref[0, last, :, :chunk] = dot_last(
            (col == slot + tile_cols - HALO).astype(F32), stacked
        )
        edge_ref[1, last, :, :chunk] = dot_last((col == slot).astype(F32), stacked)

    places = (lax.axis_index("row") * tile_rows + at_row).astype(F32)
    row_part = jnp.where((lane >= t_end) & (lane < r_end), waves(jnp.full((1, 1), places)), 0.0)
    base = row_of(b_ref) + row_part
    stream = dot_plain(pixels_ref[...], w_ref[...])
    position = jnp.concatenate(
        [col_ref[...] + (time_ref[f : f + 1, :] + base) for f in range(frames)], 0
    )
    stream = stream + position
    stream_ref[...] = stream
    centre = stream - jnp.mean(stream, -1, keepdims=True)
    spread = jnp.mean(centre * centre, -1, keepdims=True)
    normed = centre * lax.rsqrt(spread + EPS) * row_of(gain_ref) + row_of(shift_ref)
    low = normed.astype(BF16)
    normed_ref[...] = low
    n_ref[...] = low.astype(F32)
    for j in range(HALO):
        target = j * tile_rows + at_row
        for f in range(frames):
            near = f * tile_cols + j
            far = near + tile_cols - HALO
            edge_ref[0, target, f : f + 1, :] = n_ref[far : far + 1, :]
            edge_ref[1, target, f : f + 1, :] = n_ref[near : near + 1, :]

    @pl.when(at_row < HALO)
    def _():
        low_ref[pl.ds(pl.multiple_of(at_row * line, line), line), :] = low

    @pl.when(at_row >= tile_rows - HALO)
    def _():
        start = (at_row - (tile_rows - HALO)) * line
        high_ref[pl.ds(pl.multiple_of(start, line), line), :] = low

    @pl.when(at_row == tile_rows - 1)
    def _():
        tail_ref[...] = edge_ref[0].reshape(tail_ref.shape).astype(BF16)
        head_ref[...] = edge_ref[1].reshape(head_ref.shape).astype(BF16)
        zeros = jnp.zeros((8, width - band), BF16)
        total = flags_ref.shape[1]
        low_ref[band : band + 8, :band] = flags_ref[:, :band].astype(BF16)
        low_ref[band : band + 8, band:] = zeros
        high_ref[band : band + 8, :band] = flags_ref[:, total - band :].astype(BF16)
        high_ref[band : band + 8, band:] = zeros


def embed(stamps, count, visible, pixels, w, b, gain, shift, wave):
    tokens, depth = pixels.shape
    width = w.shape[1]
    frames, tile_rows, tile_cols = visible.shape
    line = frames * tile_cols
    band = HALO * line
    side = HALO * tile_rows * 8
    smem = pl.BlockSpec(memory_space=pltpu.SMEM)
    block = pl.BlockSpec((line, width), lambda r: (r, 0))
    return pl.pallas_call(
        embed_kernel,
        grid=(tile_rows,),
        in_specs=[
            smem,
            smem,
            whole(visible.shape),
            pl.BlockSpec((line, depth), lambda r: (r, 0)),
            held(w.shape),
            whole((width,)),
            whole((width,)),
            whole((width,)),
            whole((1, width)),
        ],
        out_specs=[
            block,
            block,
            whole((band + 8, width)),
            whole((band + 8, width)),
            whole((side + 8, width)),
            whole((side + 8, width)),
            whole((8, tokens)),
        ],
        out_shape=[
            jax.ShapeDtypeStruct((tokens, width), F32),
            jax.ShapeDtypeStruct((tokens, width), BF16),
            jax.ShapeDtypeStruct((band + 8, width), BF16),
            jax.ShapeDtypeStruct((band + 8, width), BF16),
            jax.ShapeDtypeStruct((side + 8, width), BF16),
            jax.ShapeDtypeStruct((side + 8, width), BF16),
            jax.ShapeDtypeStruct((8, tokens), F32),
        ],
        scratch_shapes=[
            pltpu.VMEM((2, side // 8 + 1, 8, width), F32),
            pltpu.VMEM((8, width), F32),
            pltpu.VMEM((tile_cols, width), F32),
            pltpu.VMEM((line, width), F32),
        ],
        compiler_params=params(60),
        cost_estimate=cost(2 * tokens * depth * width, 10 << 20),
        name="embed",
    )(stamps, count, visible, pixels, w, b, gain, shift, wave)


def decode_back_kernel(
    cot_ref, w_pix_ref, w_dec_ref, dec_ref, out_ref, mlp_ref, sum_pix, sum_dec, sum_down
):
    @pl.when(pl.program_id(0) == 0)
    def _():
        sum_pix[...] = jnp.zeros_like(sum_pix)
        sum_dec[...] = jnp.zeros_like(sum_dec)
        sum_down[...] = jnp.zeros_like(sum_down)

    grad_dec = dot_last(cot_ref[...], w_pix_ref[...]).astype(BF16)
    dec_ref[...] = grad_dec
    grad_out = dot_last(grad_dec, w_dec_ref[...])
    out_ref[...] = grad_out
    low = grad_out.astype(BF16)
    mlp_ref[...] = low
    sum_pix[...] += jnp.sum(cot_ref[...].astype(F32), 0, keepdims=True)
    sum_dec[...] += jnp.sum(grad_dec.astype(F32), 0, keepdims=True)
    sum_down[...] += jnp.sum(low.astype(F32), 0, keepdims=True)


def decode_back(cot, w_pix, w_dec):
    tokens, pix = cot.shape
    width, dec = w_dec.shape

    def block(size):
        return pl.BlockSpec((BLOCK, size), lambda i: (i, 0))

    return pl.pallas_call(
        decode_back_kernel,
        grid=(tokens // BLOCK,),
        in_specs=[block(pix), held(w_pix.shape), held(w_dec.shape)],
        out_specs=[
            block(dec),
            block(width),
            block(width),
            whole((1, pix)),
            whole((1, dec)),
            whole((1, width)),
        ],
        out_shape=[
            jax.ShapeDtypeStruct((tokens, dec), BF16),
            jax.ShapeDtypeStruct((tokens, width), F32),
            jax.ShapeDtypeStruct((tokens, width), BF16),
            jax.ShapeDtypeStruct((1, pix), F32),
            jax.ShapeDtypeStruct((1, dec), F32),
            jax.ShapeDtypeStruct((1, width), F32),
        ],
        compiler_params=params(16),
        cost_estimate=cost(2 * tokens * dec * (pix + width), 10 << 20),
        name="decode_back",
    )(cot, w_pix, w_dec)


def own_qkv_kernel(x_ref, w_ref, bq_ref, bv_ref, q_ref, k_ref, v_ref):
    width = x_ref.shape[1]
    x = x_ref[...]
    q_ref[...] = (dot_plain(x, w_ref[:, :width]) + row_of(bq_ref)).astype(BF16)
    k_ref[...] = dot_plain(x, w_ref[:, width : 2 * width]).astype(BF16)
    v_ref[...] = (dot_plain(x, w_ref[:, 2 * width :]) + row_of(bv_ref)).astype(BF16)


def own_qkv(x, w, bq, bv):
    tokens, width = x.shape
    block = pl.BlockSpec((BLOCK, width), lambda i: (i, 0))
    return pl.pallas_call(
        own_qkv_kernel,
        grid=(tokens // BLOCK,),
        in_specs=[block, held(w.shape), whole((width,)), whole((width,))],
        out_specs=[block] * 3,
        out_shape=[jax.ShapeDtypeStruct((tokens, width), BF16)] * 3,
        compiler_params=params(16),
        cost_estimate=cost(6 * tokens * width * width, 8 << 20),
        name="own_qkv",
    )(x, w, bq, bv)


def strip_kv_kernel(
    reach_ref, upper_ref, lower_ref, left_ref, right_ref, flags_ref, w_ref, bv_ref,
    k_ref, v_ref, rows_ref, bias_ref,
):
    band = upper_ref.shape[0] - 8
    side = left_ref.shape[0] - 8
    tokens = flags_ref.shape[1]
    total = rows_ref.shape[0]
    at = pl.program_id(0)

    @pl.when(at == 0)
    def _():
        rows_ref[:band, :] = upper_ref[:band, :]
        rows_ref[band : 2 * band, :] = lower_ref[:band, :]
        rows_ref[2 * band : 2 * band + side, :] = left_ref[:side, :]
        rows_ref[2 * band + side : 2 * (band + side), :] = right_ref[:side, :]
        if total > 2 * (band + side):
            rows_ref[2 * (band + side) :, :] = jnp.zeros(
                (total - 2 * (band + side), rows_ref.shape[1]), BF16
            )
        reach = reach_ref[0]
        line = band // HALO
        where = lax.broadcasted_iota(jnp.int32, (1, band), 1) // line
        near = (reach >= where + 1).astype(F32)
        far = (reach >= HALO - where).astype(F32)
        upper_ok = upper_ref[band : band + 1, :band].astype(F32) * far
        lower_ok = lower_ref[band : band + 1, :band].astype(F32) * near
        chunk = side // HALO
        spare = total - 2 * band
        source = lax.broadcasted_iota(jnp.int32, (LANES, spare), 0)
        target = lax.broadcasted_iota(jnp.int32, (LANES, spare), 1)
        sides = jnp.zeros((8, spare), F32)
        for j in range(HALO):
            for part, ref, need in ((0, left_ref, HALO - j), (1, right_ref, j + 1)):
                place = (target == source + part * side + j * chunk) & (source < chunk)
                line_ok = jnp.broadcast_to(
                    ref[side : side + 8, :LANES].astype(F32)[j : j + 1], (8, LANES)
                )
                moved = dot_plain(line_ok.astype(BF16), place.astype(BF16))
                sides = sides + jnp.where(reach >= need, moved, 0.0)
        bias_ref[:, :tokens] = jnp.where(flags_ref[...] > 0.5, 0.0, NEG_FILL)
        bias_ref[:, tokens : tokens + band] = jnp.broadcast_to(
            jnp.where(upper_ok > 0.5, 0.0, NEG_FILL), (8, band)
        )
        bias_ref[:, tokens + band : tokens + 2 * band] = jnp.broadcast_to(
            jnp.where(lower_ok > 0.5, 0.0, NEG_FILL), (8, band)
        )
        bias_ref[:, tokens + 2 * band :] = jnp.where(sides > 0.5, 0.0, NEG_FILL)
        k_ref[...] = dot_plain(rows_ref[...], w_ref[...]).astype(BF16)

    @pl.when(at == 1)
    def _():
        v_ref[...] = (dot_plain(rows_ref[...], w_ref[...]) + row_of(bv_ref)).astype(BF16)


def strip_kv(reach, upper, lower, left, right, flags, w, bv):
    width = w.shape[0]
    tokens = flags.shape[1]
    keys = 2 * (upper.shape[0] - 8) + 2 * (left.shape[0] - 8)
    total = -(-(tokens + keys) // LANES) * LANES - tokens
    strip = jax.ShapeDtypeStruct((total, width), BF16)
    return pl.pallas_call(
        strip_kv_kernel,
        grid=(2,),
        in_specs=[
            pl.BlockSpec(memory_space=pltpu.SMEM),
            whole(upper.shape),
            whole(lower.shape),
            whole(left.shape),
            whole(right.shape),
            whole(flags.shape),
            pl.BlockSpec((width, width), lambda i: (0, i + 1)),
            whole((width,)),
        ],
        out_specs=[whole((total, width))] * 3 + [whole((8, tokens + total))],
        out_shape=[strip] * 3 + [jax.ShapeDtypeStruct((8, tokens + total), F32)],
        compiler_params=params(16),
        cost_estimate=cost(4 * total * width * width, 8 << 20),
        name="strip_kv",
    )(reach, upper, lower, left, right, flags, w, bv)


def attend_kernel(
    q_ref, k_ref, v_ref, ks_ref, vs_ref, bias_ref, out_ref, log_ref, s_ref, keys_ref, values_ref, own_ref
):
    tokens = q_ref.shape[0]
    keys = keys_ref.shape[0]
    keys_ref[:tokens, :] = k_ref[...]
    keys_ref[tokens:, :] = ks_ref[...]
    for ref, rows in ((v_ref, slice(0, tokens)), (vs_ref, slice(tokens, keys))):
        values = ref[...]
        lane = lax.broadcasted_iota(jnp.int32, values.shape, 1)
        values_ref[0, rows, :] = jnp.where(lane < HEAD_WIDTH, values, jnp.ones_like(values))
        values_ref[1, rows, :] = jnp.where(lane >= HEAD_WIDTH, values, jnp.ones_like(values))

    @pl.when(pl.program_id(0) == 0)
    def _():
        own_ref[...] = bias_ref[:, :tokens].T[:, 0:1]

    block = tokens // 2
    lane = lax.broadcasted_iota(jnp.int32, (block, LANES), 1)
    spans = [(at, min(KEY_BLOCK, keys - at)) for at in range(0, keys, KEY_BLOCK)]
    units = [(at, head) for at in range(0, tokens, block) for head in range(2)]

    def query(unit):
        at, head = unit
        return one_head(q_ref[at : at + block, :], head)

    def score(q_head, span, slot, top):
        at, size = span
        scores = dot_last(q_head, keys_ref[at : at + size, :]) + bias_ref[0:1, at : at + size]
        s_ref[slot, :, at : at + size] = scores
        for part in range(0, size, LANES):
            piece = scores[:, part : part + LANES]
            top = piece if top is None else jnp.maximum(top, piece)
        return top

    def own_term(unit, q_head, top):
        at = unit[0]
        own_keys = keys_ref[at : at + block, :].astype(F32)
        score_own = jnp.sum(q_head.astype(F32) * own_keys, 1, keepdims=True)
        score_own = jnp.where(own_ref[at : at + block, :] < 0, score_own, NEG_FILL)
        top = jnp.maximum(jnp.max(top, 1, keepdims=True), score_own) * LOG_SCALE
        return top, jnp.exp2(score_own * LOG_SCALE - top).astype(BF16).astype(F32)

    def weigh(unit, span, slot, top, mixed):
        at, size = span
        weights = jnp.exp2(s_ref[slot, :, at : at + size] * LOG_SCALE - top).astype(BF16)
        part = dot_plain(weights, values_ref[unit[1], at : at + size, :])
        return part if mixed is None else mixed + part

    q_head, best = query(units[0]), None
    for span in spans:
        best = score(q_head, span, 0, best)
    top, own = own_term(units[0], q_head, best)
    first = None
    for number, unit in enumerate(units):
        at, head = unit
        follows = units[number + 1] if number + 1 < len(units) else None
        q_head = query(follows) if follows else None
        best = mixed = None
        for span in spans:
            if follows:
                best = score(q_head, span, (number + 1) % 2, best)
            mixed = weigh(unit, span, number % 2, top, mixed)
        mixed = mixed + own * values_ref[head, at : at + block, :].astype(F32)
        total = mixed[:, HEAD_WIDTH : HEAD_WIDTH + 1] if head == 0 else mixed[:, 0:1]
        log_ref[0, head, at : at + block] = (top + jnp.log2(total))[:, 0]
        if head == 0:
            first = mixed / total
        else:
            out_ref[at : at + block, :] = jnp.where(lane < HEAD_WIDTH, first, mixed / total)
        if follows:
            top, own = own_term(follows, q_head, best)


def attend(q, k, v, ks, vs, bias):
    tokens, width = q.shape
    keys = tokens + ks.shape[0]
    pairs = width // LANES
    own = pl.BlockSpec((tokens, LANES), lambda p: (0, p))
    strip = pl.BlockSpec((keys - tokens, LANES), lambda p: (0, p))
    return pl.pallas_call(
        attend_kernel,
        grid=(pairs,),
        in_specs=[own, own, own, strip, strip, whole((8, keys))],
        out_specs=[own, pl.BlockSpec((1, 2, tokens), lambda p: (p, 0, 0))],
        out_shape=[
            jax.ShapeDtypeStruct((tokens, width), F32),
            jax.ShapeDtypeStruct((pairs, 2, tokens), F32),
        ],
        scratch_shapes=[
            pltpu.VMEM((2, tokens // 2, keys), F32),
            pltpu.VMEM((keys, LANES), BF16),
            pltpu.VMEM((2, keys, LANES), BF16),
            pltpu.VMEM((tokens, 1), F32),
        ],
        compiler_params=params(24),
        cost_estimate=cost(16 * tokens * keys * width, 8 << 20),
        name="attend",
    )(q, k, v, ks, vs, bias)


def attend_back_kernel(
    q_ref, k_ref, v_ref, ks_ref, vs_ref, do_ref, o_ref, log_ref, bias_ref,
    dq_ref, dk_ref, dv_ref, dks_ref, dvs_ref, sum_q, sum_v,
    keys_ref, values_ref, kt_ref, mask_ref,
):
    tokens = q_ref.shape[0]
    keys_ref[:tokens, :] = k_ref[...]
    keys_ref[tokens:, :] = ks_ref[...]
    values_ref[:tokens, :] = v_ref[...]
    values_ref[tokens:, :] = vs_ref[...]
    kt_ref[...] = keys_ref[...].T

    @pl.when(pl.program_id(0) == 0)
    def _():
        mask_ref[...] = bias_ref[...].T[:, 0:1]

    q, do = q_ref[...], do_ref[...]
    wide_q, wide_do, wide_k = q.astype(F32), do.astype(F32), k_ref[...].astype(F32)
    with_out = (wide_do * o_ref[...]).T
    with_key = (wide_q * wide_k).T
    with_value = (wide_do * v_ref[...].astype(F32)).T
    hidden = bias_ref[0:1, :tokens] < 0
    dk = dv = None
    dq, own_weights, own_grads = [], [], []
    for head in range(2):
        part = slice(head * HEAD_WIDTH, (head + 1) * HEAD_WIDTH)
        delta = jnp.sum(with_out[part], axis=0, keepdims=True)
        log_total = log_ref[0, head : head + 1, :]
        own = jnp.sum(with_key[part], axis=0, keepdims=True) * LOG_SCALE - log_total
        own = jnp.where(hidden, jnp.exp2(jnp.where(hidden, own, 0.0)), 0.0)
        own_grad = own * (jnp.sum(with_value[part], axis=0, keepdims=True) - delta)
        own_weights.append(own.astype(BF16).astype(F32))
        own_grads.append(own_grad.astype(BF16).astype(F32))
        q_head = one_head(q, head)
        do_head = one_head(do, head)
        scores = dot_last(keys_ref[...], q_head) + mask_ref[...]
        weights = jnp.exp2(scores * LOG_SCALE - log_total)
        back = dot_last(values_ref[...], do_head)
        grad = (weights * (back - delta)).astype(BF16)
        dv_part = dot_plain(weights.astype(BF16), do_head)
        dk_part = dot_plain(grad, q_head)
        dv = dv_part if dv is None else dv + dv_part
        dk = dk_part if dk is None else dk + dk_part
        dq.append(dot_plain(kt_ref[...], grad))

    def per_lane(rows):
        return jnp.concatenate([jnp.broadcast_to(row, (HEAD_WIDTH, tokens)) for row in rows], 0).T

    own, own_grad = per_lane(own_weights), per_lane(own_grads)
    dv_own = (dv[:tokens] + own * wide_do).astype(BF16)
    dv_strip = dv[tokens:].astype(BF16)
    dv_ref[...] = dv_own
    dvs_ref[...] = dv_strip
    dk_ref[...] = ((dk[:tokens] + own_grad * wide_q) * SCALE).astype(BF16)
    dks_ref[...] = (dk[tokens:] * SCALE).astype(BF16)
    joined = jnp.concatenate([dq[0][:HEAD_WIDTH], dq[1][HEAD_WIDTH:]], axis=0).T
    low = ((joined + own_grad * wide_k) * SCALE).astype(BF16)
    dq_ref[...] = low
    sum_q[...] = jnp.sum(low.astype(F32), 0, keepdims=True)
    sum_v[...] = jnp.sum(dv_own.astype(F32), 0, keepdims=True) + jnp.sum(
        dv_strip.astype(F32), 0, keepdims=True
    )


def attend_back(q, k, v, ks, vs, do, o, log_total, bias, first, count, before, after):
    tokens, width = q.shape
    keys = tokens + ks.shape[0]
    own = pl.BlockSpec((tokens, LANES), lambda p: (0, p + first))
    strip = pl.BlockSpec((keys - tokens, LANES), lambda p: (0, p + first))
    line = pl.BlockSpec((1, LANES), lambda p: (0, p + first))
    return run(
        attend_back_kernel, "attend_back", (q, k, v, ks, vs, do, o, log_total, bias),
        [jax.ShapeDtypeStruct((tokens, width), BF16)] * 3
        + [jax.ShapeDtypeStruct((keys - tokens, width), BF16)] * 2
        + [jax.ShapeDtypeStruct((1, width), F32)] * 2,
        [
            own, own, own, strip, strip, own, own,
            pl.BlockSpec((1, 2, tokens), lambda p: (p + first, 0, 0)),
            whole((8, keys)),
        ],
        [own, own, own, strip, strip, line, line], grid=(count,), after=tuple(before) + tuple(after),
        aliases={9 + i: i for i in range(len(before))},
        estimate=cost(24 * tokens * keys * LANES * count, 3 * count << 20), megabytes=40,
        scratch=[
            pltpu.VMEM((keys, LANES), BF16),
            pltpu.VMEM((keys, LANES), BF16),
            pltpu.VMEM((LANES, keys), BF16),
            pltpu.VMEM((keys, 1), F32),
        ],
    )


def dot_first(a, b):
    return lax.dot_general(a, b, (((0,), (0,)), ((), ())), preferred_element_type=F32)


def mlp_kernel(
    one_ref, att_ref, gout_ref, w_out_ref, b_out_ref, gain_ref, shift_ref, w_up_ref, b_up_ref,
    w_down_ref, b_down_ref, w_dec_ref, b_dec_ref, w_pix_ref, b_pix_ref,
    pix_ref, normed_ref, act_ref, gup_ref, low_ref, decoded_ref, attended_ref,
    gtwo_ref, gatt_ref, gattended_ref, sum_up, sum_out, sum_gain, sum_shift,
    bias_ref, out_ref, gnormed_ref,
):
    @pl.when(pl.program_id(0) == 0)
    def _():
        bias_ref[...] = row_of(b_up_ref)
        for ref in (sum_up, sum_out, sum_gain, sum_shift):
            ref[...] = jnp.zeros_like(ref)

    ff = w_up_ref.shape[1]
    attended = att_ref[...].astype(BF16)
    attended_ref[...] = attended
    two = one_ref[...] + dot_plain(attended, w_out_ref[...]) + row_of(b_out_ref)
    centre = two - jnp.mean(two, -1, keepdims=True)
    inverse = lax.rsqrt(jnp.mean(centre * centre, -1, keepdims=True) + EPS)
    gain = row_of(gain_ref)
    normed = (centre * inverse * gain + row_of(shift_ref)).astype(BF16)
    normed_ref[...] = normed
    gout = gout_ref[...]
    gmlp = gout.astype(BF16)
    out_ref[...] = two + row_of(b_down_ref)
    gnormed_ref[...] = jnp.zeros_like(two)

    def step(i, carry):
        cols = pl.ds(pl.multiple_of(i * FF_BLOCK, FF_BLOCK), FF_BLOCK)
        up = dot_plain(normed, w_up_ref[:, cols]) + bias_ref[:, cols]
        bell = 0.5 * (1.0 + lax.erf(up * math.sqrt(0.5)))
        act = (up * bell).astype(BF16)
        slope = bell + up * (jnp.exp2(up * up * (-0.5 * math.log2(math.e))) * (2 * math.pi) ** -0.5)
        act_ref[:, cols] = act
        out_ref[...] += dot_plain(act, w_down_ref[cols, :])
        gup = (dot_last(gmlp, w_down_ref[cols, :]) * slope).astype(BF16)
        gup_ref[:, cols] = gup
        sum_up[:, cols] += jnp.sum(gup.astype(F32), 0, keepdims=True)
        gnormed_ref[...] += dot_last(gup, w_up_ref[:, cols])
        return carry

    lax.fori_loop(0, ff // FF_BLOCK, step, 0)
    out = out_ref[...]
    gnormed = gnormed_ref[...]
    low = out.astype(BF16)
    low_ref[...] = low
    decoded = (dot_plain(low, w_dec_ref[...]) + row_of(b_dec_ref)).astype(BF16)
    decoded_ref[...] = decoded
    pix_ref[...] = (dot_plain(decoded, w_pix_ref[...]) + row_of(b_pix_ref)).astype(BF16)
    hat = centre * inverse
    sum_gain[...] += jnp.sum(gnormed * hat, 0, keepdims=True)
    sum_shift[...] += jnp.sum(gnormed, 0, keepdims=True)
    scaled = gnormed * gain
    back = inverse * (
        scaled
        - jnp.mean(scaled, -1, keepdims=True)
        - hat * jnp.mean(scaled * hat, -1, keepdims=True)
    )
    gtwo = gout + back
    gtwo_ref[...] = gtwo
    gatt = gtwo.astype(BF16)
    gatt_ref[...] = gatt
    sum_out[...] += jnp.sum(gatt.astype(F32), 0, keepdims=True)
    gattended_ref[...] = dot_last(gatt, w_out_ref[...]).astype(BF16)


def mlp(one, att, gout, w_out, b_out, gain, shift, w_up, b_up, w_down, b_down, w_dec, b_dec, w_pix, b_pix):
    tokens, width = one.shape
    ff, dec, pix = w_up.shape[1], w_dec.shape[1], w_pix.shape[1]

    def block(size):
        return pl.BlockSpec((BLOCK, size), lambda i: (i, 0))

    def out(size, kind=BF16):
        return jax.ShapeDtypeStruct((tokens, size), kind)

    def vector(size):
        return jax.ShapeDtypeStruct((1, size), F32)

    weights = [w_out, b_out, gain, shift, w_up, b_up, w_down, b_down, w_dec, b_dec, w_pix, b_pix]
    return pl.pallas_call(
        mlp_kernel,
        grid=(tokens // BLOCK,),
        in_specs=[block(width)] * 3 + [held(item.shape) for item in weights],
        out_specs=[
            block(pix), block(width), block(ff), block(ff), block(width), block(dec), block(width),
            block(width), block(width), block(width),
            whole((1, ff)), whole((1, width)), whole((1, width)), whole((1, width)),
        ],
        out_shape=[
            out(pix), out(width), out(ff), out(ff), out(width), out(dec), out(width),
            out(width, F32), out(width), out(width),
            vector(ff), vector(width), vector(width), vector(width),
        ],
        scratch_shapes=[
            pltpu.VMEM((1, ff), F32),
            pltpu.VMEM((BLOCK, width), F32),
            pltpu.VMEM((BLOCK, width), F32),
        ],
        compiler_params=params(48),
        cost_estimate=cost(2 * tokens * width * (2 * width + 4 * ff + dec) + 2 * tokens * dec * pix, 40 << 20),
        name="mlp",
    )(one, att, gout, *weights)


def quarter_at(step, core):
    return 2 * (step % 2) + jnp.where(step < 2, 1 - core, core)


def lay_columns(ref, at, values, width):
    rows, cols = values.shape
    for i in range(cols // width):
        ref[0, at + i * rows : at + (i + 1) * rows, :] = values[:, i * width : (i + 1) * width]


def padded(rows):
    granule = 8 * lax.axis_size("col")
    return -(-rows // granule) * granule


def blank(ref, at):
    if at < ref.shape[1]:
        ref[0, at:, :] = jnp.zeros((ref.shape[1] - at, ref.shape[2]), BF16)


def pair_specs(rows, width):
    return [
        pl.BlockSpec((1, rows, width), lambda s, c: (jnp.minimum(s, 1), 0, 0)),
        pl.BlockSpec((1, rows, width), lambda s, c: (jnp.maximum(s - 2, 0), 0, 0)),
    ]


def grads_down_kernel(
    places, act_ref, gmlp_ref, decoded_ref, cot_ref, low_ref, gdec_ref, send_ref, keep_ref, lt_ref
):
    step = pl.program_id(0)

    @pl.when(step == 0)
    def _():
        lt_ref[...] = low_ref[...].T

    width = gmlp_ref.shape[1]
    part = width // 4
    rows = pl.ds(pl.multiple_of(quarter_at(step, places[0]) * part, part), part)
    down = dot_first(act_ref[...], gmlp_ref[...]).astype(BF16)
    pix = dot_first(decoded_ref[...], cot_ref[...]).astype(BF16)
    dec = dot_plain(lt_ref[rows, :], gdec_ref[...]).astype(BF16)
    at = down.shape[0] + pix.size // width
    cut, side = part * 2 // 3, dec.shape[1]
    rest = width - side
    for is_sent, ref in ((True, send_ref), (False, keep_ref)):

        @pl.when((step < 2) == is_sent)
        def _():
            ref[0, : down.shape[0], :] = down
            lay_columns(ref, down.shape[0], pix, width)
            ref[0, at : at + cut, :side] = dec[:cut]
            ref[0, at : at + part - cut, side:] = dec[cut:, :rest]
            ref[0, at + part - cut : at + cut, side:] = dec[cut:, rest:]
            blank(ref, at + cut)


def grads_down(places, act, gmlp, decoded, cot, low, gdec):
    tokens, ff = act.shape
    width, dec, pix = gmlp.shape[1], decoded.shape[1], cot.shape[1]
    rows = padded(ff // 4 + (dec // 4) * (pix // width) + dec // 4)
    return run(
        grads_down_kernel, "grads_down", (act, gmlp, decoded, cot, low, gdec),
        [jax.ShapeDtypeStruct((2, rows, width), BF16)] * 2,
        [
            pl.BlockSpec((tokens, ff // 4), lambda s, c: (0, quarter_at(s, c[0]))),
            held(gmlp.shape),
            pl.BlockSpec((tokens, dec // 4), lambda s, c: (0, quarter_at(s, c[0]))),
            held(cot.shape),
            held(low.shape),
            held(gdec.shape),
        ],
        pair_specs(rows, width), grid=(4,), places=places,
        estimate=cost(2 * tokens * (ff * width + dec * (pix + width)), 20 << 20),
        megabytes=32, scratch=[pltpu.VMEM((width, tokens), BF16)],
    )


def grads_up_kernel(
    places, normed_ref, gup_ref, att_ref, gatt_ref, send_ref, keep_ref, nt_ref, at_ref
):
    step = pl.program_id(0)

    @pl.when(step == 0)
    def _():
        nt_ref[...] = normed_ref[...].T
        at_ref[...] = att_ref[...].T

    width = normed_ref.shape[1]
    part = width // 4
    rows = pl.ds(pl.multiple_of(quarter_at(step, places[0]) * part, part), part)
    up = dot_plain(nt_ref[rows, :], gup_ref[...]).astype(BF16)
    out = dot_plain(at_ref[rows, :], gatt_ref[...]).astype(BF16)
    at = up.size // width
    for is_sent, ref in ((True, send_ref), (False, keep_ref)):

        @pl.when((step < 2) == is_sent)
        def _():
            lay_columns(ref, 0, up, width)
            ref[0, at : at + part, :] = out
            blank(ref, at + part)


def grads_up(places, normed, gup, attended, gatt, after):
    tokens, width = normed.shape
    ff = gup.shape[1]
    rows = padded(ff // 4 + width // 4)
    operands = (normed, gup, attended, gatt)
    return run(
        grads_up_kernel, "grads_up", operands, [jax.ShapeDtypeStruct((2, rows, width), BF16)] * 2,
        [held(item.shape) for item in operands], pair_specs(rows, width), grid=(4,), places=places,
        after=after, estimate=cost(2 * tokens * width * (ff + width), 16 << 20),
        scratch=[pltpu.VMEM((width, tokens), BF16)] * 2,
    )


def strip_back_kernel(dk_ref, dv_ref, w_ref, upper_ref, lower_ref, left_ref, right_ref):
    width = w_ref.shape[0]
    band, side = upper_ref.shape[0], left_ref.shape[0]
    back = (
        dot_last(dk_ref[...], w_ref[:, width : 2 * width]) + dot_last(dv_ref[...], w_ref[:, 2 * width :])
    ).astype(BF16)
    upper_ref[...] = back[:band]
    lower_ref[...] = back[band : 2 * band]
    left_ref[...] = back[2 * band : 2 * band + side]
    right_ref[...] = back[2 * band + side : 2 * (band + side)]


def strip_back(dk, dv, w, band, side, after):
    total, width = dk.shape
    sizes = (band, band, side, side)
    return run(
        strip_back_kernel, "strip_back", (dk, dv, w),
        [jax.ShapeDtypeStruct((rows, width), BF16) for rows in sizes],
        [whole(item.shape) for item in (dk, dv, w)], [whole((rows, width)) for rows in sizes],
        after=after, estimate=cost(4 * total * width * width, 8 << 20), megabytes=24,
    )


def grads_qkv_kernel(
    core_ref, normed_ref, rows_ref, dq_ref, dk_ref, dv_ref, dks_ref, dvs_ref,
    send_ref, keep_ref, nt_ref, st_ref,
):
    step = pl.program_id(0)

    @pl.when(step == 0)
    def _():
        nt_ref[...] = normed_ref[...].T
        st_ref[...] = rows_ref[...].T

    width = normed_ref.shape[1]
    part = width // 4
    rows = pl.ds(pl.multiple_of(quarter_at(step, core_ref[0]) * part, part), part)
    own, strip = nt_ref[rows, :], st_ref[rows, :]
    parts = (
        dot_plain(own, dq_ref[...]),
        dot_plain(own, dk_ref[...]) + dot_plain(strip, dks_ref[...]),
        dot_plain(own, dv_ref[...]) + dot_plain(strip, dvs_ref[...]),
    )
    for is_sent, ref in ((True, send_ref), (False, keep_ref)):

        @pl.when((step < 2) == is_sent)
        def _():
            for i, values in enumerate(parts):
                ref[0, i * part : (i + 1) * part, :] = values.astype(BF16)
            blank(ref, len(parts) * part)


def grads_qkv(places, normed, rows, dq, dk, dv, dks, dvs, after):
    tokens, width = normed.shape
    total = rows.shape[0]
    operands = (normed, rows, dq, dk, dv, dks, dvs)
    size = padded(3 * width // 4)
    return run(
        grads_qkv_kernel, "grads_qkv", operands, [jax.ShapeDtypeStruct((2, size, width), BF16)] * 2,
        [held(item.shape) for item in operands], pair_specs(size, width), grid=(4,), places=places,
        after=after, estimate=cost(2 * width * width * (3 * tokens + 2 * total), 20 << 20),
        scratch=[
            pltpu.VMEM((width, tokens), BF16),
            pltpu.VMEM((width, total), BF16),
        ],
    )


def embed_back_kernel(
    frames, stream_ref, dq_ref, dk_ref, dv_ref, w_ref, gtwo_ref, gain_ref, above_ref, below_ref, left_ref,
    right_ref, emb_ref, sum_patch, sum_gain, sum_shift, g_ref, side_ref,
):
    at_row = pl.program_id(0)
    width = stream_ref.shape[1]
    line = stream_ref.shape[0]
    tile_rows = left_ref.shape[0] // (8 * HALO)
    tile_cols = line // frames

    @pl.when(at_row == 0)
    def _():
        side_ref[0] = left_ref[...].astype(F32).reshape(side_ref.shape[1:])
        side_ref[1] = right_ref[...].astype(F32).reshape(side_ref.shape[1:])
        for ref in (sum_patch, sum_gain, sum_shift):
            ref[...] = jnp.zeros_like(ref)

    g_ref[...] = (
        dot_last(dq_ref[...], w_ref[:, :width])
        + dot_last(dk_ref[...], w_ref[:, width : 2 * width])
        + dot_last(dv_ref[...], w_ref[:, 2 * width :])
    )

    @pl.when(at_row < HALO)
    def _():
        g_ref[...] += above_ref[pl.ds(pl.multiple_of(at_row * line, line), line), :].astype(F32)

    @pl.when(at_row >= tile_rows - HALO)
    def _():
        start = (at_row - (tile_rows - HALO)) * line
        g_ref[...] += below_ref[pl.ds(pl.multiple_of(start, line), line), :].astype(F32)

    for j in range(HALO):
        source = j * tile_rows + at_row
        for f in range(frames):
            near = f * tile_cols + j
            far = near + tile_cols - HALO
            g_ref[near : near + 1, :] += side_ref[0, source, f : f + 1, :]
            g_ref[far : far + 1, :] += side_ref[1, source, f : f + 1, :]
    stream = stream_ref[...]
    grad = g_ref[...]
    centre = stream - jnp.mean(stream, -1, keepdims=True)
    inverse = lax.rsqrt(jnp.mean(centre * centre, -1, keepdims=True) + EPS)
    hat = centre * inverse
    sum_gain[...] += jnp.sum(grad * hat, 0, keepdims=True)
    sum_shift[...] += jnp.sum(grad, 0, keepdims=True)
    scaled = grad * row_of(gain_ref)
    one = gtwo_ref[...] + inverse * (
        scaled
        - jnp.mean(scaled, -1, keepdims=True)
        - hat * jnp.mean(scaled * hat, -1, keepdims=True)
    )
    sum_patch[...] += jnp.sum(one, 0, keepdims=True)
    emb_ref[...] = one.astype(BF16)


def embed_back(stream, dq, dk, dv, w, gtwo, gain, above, below, left, right, tile_rows, frames, hold):
    tokens, width = stream.shape
    line = tokens // tile_rows
    block = pl.BlockSpec((line, width), lambda r: (r, 0))
    vector = jax.ShapeDtypeStruct((1, width), F32)
    return run(
        functools.partial(embed_back_kernel, frames), "embed_back",
        (stream, dq, dk, dv, w, gtwo, gain, above, below, left, right),
        [jax.ShapeDtypeStruct((tokens, width), BF16)] + [vector] * 3,
        [
            block, block, block, block, held(w.shape), block, whole((width,)),
            whole(above.shape), whole(below.shape), whole(left.shape), whole(right.shape),
        ],
        [block] + [whole((1, width))] * 3, grid=(tile_rows,), hold=hold,
        estimate=cost(6 * tokens * width * width, 16 << 20),
        scratch=[pltpu.VMEM((line, width), F32), pltpu.VMEM((2, left.shape[0] // 8, 8, width), F32)],
    )


def lay_vectors(ref, at, vectors, quarter):
    width = ref.shape[2]
    ref[0, at:, :] = jnp.zeros((ref.shape[1] - at, width), BF16)
    lines = []
    for item in vectors:
        part = item.shape[1] // 4
        mine = jnp.zeros((1, part), F32)
        for q in range(4):
            mine = jnp.where(quarter == q, item[:, q * part : (q + 1) * part], mine)
        if part < width:
            mine = jnp.concatenate([mine, jnp.zeros((1, width - part), F32)], 1)
        lines.append(mine)
    pad = -(-len(lines) // 16) * 16 - len(lines)
    block = jnp.concatenate(lines + [jnp.zeros((pad, width), F32)], 0)
    high = block.astype(BF16)
    ref[0, at : at + block.shape[0], :] = high
    ref[0, at + block.shape[0] : at + 2 * block.shape[0], :] = (block - high.astype(F32)).astype(BF16)


def grads_patch_kernel(core_ref, pixels_ref, emb_ref, *refs):
    vectors, (send_ref, keep_ref) = refs[:-2], refs[-2:]
    step = pl.program_id(0)
    quarter = quarter_at(step, core_ref[0])
    patch = dot_first(pixels_ref[...], emb_ref[...]).astype(BF16)
    for is_sent, ref in ((True, send_ref), (False, keep_ref)):

        @pl.when((step < 2) == is_sent)
        def _():
            ref[0, : patch.shape[0], :] = patch
            lay_vectors(ref, patch.shape[0], [item[...] for item in vectors], quarter)


def grads_patch(places, pixels, emb, vectors, after):
    tokens, pix = pixels.shape
    width = emb.shape[1]
    rows = padded(pix // 4 + 64)
    return run(
        grads_patch_kernel, "grads_patch", (pixels, emb, *vectors),
        [jax.ShapeDtypeStruct((2, rows, width), BF16)] * 2,
        [
            pl.BlockSpec((tokens, pix // 4), lambda s, c: (0, quarter_at(s, c[0]))),
            held(emb.shape),
        ]
        + [whole(item.shape) for item in vectors],
        pair_specs(rows, width), grid=(4,), places=places, after=after,
        estimate=cost(2 * tokens * pix * width, 8 << 20),
    )


def pixel_back_kernel(emb_ref, w_ref, out_ref):
    out_ref[...] = dot_last(emb_ref[...], w_ref[...]).astype(BF16)


def pixel_back(emb, w, after):
    tokens, width = emb.shape
    pix = w.shape[0]
    return run(
        pixel_back_kernel, "pixel_back", (emb, w), jax.ShapeDtypeStruct((tokens, pix), BF16),
        [pl.BlockSpec((BLOCK, width), lambda i: (i, 0)), held(w.shape)],
        pl.BlockSpec((BLOCK, pix), lambda i: (i, 0)), grid=(tokens // BLOCK,), after=after,
        estimate=cost(2 * tokens * pix * width, 8 << 20),
    )


def swap(value, axis, stride):
    count = lax.axis_size(axis)
    return lax.ppermute(value, axis, [(i, i ^ stride) for i in range(count)])


def rotate(value, axis, steps):
    count = lax.axis_size(axis)
    return lax.ppermute(value, axis, [(i, (i + steps) % count) for i in range(count)])


def run(
    kernel, name, operands, out_shape, in_specs, out_specs, *, grid=(1,), places=None, after=(), hold=(),
    estimate=None, scratch=(), megabytes=28, aliases=None,
):
    scalars = () if places is None else (places,)
    count = len(scalars) + len(operands)
    extra = tuple(after) + tuple(hold)
    any_space = pl.BlockSpec(memory_space=pl.ANY)
    shapes = list(out_shape) if isinstance(out_shape, (list, tuple)) else [out_shape]
    specs = list(out_specs) if isinstance(out_specs, (list, tuple)) else [out_specs]
    own = len(shapes)

    def body(*refs):
        results = refs[count + len(extra) :]
        kernel(*refs[:count], *results[:own], *results[own + len(hold) :])

    at = count + len(after)
    aliases = dict(aliases or {})
    aliases.update({at + i: own + i for i in range(len(hold))})
    results = pl.pallas_call(
        body,
        grid_spec=pltpu.PrefetchScalarGridSpec(
            num_scalar_prefetch=len(scalars),
            grid=grid,
            in_specs=list(in_specs) + [any_space] * len(extra),
            out_specs=specs + [any_space] * len(hold),
            scratch_shapes=list(scratch),
        ),
        out_shape=shapes + [jax.ShapeDtypeStruct(item.shape, item.dtype) for item in hold],
        input_output_aliases=aliases,
        compiler_params=params(megabytes),
        cost_estimate=estimate,
        name=name,
    )(*scalars, *operands, *extra)
    return results[0] if len(results) == 1 else results


def by_rows(rows, body):
    size = next(n for n in (96, 80, 72, 64, 56, 48, 40, 32, 24, 16, 8) if rows % n == 0)

    def step(i, carry):
        body(pl.ds(pl.multiple_of(i * size, 8), size))
        return carry

    lax.fori_loop(0, rows // size, step, 0)


def add_across_kernel(places, keep_ref, came_ref, out_ref):
    def body(at):
        total = keep_ref[0, at, :].astype(F32) + came_ref[0, at, :].astype(F32)
        out_ref[at, :] = total.astype(BF16)

    by_rows(out_ref.shape[0], body)


def add_across(places, keep, came, after):
    rows, width = keep.shape[1:]
    block = pl.BlockSpec((1, rows // 2, width), lambda i, p: (1 - p[1], i, 0))
    return run(
        add_across_kernel, "add_across", (keep, came), jax.ShapeDtypeStruct((rows, width), BF16),
        [block, block], pl.BlockSpec((rows // 2, width), lambda i, p: (i, 0)),
        grid=(2,), places=places, after=after, estimate=cost(rows * width, 6 * rows * width),
        megabytes=16,
    )


def add_down_kernel(places, *refs):
    terms, outs = refs[:-2], refs[-2:]
    lead = outs[0].shape[:-2]

    for half, out_ref in enumerate(outs):

        @pl.when(pl.program_id(0) == half)
        def _():
            for i in range(lead[0] if lead else 1):

                def body(at):
                    total = sum(
                        (ref[i if lead else 0, at, :] if len(ref.shape) == 3 else ref[at, :]).astype(F32)
                        for ref in terms
                    ).astype(BF16)
                    if lead:
                        out_ref[i, at, :] = total
                    else:
                        out_ref[at, :] = total

                by_rows(out_ref.shape[-2], body)


def add_down(places, bit, terms, after, hold=()):
    shape = terms[-1].shape
    lead = shape[:-2]
    half, width = shape[-2] // 2, shape[-1]

    def which(h, p):
        return jnp.where(h == 0, 1 - p[bit], p[bit])

    same = pl.BlockSpec(lead + (half, width), lambda h, p: (0,) * len(lead) + (which(h, p), 0))
    pair = pl.BlockSpec((1, half, width), lambda h, p: (p[1], which(h, p), 0))
    out = pl.BlockSpec(lead + (half, width), lambda h, p: (0,) * len(lead) + (0, 0))
    return run(
        add_down_kernel, "add_down", terms,
        [jax.ShapeDtypeStruct(lead + (half, width), BF16)] * 2,
        [same if item.ndim == len(shape) else pair for item in terms], [out, out],
        grid=(2,), places=places, after=after, hold=hold,
        estimate=cost(half * width, 6 * half * width), megabytes=24,
    )


def add_x(places, terms, after, hold=()):
    rows, width = terms[0].shape[1:]
    block = pl.BlockSpec(
        (1, rows, width), lambda h, p: (jnp.where(h == 0, 1 - p[1], p[1]), 0, 0)
    )
    out = pl.BlockSpec((rows, width), lambda h, p: (0, 0))
    return run(
        add_down_kernel, "add_x", terms, [jax.ShapeDtypeStruct((rows, width), BF16)] * 2,
        [block] * len(terms), [out, out], grid=(2,), places=places, after=after, hold=hold,
        estimate=cost(rows * width, 6 * rows * width), megabytes=16,
    )


def add_whole_kernel(a_ref, b_ref, out_ref):
    def body(at):
        out_ref[at, :] = (a_ref[at, :].astype(F32) + b_ref[at, :].astype(F32)).astype(BF16)

    by_rows(out_ref.shape[0], body)


def add_whole(a, b, after):
    return run(
        add_whole_kernel, "add_whole", (a, b), jax.ShapeDtypeStruct(a.shape, BF16),
        [whole(a.shape)] * 2, whole(a.shape), after=after, estimate=cost(a.size, 6 * a.size),
        megabytes=16,
    )


def join_kernel(bit, places, own_ref, other_ref, out_ref):
    rows = own_ref.shape[0]
    mine = pl.multiple_of(places[bit] * rows, 8)
    theirs = pl.multiple_of((1 - places[bit]) * rows, 8)

    def body(at):
        out_ref[pl.ds(pl.multiple_of(mine + at.start, 8), at.size), :] = own_ref[at, :]
        out_ref[pl.ds(pl.multiple_of(theirs + at.start, 8), at.size), :] = other_ref[at, :]

    by_rows(rows, body)


def join(places, bit, own, other, after):
    rows, width = own.shape
    return run(
        functools.partial(join_kernel, bit), "join", (own, other),
        jax.ShapeDtypeStruct((2 * rows, width), BF16), [whole(own.shape)] * 2,
        whole((2 * rows, width)), places=places, after=after,
        estimate=cost(own.size, 8 * own.size), megabytes=16,
    )


def wide(full_ref, at, rows, cols, out_ref):
    width = full_ref.shape[1]
    for i in range(cols // width):

        def body(to):
            source = pl.ds(pl.multiple_of(at + i * rows + to.start, 8), to.size)
            out_ref[to, i * width : (i + 1) * width] = full_ref[source, :]

        by_rows(rows, body)


def finish_kernel(bit, lay_out, places, own_ref, other_ref, *refs):
    outs, full_ref = refs[:-1], refs[-1]
    rows = own_ref.shape[0]
    mine = pl.multiple_of(places[bit] * rows, 8)
    theirs = pl.multiple_of((1 - places[bit]) * rows, 8)

    def body(at):
        full_ref[pl.ds(pl.multiple_of(mine + at.start, 8), at.size), :] = own_ref[at, :].astype(F32)
        full_ref[pl.ds(pl.multiple_of(theirs + at.start, 8), at.size), :] = other_ref[at, :].astype(F32)

    by_rows(rows, body)
    lay_out(full_ref, *outs)


def finish(places, bit, own, other, lay_out, shapes, after):
    rows, width = own.shape
    return run(
        functools.partial(finish_kernel, bit, lay_out), "finish", (own, other),
        [jax.ShapeDtypeStruct(shape, F32) for shape in shapes], [whole(own.shape)] * 2,
        [whole(shape) for shape in shapes], places=places, after=after,
        estimate=cost(own.size, 16 * own.size), megabytes=16, scratch=[pltpu.VMEM((2 * rows, width), F32)],
    )


class Reduction:
    def __init__(self, order, places, pair, lay_out, shapes, late_x=False):
        self.send, self.keep = pair
        self.order, self.places = order, places
        self.lay_out, self.shapes = lay_out, shapes
        last = lax.axis_size("col").bit_length() - 2
        self.steps = [("down", i) for i in range(last)]
        if late_x:
            self.steps += [("down", last), ("x", 0), ("up", last)]
        else:
            self.steps = [("across", 0)] + self.steps + [("full", last)]
        self.steps += [("up", i) for i in reversed(range(last))] + [("end", 0)]
        self.pending = (None, 0)
        self.sent = self.result = None

    def after(self):
        return (self.order[-1].sent,) if self.order and self.order[-1] is not self else ()

    def terms(self):
        kind, bit = self.pending
        if kind is None:
            self.came = swap(self.send, "row", 1)
            return self.keep, self.came
        if kind == "across":
            return self.keep, self.came, swap(self.sent, "row", 2)
        if kind == "x":
            return self.mine, swap(self.sent, "row", 2)
        return self.mine, swap(self.sent, "col", 1 << bit)

    def advance(self, then=None):
        kind, bit = self.steps.pop(0)
        places, after = self.places, self.after()
        terms = self.terms()
        hold = () if then is None else (then.send,)
        kept = ()
        if kind == "across":
            self.sent = add_across(places, *terms, after)
        elif kind == "down":
            self.sent, self.mine, *kept = add_down(places, 2 + bit, terms, after, hold)
        elif kind == "x":
            self.sent, self.mine, *kept = add_x(places, terms, after, hold)
        elif kind == "end":
            result = finish(places, 2 + self.pending[1], *terms, self.lay_out, self.shapes, after)
            self.result = result if isinstance(result, (list, tuple)) else [result]
            self.sent = self.result[0]
        elif self.pending[0] == "up":
            self.sent = self.mine = join(places, 2 + self.pending[1], *terms, after)
        else:
            self.sent = self.mine = add_whole(*terms, after)
        if kept:
            (then.send,) = kept
        self.pending = (kind, bit)
        self.order.append(self)


class Ready:
    def __init__(self, value):
        self.sent = value


def wave_numbers(width):
    def of(part):
        half = part // 2
        one = np.float32(1.0) / np.float32(10000.0) ** (
            np.arange(half, dtype=np.float32) / np.float32(half)
        )
        return [one, one]

    unit = width // 16
    return np.concatenate(of(4 * unit) + of(6 * unit) + of(6 * unit)).astype(np.float32)[None, :]


def per_device(
    pixels, timestamps, frame_count, visible, halo_reach, w_patch, b_patch, gain_one, shift_one,
    w_qkv, b_query, b_value, w_out, b_out, gain_two, shift_two, w_up, b_up, w_down, b_down,
    w_dec, b_dec, w_pix, b_pix, cotangent,
):
    tile_rows, tile_cols, frames, pix_width = pixels.shape
    model_width = w_patch.shape[1]
    tokens = tile_rows * tile_cols * frames
    ff = w_up.shape[1]
    grid_shape = (tile_rows, frames, tile_cols)
    side = tile_rows * 8 * HALO
    band = HALO * frames * tile_cols
    row_at, col_at = lax.axis_index("row"), lax.axis_index("col")
    col_bits = lax.axis_size("col").bit_length() - 1
    places = jnp.stack(
        [row_at % 2, row_at // 2] + [(col_at >> i) % 2 for i in range(col_bits)]
    ).astype(jnp.int32)

    flat_pixels = pixels.transpose(0, 2, 1, 3).reshape(tokens, pix_width)
    flat_cotangent = cotangent.transpose(0, 2, 1, 3).reshape(tokens, pix_width)
    stream_one, normed_one, high, low, tail, head, flags = embed(
        timestamps.reshape(-1), frame_count.reshape(-1), visible.transpose(2, 0, 1), flat_pixels,
        w_patch, b_patch, gain_one, shift_one, wave_numbers(model_width),
    )
    upper = rotate(high, "row", 1)
    lower = rotate(low, "row", -1)
    left = rotate(tail, "col", 1)
    right = rotate(head, "col", -1)
    query, key, value = own_qkv(normed_one, w_qkv, b_query, b_value)
    grad_dec, grad_stream, grad_mlp, sum_pix, sum_dec, sum_down = decode_back(
        flat_cotangent, w_pix, w_dec
    )
    strip_key, strip_value, strip_rows, bias = strip_kv(
        halo_reach.reshape(-1), upper, lower, left, right, flags, w_qkv, b_value
    )
    mixed, log_total = attend(query, key, value, strip_key, strip_value, bias)
    (
        pixel_out, normed_two, act, grad_pre, stream_low, decoded, attended,
        grad_two, grad_att, grad_attended, sum_up, sum_out, sum_gain_two, sum_shift_two,
    ) = mlp(
        stream_one, mixed, grad_stream, w_out, b_out, gain_two, shift_two,
        w_up, b_up, w_down, b_down, w_dec, b_dec, w_pix, b_pix,
    )
    fixed = (query, key, value, strip_key, strip_value)
    rest = (mixed, log_total, bias)
    pairs = model_width // LANES
    third = pairs // 3
    quarter = model_width // 4
    patch_rows, down_rows = pix_width // 4, ff // 4
    pix_rows, up_rows = w_dec.shape[1] // 4, quarter * (ff // model_width)
    dec_width = w_dec.shape[1]
    cut = quarter * 2 // 3
    order = []

    def lay_down(full, down_ref, pix_ref, dec_ref):
        wide(full, 0, down_rows, model_width, down_ref)
        wide(full, down_rows, pix_rows, pix_width, pix_ref)
        at, tall = down_rows + pix_rows * (pix_width // model_width), quarter - cut
        dec_ref[:cut, :] = full[at : at + cut, :dec_width]
        dec_ref[cut:, : model_width - dec_width] = full[at : at + tall, dec_width:]
        dec_ref[cut:, model_width - dec_width :] = full[at + tall : at + cut, dec_width:]

    def lay_up(full, up_ref, out_ref):
        wide(full, 0, quarter, ff, up_ref)
        wide(full, up_rows, quarter, model_width, out_ref)

    def lay_middle(full, qkv_ref):
        wide(full, 0, quarter, 3 * model_width, qkv_ref)

    def lay_last(full, patch_ref, *refs):
        wide(full, 0, patch_rows, model_width, patch_ref)
        lines = -(-len(refs) // 16) * 16
        for i, ref in enumerate(refs):
            at = patch_rows + i
            size = ref.shape[1]
            ref[...] = full[at : at + 1, :size] + full[at + lines : at + lines + 1, :size]

    down = Reduction(
        order, places,
        grads_down(places, act, grad_mlp, decoded, flat_cotangent, stream_low, grad_dec), lay_down,
        [(down_rows, model_width), (pix_rows, pix_width), (quarter, dec_width)], late_x=True,
    )
    up = Reduction(
        order, places, grads_up(places, normed_two, grad_pre, attended, grad_att, (down.keep,)),
        lay_up, [(quarter, ff), (quarter, model_width)],
    )
    down.advance()
    up.advance()
    most = pairs * 2 // 3
    back = attend_back(*fixed, grad_attended, *rest, 0, most, (), (down.sent, up.sent))
    order.append(Ready(back[0]))
    down.advance()
    up.advance()
    back = attend_back(
        *fixed, grad_attended, *rest, most, pairs - most, back, (up.sent, down.sent)
    )
    dq, dk, dv, dks, dvs, sum_query, sum_value = back
    order.append(Ready(dq))
    down.advance()
    up.advance()
    upper_back, lower_back, left_back, right_back = strip_back(
        dks, dvs, w_qkv, band, side, (up.sent,)
    )
    from_right = rotate(left_back, "col", -1)
    from_left = rotate(right_back, "col", 1)
    from_below = rotate(upper_back, "row", -1)
    from_above = rotate(lower_back, "row", 1)
    middle = Reduction(
        order, places,
        grads_qkv(places, normed_one, strip_rows, dq, dk, dv, dks, dvs, (upper_back,)),
        lay_middle, [(quarter, 3 * model_width)],
    )
    grad_emb, sum_patch, sum_gain_one, sum_shift_one, up.sent = embed_back(
        stream_one, dq, dk, dv, w_qkv, grad_two, gain_one, from_above,
        from_below, from_left, from_right, tile_rows, frames, (up.sent,),
    )
    vectors = [
        sum_patch, sum_gain_one, sum_shift_one, sum_query, sum_value, sum_out, sum_gain_two,
        sum_shift_two, sum_up, sum_down, sum_dec, sum_pix,
    ]
    order.append(Ready(grad_emb))
    down.advance(middle)
    last = Reduction(
        order, places, grads_patch(places, flat_pixels, grad_emb, vectors, (down.sent,)),
        lay_last, [(patch_rows, model_width)] + [(1, item.shape[1] // 4) for item in vectors],
    )
    groups = {"d": down, "u": up, "m": middle, "l": last}
    for turn in EVENTS:
        if turn == "p":
            pixel_grad = pixel_back(grad_emb, w_patch, (order[-1].sent,))
            order.append(Ready(pixel_grad))
        elif groups[turn].steps:
            groups[turn].advance()
    while any(each.steps for each in groups.values()):
        for each in groups.values():
            if each.steps:
                each.advance()
    share_down, share_pix, share_dec = down.result
    share_up, share_out = up.result
    (share_qkv,) = middle.result
    share_patch, *pieces = last.result
    pieces = [item.reshape(-1) for item in pieces]

    def to_scene(flat):
        return flat.reshape(grid_shape + (pix_width,)).transpose(0, 2, 1, 3)

    return (
        to_scene(pixel_out), to_scene(pixel_grad), share_patch, pieces[0], pieces[1], pieces[2],
        share_qkv, pieces[3], pieces[4], share_out, pieces[5], pieces[6], pieces[7], share_up,
        pieces[8], share_down, pieces[9], share_dec, pieces[10], share_pix, pieces[11],
    )


def solution(mesh):
    tiles = P("row", "col", None, None)
    return jax.shard_map(
        per_device,
        mesh=mesh,
        in_specs=(
            tiles,
            P("row", "col", None),
            P("row", "col"),
            P("row", "col", None),
            P("row", "col"),
        )
        + (P(),) * 19
        + (tiles,),
        out_specs=(
            tiles,
            tiles,
            P("row", None),
            P("row"),
            P("row"),
            P("row"),
            P("row", None),
            P("row"),
            P("row"),
            P("row", None),
            P("row"),
            P("row"),
            P("row"),
            P("row", None),
            P("row"),
            P("row", None),
            P("row"),
            P("row", None),
            P("row"),
            P("row", None),
            P("row"),
        ),
        check_vma=False,
    )
```
